32 devices in a mesh: dp: 8 (over z, x), bn: 4 (over y, core).
Axes of the slice: x: 2, y: 2, z: 4, core: 2. Of those that a mesh axis runs over, the one named last changes fastest.
Arguments:
- features: bfloat16 [512, 8, 2048], P(('dp', 'bn')), may hold values from -6 to 6
- shuffle_masks: int32 [16], replicated, may hold values from 0 to 7, as said below
- conv_in: bfloat16 [2048, 512], replicated, may hold values from -0.125 to 0.125
- conv_mid: bfloat16 [3, 512, 512], replicated, may hold values from -0.15625 to 0.15625
- conv_out: bfloat16 [512, 2048], replicated, may hold values from -0.25 to 0.25
- head: bfloat16 [2048, 128], replicated, may hold values from -0.125 to 0.125
- queries: bfloat16 [512, 128], P(('dp', 'bn'))
- queue: bfloat16 [65536, 128], P('dp')
- positive: int32 [512], P(('dp', 'bn')), may hold values from 0 to 511, as said below
Outputs:
- loss_rows: float32 [512], P(('dp', 'bn'))
The draws below stay inside these ranges and needn't reach their ends.
Inputs may be any that keep to these rules, and one draw needn't show every extreme that they name: `shuffle_masks`: every binary digit of a dp index is set in exactly half of the entries. positive[i] names a crop with the same bn index as crop i.
All inputs are finite; a program needn't handle non-finite values.
Results may differ from the reference program's by a relative error of at most 0.0023.
Values may be sent and summed in bfloat16 or wider, within the bound.
A program may use at most 64 MiB of HBM per device.

```python
import math
import jax
import jax.numpy as jnp
from jax import lax

CH = 2048
MID = 512
EMB = 128
QUEUE = 65536
POS = 8
CROP_DEV = 16
CROPS = 512
DP_BITS = 3
N_DP = 8
N_BN = 4


def query_base(key):
    base_rows = jax.random.normal(jax.random.fold_in(key, 11), (CROPS, EMB), jnp.float32)
    return base_rows


def draw_queries(key, part):
    base_rows = query_base(key)
    return base_rows.astype(jnp.bfloat16)


def draw_queue(key, part):
    base_rows = query_base(key)
    owner_row = jax.random.randint(jax.random.fold_in(key, 13), (QUEUE,), 0, CROPS, jnp.int32)
    planted_mask = jax.random.randint(jax.random.fold_in(key, 16), (QUEUE,), 0, 2, jnp.int32) == 1
    noise_rows = jax.random.normal(jax.random.fold_in(key, 14), (QUEUE, EMB), jnp.float32)
    noise_level = jax.random.uniform(jax.random.fold_in(key, 17), (QUEUE, 1), jnp.float32, 0.08, 0.4)
    planted = jnp.take(base_rows, owner_row, axis=0) + noise_level * noise_rows
    queue_rows = jnp.where(planted_mask[:, None], planted, noise_rows)
    return queue_rows.astype(jnp.bfloat16)


def draw_shuffle_masks(key, part):
    half = CROP_DEV // 2
    total = jnp.zeros((CROP_DEV,), jnp.int32)
    for level in range(DP_BITS):
        order = jax.random.permutation(jax.random.fold_in(key, 40 + level), CROP_DEV - 2).astype(jnp.int32) + 2
        chosen = jnp.concatenate([jnp.zeros((1,), jnp.int32), order[:half - 1]])
        flags = jnp.zeros((CROP_DEV,), jnp.int32).at[chosen].set(1)
        total = total + flags * 2 ** level
    return total


def draw_positive(key, part):
    crop_ids = jnp.arange(CROPS, dtype=jnp.int32)
    group_of = crop_ids // CROP_DEV % N_BN
    column = jax.random.randint(jax.random.fold_in(key, 31), (CROPS,), 0, N_DP, jnp.int32)
    slot_of = jax.random.randint(jax.random.fold_in(key, 32), (CROPS,), 0, CROP_DEV, jnp.int32)
    picked = (column * N_BN + group_of) * CROP_DEV + slot_of
    picked = picked.at[0].set(0)
    return picked.at[CROPS - 1].set(CROPS - 1)


def block_scale(key, shape, shards, low, top_value):
    loudness = 1.0
    for position, shards_of in shards:
        heights = jax.random.uniform(jax.random.fold_in(jax.random.fold_in(key, 6), position), (shards_of,), jnp.float32, low / len(shards), top_value / len(shards))
        loudness = loudness * jnp.repeat(jnp.exp(heights), shape[position] // shards_of).reshape((-1,) + (1,) * (len(shape) - 1 - position))
    return loudness


def bell_draw(rng, dims, scale, limit, cuts=(), kind=jnp.bfloat16):
    drawn = scale * jax.random.normal(rng, dims, jnp.float32)
    if cuts:
        drawn = drawn * block_scale(rng, dims, cuts, -0.22, 0.18)
    return jnp.clip(drawn, -limit, limit).astype(kind)


def setup_inputs(seed: int = 0) -> dict:
    arg_keys = jax.random.split(jax.random.key(seed), 10)
    features = bell_draw(arg_keys[0], (CROPS, POS, CH), 1.0, 6.0, ((0, 32),))
    shuffle_masks = draw_shuffle_masks(jax.random.fold_in(arg_keys[9], 71), 0)
    conv_in = bell_draw(arg_keys[2], (CH, MID), CH ** -0.5, 0.125)
    conv_mid = bell_draw(arg_keys[3], (3, MID, MID), (3 * MID) ** -0.5, 0.15625)
    conv_out = bell_draw(arg_keys[4], (MID, CH), MID ** -0.5, 0.25)
    head = bell_draw(arg_keys[5], (CH, EMB), CH ** -0.5, 0.125)
    queries = draw_queries(jax.random.fold_in(arg_keys[9], 71), 0)
    queue = draw_queue(jax.random.fold_in(arg_keys[9], 71), 0)
    positive = draw_positive(jax.random.fold_in(arg_keys[9], 71), 0)
    return {"features": features, "shuffle_masks": shuffle_masks, "conv_in": conv_in, "conv_mid": conv_mid, "conv_out": conv_out, "head": head, "queries": queries, "queue": queue, "positive": positive}


EPS_BN = 1e-05
EPS_UNIT = 1e-06
INV_TEMP = 1.0 / 0.07

def unit_rows(values):
    values = values.astype(jnp.float32)
    return values * lax.rsqrt(lax.optimization_barrier(jnp.sum(values * values, axis=-1, keepdims=True)) + EPS_UNIT)

def group_norm(values):
    center = lax.optimization_barrier(jnp.mean(values, axis=1, keepdims=True))
    spread = lax.optimization_barrier(jnp.mean(jnp.square(values - center), axis=1, keepdims=True))
    return (values - center) * lax.rsqrt(spread + EPS_BN)

def project(values, weight):
    shaped = values.reshape(-1, values.shape[-1])
    out = jnp.dot(shaped, weight, preferred_element_type=jnp.float32)
    return out.reshape(values.shape[:-1] + (weight.shape[1],))

def reference(features, shuffle_masks, conv_in, conv_mid, conv_out, head, queries, queue, positive):
    dp_ids = jnp.arange(N_DP, dtype=jnp.int32)
    source = jnp.bitwise_xor(dp_ids[:, None], shuffle_masks[None, :].astype(jnp.int32))
    bn_ids = jnp.arange(N_BN, dtype=jnp.int32)[None, :, None]
    slot_ids = jnp.arange(CROP_DEV, dtype=jnp.int32)[None, None, :]
    feature_grid = features.reshape(N_DP, N_BN, CROP_DEV, POS, CH)
    shuffled = feature_grid[source[:, None, :], bn_ids, slot_ids]
    flat_rows = shuffled.reshape(N_DP, N_BN * CROP_DEV * POS, CH)
    first_act = jax.nn.relu(group_norm(project(flat_rows, conv_in))).astype(jnp.bfloat16)
    tap_maps = first_act.reshape(N_DP, N_BN * CROP_DEV, POS, MID)
    padded = jnp.pad(tap_maps, ((0, 0), (0, 0), (1, 1), (0, 0)))
    second_sum = jnp.zeros((N_DP, N_BN * CROP_DEV, POS, MID), jnp.float32)
    for tap in range(3):
        second_sum = second_sum + project(padded[:, :, tap:tap + POS, :], conv_mid[tap])
    second_act = jax.nn.relu(group_norm(second_sum.reshape(N_DP, -1, MID))).astype(jnp.bfloat16)
    third_sum = project(second_act, conv_out)
    block = jax.nn.relu(group_norm(third_sum) + flat_rows.astype(jnp.float32)).astype(jnp.bfloat16)
    pooled = lax.optimization_barrier(jnp.mean(block.reshape(N_DP, N_BN * CROP_DEV, POS, CH).astype(jnp.float32), axis=2)).astype(jnp.bfloat16)
    key_unit = unit_rows(project(pooled, head)).astype(jnp.bfloat16)
    key_grid = key_unit.reshape(N_DP, N_BN, CROP_DEV, EMB)
    restored = key_grid[source[:, None, :], bn_ids, slot_ids].reshape(CROPS, EMB)
    query_unit = unit_rows(queries).astype(jnp.bfloat16)
    queue_unit = unit_rows(queue).astype(jnp.bfloat16)
    picked = jnp.take(restored, positive.astype(jnp.int32), axis=0)
    positive_logit = lax.optimization_barrier(jnp.sum(query_unit.astype(jnp.float32) * picked.astype(jnp.float32), axis=-1)) * INV_TEMP
    block_rows = math.gcd(CROPS, 256)
    blocks = query_unit.reshape(CROPS // block_rows, block_rows, EMB)

    def queue_terms(query_block):
        scores = jnp.dot(query_block, queue_unit.T, preferred_element_type=jnp.float32) * INV_TEMP
        return lax.optimization_barrier(jnp.sum(jnp.exp(scores - INV_TEMP), axis=1))
    negative = lax.map(queue_terms, blocks).reshape(CROPS)
    return jnp.log(jnp.exp(positive_logit - INV_TEMP) + negative) + INV_TEMP - positive_logit
```

```python
import functools

import jax
import jax.numpy as jnp
from jax import lax
from jax.experimental import pallas as pl
from jax.experimental.pallas import tpu as pltpu
from jax.sharding import PartitionSpec as P

EPS_BN = 1e-05
EPS_UNIT = 1e-06
INV_TEMP = 1.0 / 0.07


def partner_2(value, axis, distance):
    return lax.ppermute(value, axis, [(i, i ^ 1 << distance) for i in range(lax.axis_size(axis))])


def unit_rows(values):
    values = values.astype(jnp.float32)
    return values * lax.rsqrt(jnp.sum(values * values, axis=-1, keepdims=True) + EPS_UNIT)


def group_norm(values, row_total):
    first = lax.psum(jnp.sum(values, axis=0), "bn")
    center = first / row_total
    spread = lax.psum(jnp.sum(jnp.square(values - center), axis=0), "bn") / row_total
    return (values - center) * lax.rsqrt(spread + EPS_BN)


def moving_slots(shuffle_masks, level, half):
    flags = jnp.bitwise_and(jnp.right_shift(shuffle_masks, level), 1)
    return jnp.argsort(1 - flags, stable=True)[:half]


def on_device_moving(features, shuffle_masks, conv_in, conv_mid, conv_out, head, queries, queue, positive):
    dp_count = lax.axis_size("dp")
    bn_count = lax.axis_size("bn")
    bit_count = dp_count.bit_length() - 1
    crop_dev, positions, channels = features.shape
    half = crop_dev // 2
    middle = conv_in.shape[1]
    query_unit = unit_rows(queries).astype(jnp.bfloat16)
    query_all = lax.all_gather(query_unit, "dp", axis=0, tiled=True)
    shuffled = features
    for level in range(bit_count):
        moving = moving_slots(shuffle_masks, level, half)
        chosen = (moving[:, None] == jnp.arange(crop_dev)[None, :]).astype(jnp.bfloat16)
        leaving = jnp.dot(
            chosen, shuffled.reshape(crop_dev, positions * channels), preferred_element_type=jnp.float32
        ).astype(jnp.bfloat16)
        partner = partner_2(leaving.reshape(half, positions, channels), "dp", level)
        shuffled = shuffled.at[moving].set(partner)
    row_total = crop_dev * positions * bn_count
    flat_rows = shuffled.reshape(crop_dev * positions, channels)
    first_sum = jnp.dot(flat_rows, conv_in, preferred_element_type=jnp.float32)
    first_act = jax.nn.relu(group_norm(first_sum, row_total)).astype(jnp.bfloat16)
    tap_maps = first_act.reshape(crop_dev, positions, middle)
    padded = jnp.pad(tap_maps, ((0, 0), (1, 1), (0, 0)))
    stacked = jnp.concatenate([padded[:, tap : tap + positions, :] for tap in range(3)], axis=2)
    second_sum = jnp.dot(
        stacked.reshape(crop_dev * positions, 3 * middle),
        conv_mid.reshape(3 * middle, middle),
        preferred_element_type=jnp.float32,
    )
    second_act = jax.nn.relu(group_norm(second_sum, row_total)).astype(jnp.bfloat16)
    third_sum = jnp.dot(second_act, conv_out, preferred_element_type=jnp.float32)
    block = jax.nn.relu(group_norm(third_sum, row_total) + flat_rows.astype(jnp.float32)).astype(
        jnp.bfloat16
    )
    pooled = jnp.mean(
        block.reshape(crop_dev, positions, channels).astype(jnp.float32), axis=1
    ).astype(jnp.bfloat16)
    key_unit = unit_rows(jnp.dot(pooled, head, preferred_element_type=jnp.float32)).astype(
        jnp.bfloat16
    )
    for level in range(bit_count):
        moving = moving_slots(shuffle_masks, level, half)
        partner = partner_2(jnp.take(key_unit, moving, axis=0), "dp", level)
        key_unit = key_unit.at[moving].set(partner)
    queue_unit = unit_rows(queue).astype(jnp.bfloat16)
    scores = jnp.dot(query_all, queue_unit.T, preferred_element_type=jnp.float32) * INV_TEMP
    queue_part = jnp.sum(jnp.exp(scores - INV_TEMP), axis=1)
    key_all = lax.all_gather(key_unit, "dp", axis=0, tiled=True)
    slot_of = positive % crop_dev
    column = positive // crop_dev // bn_count
    picked = jnp.take(key_all, column * crop_dev + slot_of, axis=0)
    positive_logit = (
        jnp.sum(query_unit.astype(jnp.float32) * picked.astype(jnp.float32), axis=-1) * INV_TEMP
    )
    negative = lax.psum_scatter(queue_part, "dp", scatter_dimension=0, tiled=True)
    return jnp.log(jnp.exp(positive_logit - INV_TEMP) + negative) + INV_TEMP - positive_logit


MESH = pl.DeviceIdType.MESH
LANES = 128
QUEUE_STEPS = 8
PANELS = 4
PHASES = (
    "query", "queue", "key", "sum1", "bn1", "bn2", "bn3", "class", "far",
    "a0", "a1", "a2", "b0", "b1", "b2",
)
ORDERS = {"a": (2, 0, 1), "b": (0, 1, 2)}


def shuffled_kernel(
    n_dp, n_bn,
    masks_hbm, positive_hbm, queries_hbm, x_hbm, in_hbm, mid_hbm, out_hbm, head_hbm, queue_hbm,
    loss_ref,
    masks, positive, queries,
    x_ref, in_ref, mid_ref, out_ref, head_ref, queue_ref,
    h_ref, wide_ref, class_ref, mean_ref, scale_ref,
    dev_ref, class_send, class_recv, far_send, far_recv,
    a_send, a_pair, a_last, b_send, b_pair, b_last,
    sum_send, sum_recv, own1, all1, own2, all2, own3, all3,
    query_own, query_all, part_own, part_all, key_own, key_all,
    load_sem, panel_sem, send_sem, recv_sem,
):
    f32, bf16 = jnp.float32, jnp.bfloat16
    d = lax.axis_index("dp")
    b = lax.axis_index("bn")
    rows, channels = x_ref.shape
    slots = masks.shape[0]
    cells = rows // slots
    half = rows // 2
    middle = in_ref.shape[1]
    wide_half = channels // 2
    total = float(rows * n_bn)

    panel = channels // PANELS
    panels = [
        pltpu.make_async_copy(
            in_hbm.at[pl.ds(i * panel, panel)], in_ref.at[pl.ds(i * panel, panel)], panel_sem.at[i]
        )
        for i in range(PANELS)
    ]
    loads = [
        pltpu.make_async_copy(src, dst, load_sem.at[i])
        for i, (src, dst) in enumerate(
            [(masks_hbm, masks), (positive_hbm, positive), (queries_hbm, queries), (x_hbm, x_ref), (queue_hbm, queue_ref), (mid_hbm, mid_ref), (out_hbm, out_ref), (head_hbm, head_ref)]
        )
    ]
    for load in loads[:4] + panels:
        load.start()

    barrier = pltpu.get_barrier_semaphore()
    dp_peers = [(d ^ k, b) for k in range(1, n_dp)]
    bn_peers = [(d, lax.rem(b + k, n_bn)) for k in range(1, n_bn)]
    for peer in dp_peers + bn_peers:
        pl.semaphore_signal(barrier, inc=1, device_id=peer, device_id_type=MESH)

    def push(phase, src, dst, peer):
        i = PHASES.index(phase)
        pltpu.make_async_remote_copy(
            src_ref=src, dst_ref=dst, send_sem=send_sem.at[i], recv_sem=recv_sem.at[i],
            device_id=peer, device_id_type=MESH,
        ).start()

    def arrived(phase, view):
        pltpu.make_async_copy(view, view, recv_sem.at[PHASES.index(phase)]).wait()

    def sent(phase, view):
        pltpu.make_async_copy(view, view, send_sem.at[PHASES.index(phase)]).wait()

    def most(ref):
        return ref.at[pl.ds(0, ref.shape[0] - 1)]

    def column_peers(phase, src, dst):
        for peer in dp_peers:
            push(phase, src, dst.at[d], peer)

    def exact(a, c):
        return jnp.dot(a, c, preferred_element_type=f32, precision=lax.Precision.HIGHEST)

    def dot(a, c):
        return jnp.dot(a, c, preferred_element_type=f32)

    for load in loads[:3]:
        load.wait()

    q = queries[...].astype(f32)
    query_unit = (q * lax.rsqrt(jnp.sum(q * q, axis=-1, keepdims=True) + EPS_UNIT)).astype(bf16)
    query_own[...] = query_unit
    query_all[d] = query_unit

    lane = lax.broadcasted_iota(jnp.int32, (slots, slots), 1)
    sub = lax.broadcasted_iota(jnp.int32, (slots, slots), 0)
    lane1 = lax.broadcasted_iota(jnp.int32, (1, slots), 1)
    lane_8 = lax.broadcasted_iota(jnp.int32, (8, LANES), 1)
    sub_8 = lax.broadcasted_iota(jnp.int32, (8, LANES), 0)
    slot_8 = lane_8 // cells
    mask_row = jnp.zeros((slots, slots), jnp.int32)
    mask_col = jnp.zeros((slots, slots), jnp.int32)
    want = jnp.zeros((1, slots), jnp.int32)
    mask_8 = jnp.zeros((8, LANES), jnp.int32)
    sources = []
    for s in range(slots):
        mask = masks[s]
        sources.append(mask ^ d)
        mask_row = jnp.where(lane == s, sources[s], mask_row)
        mask_col = jnp.where(sub == s, sources[s], mask_col)
        mask_8 = jnp.where(slot_8 == s, mask, mask_8)
        place = positive[s]
        slot = lax.rem(place, slots)
        column = lax.div(place, slots * n_bn) ^ masks[slot]
        want = jnp.where(lane1 == s, column * slots + slot, want)
    same = (mask_row == mask_col).astype(f32)
    local_mean = same / (jnp.sum(same, axis=0, keepdims=True) * float(cells))
    member = (mask_row[:n_dp] == sub[:n_dp]).astype(f32)
    counts = []
    for e in range(n_dp):
        count = jnp.int32(0)
        for s in range(slots):
            count = count + (sources[s] == e).astype(jnp.int32)
        counts.append((count * cells).astype(f32))

    bits = [(mask_8 & (1 << level)) != 0 for level in range(3)]
    kind = mask_8 & 3
    flags = jnp.where(sub_8 == 0, mask_8 & 1, jnp.where(sub_8 == 1, (mask_8 >> 1) & 1, (mask_8 >> 2) & 1))
    flags = jnp.where(sub_8 >= 3, (kind == sub_8 - 2).astype(jnp.int32), flags)
    before_r = lax.broadcasted_iota(jnp.int32, (rows, rows), 0)
    before_c = lax.broadcasted_iota(jnp.int32, (rows, rows), 1)
    earlier = jnp.logical_and(before_r % cells == 0, before_r // cells < before_c // cells)
    rank = dot(flags.astype(f32).astype(bf16), jnp.where(earlier, 1.0, 0.0).astype(bf16))
    places = jnp.where(flags != 0, rank * float(cells) + (lane_8 % cells + 1).astype(f32), 0.0)

    def every(i):
        return jnp.broadcast_to(places[i : i + 1], (8, LANES))

    to_level = [every(i) for i in range(3)]
    tag = (lane_8 + 1).astype(f32)

    def picks(count, codes):
        wanted = (lax.broadcasted_iota(jnp.int32, (count, codes.shape[1]), 0) + 1).astype(f32)
        return jnp.where(wanted == codes, 1.0, 0.0).astype(bf16)

    gather = [picks(half, places[i : i + 1]) for i in range(6)]

    def moved(table, which):
        stacked = jnp.zeros((8, LANES), f32)
        for i, line in enumerate(table):
            stacked = jnp.where(sub_8 == i, line, stacked)
        return lax.dot_general(
            stacked.astype(bf16), which, (((1,), (1,)), ((), ())), preferred_element_type=f32
        )

    low_lane = lax.broadcasted_iota(jnp.int32, (1, LANES), 1) < half

    def unless(flag, line):
        return jnp.where(flag, 0.0, line)

    routes = {}
    for name, (i, j, k) in ORDERS.items():
        table = [
            to_level[j], unless(bits[j], to_level[k]), to_level[k],
            unless(jnp.logical_or(bits[j], bits[k]), tag), unless(bits[k], tag),
        ]
        pair = moved(table, jnp.concatenate([gather[i], gather[j]], axis=0))
        second = jnp.concatenate([unless(bits[i], to_level[j])[:1], pair[0:1]], axis=1)
        third = jnp.concatenate(
            [
                unless(jnp.logical_or(bits[i], bits[j]), to_level[k])[:1],
                jnp.where(low_lane, pair[1:2], pair[2:3]),
            ],
            axis=1,
        )
        final = jnp.concatenate(
            [unless(mask_8 != 0, tag)[:1], jnp.where(low_lane, pair[3:4], pair[4:5])], axis=1
        )
        last = moved([tag], gather[k])[:1]
        routes[name] = (gather[i], picks(half, second)[:, : rows + half], picks(half, third), picks(rows, final), picks(rows, last))
    table = [to_level[2], unless(bits[2], tag)]
    near = moved(table, jnp.concatenate(gather[3:5], axis=0))
    both = moved(table, gather[5])
    far_codes = jnp.concatenate([unless(kind != 0, to_level[2])[:1], near[0:1]], axis=1)
    stay_codes = jnp.concatenate([unless(mask_8 != 0, tag)[:1], near[1:2]], axis=1)
    far_pick = (picks(half, far_codes), picks(half, both[0:1]))
    stay_pick = (picks(rows, stay_codes), picks(rows, both[1:2]))
    last_pick = routes["b"][4]

    sends = {"a": a_send, "b": b_send}
    pairs = {"a": a_pair, "b": b_pair}
    lasts = {"a": a_last, "b": b_last}
    columns = {"a": slice(0, wide_half), "b": slice(wide_half, channels)}

    def stage(name, step):
        held = x_ref[:, columns[name]]
        if step:
            held = jnp.concatenate([held, pairs[name][: step * half]], axis=0)
        sends[name][step] = dot(routes[name][step], held).astype(bf16)

    def landing(name, step):
        return lasts[name] if step == 2 else pairs[name].at[pl.ds(step * half, half)]

    def ship(name, step):
        peer = (d ^ (1 << ORDERS[name][step]), b)
        push(name + str(step), sends[name].at[step], landing(name, step), peer)

    def forward(name, step):
        arrived(name + str(step - 1), landing(name, step - 1))
        stage(name, step)
        ship(name, step)

    def features_of(name):
        arrived(name + "2", lasts[name])
        held = jnp.concatenate([x_ref[:, columns[name]], pairs[name][...]], axis=0)
        return dot(routes[name][3], held) + dot(routes[name][4], lasts[name][...])

    def to_rows(ref, at, values):
        for r in range(values.shape[1] // LANES):
            ref[at + r : at + r + 1, :] = values[:, r * LANES : (r + 1) * LANES]

    def to_line(ref, at, values):
        for r in range(values.shape[0]):
            ref[at : at + 1, r * LANES : (r + 1) * LANES] = values[r : r + 1]

    def group_peers(phase, own, every_part):
        every_part[b] = own[...]
        for peer in bn_peers:
            push(phase, own, every_part.at[b], peer)

    def group_stats(phase, every_part):
        arrived(phase, most(every_part))
        lines = every_part.shape[1] // 2
        parts = every_part[...]
        means = parts[:, :lines]
        mean = jnp.sum(means, axis=0) * (1.0 / n_bn)
        spread = jnp.sum(parts[:, lines:], axis=0) + float(rows) * jnp.sum(
            jnp.square(means - mean[None]), axis=0
        )
        return mean, lax.rsqrt(spread * (1.0 / total) + EPS_BN)

    def send_stats(phase, h, own, every_part):
        mean = jnp.sum(h, axis=0, keepdims=True) * (1.0 / rows)
        squares = jnp.sum(jnp.square(h - mean), axis=0, keepdims=True)
        to_rows(own, 0, mean)
        to_rows(own, own.shape[0] // 2, squares)
        group_peers(phase, own, every_part)

    ones = jnp.ones((LANES, LANES), bf16)
    step_rows = queue_ref.shape[0] // QUEUE_STEPS

    def queue_step(c, total_part):
        raw = queue_ref[pl.ds(c * step_rows, step_rows), :].astype(f32)
        square = raw * raw
        high = square.astype(bf16)
        low = (square - high.astype(f32)).astype(bf16)
        norm = dot(high, ones) + dot(low, ones)
        unit = (raw * lax.rsqrt(norm + EPS_UNIT)).astype(bf16)
        flat_queries = query_all[...].reshape(n_dp * slots, query_all.shape[2])
        scores = lax.dot_general(unit, flat_queries, (((1,), (1,)), ((), ())), preferred_element_type=f32)
        terms = jnp.exp(scores * INV_TEMP - INV_TEMP)
        return total_part + jnp.sum(terms.reshape(step_rows // 8, 8, n_dp * slots), axis=0)

    def queue_steps(first, last, total_part):
        return lax.fori_loop(first, last, queue_step, total_part)

    loads[3].wait()
    stage("a", 0)
    stage("b", 0)
    first = None
    for i in range(PANELS):
        panels[i].wait()
        at = slice(i * panel, (i + 1) * panel)
        term = dot(x_ref[:, at], in_ref[at])
        first = term if first is None else first + term
        if i == 0:
            for load in loads[4:]:
                load.start()
    shaped = first.reshape(slots, cells, middle)
    sums = jnp.sum(shaped, axis=1)
    center = exact(local_mean, sums)
    offset = shaped - center[:, None, :]
    squares = jnp.sum(jnp.square(offset), axis=1)
    dev_ref[...] = offset.reshape(rows, middle).astype(bf16)
    for c in range(3):
        class_send[c * half : (c + 1) * half] = dot(gather[3 + c], dev_ref[...]).astype(bf16)
    lines = middle // LANES
    for at, values in ((0, exact(member, sums)), (lines, exact(member, squares))):
        for g in range(n_dp):
            for r in range(lines):
                sum_send[g, at + r : at + r + 1, :] = values[g : g + 1, r * LANES : (r + 1) * LANES]
    sum_recv[d] = sum_send[d]

    pl.semaphore_wait(barrier, n_dp + n_bn - 2)
    for c in range(3):
        at = pl.ds(c * half, half)
        push("class", class_send.at[at], class_recv.at[at], (d ^ (c + 1), b))
    for k in range(1, n_dp):
        push("sum1", sum_send.at[d ^ k], sum_recv.at[d], (d ^ k, b))
    ship("a", 0)
    ship("b", 0)
    column_peers("query", query_own, query_all)

    part = jnp.zeros((8, n_dp * slots), f32)
    loads[4].wait()

    arrived("sum1", most(sum_recv))
    parts = sum_recv[...]
    class_sums = parts[:, :lines]
    column_mean = jnp.sum(class_sums, axis=0) * (1.0 / rows)
    column_squares = jnp.sum(parts[:, lines:], axis=0)
    class_means = []
    for e in range(n_dp):
        class_means.append(class_sums[e] / jnp.maximum(counts[e], 1.0))
        column_squares = column_squares + counts[e] * jnp.square(class_means[e] - column_mean)
    own1[:lines] = column_mean
    own1[lines:] = column_squares
    group_peers("bn1", own1, all1)

    arrived("class", class_recv)
    near_held = jnp.concatenate([dev_ref[...], class_recv[:rows]], axis=0)
    far_send[...] = (dot(far_pick[0], near_held) + dot(far_pick[1], class_recv[rows:])).astype(bf16)
    push("far", far_send, far_recv, (d ^ 4, b))

    h_ref[...] = dot(stay_pick[0], near_held) + dot(stay_pick[1], class_recv[rows:])
    arrived("query", most(query_all))
    part = queue_steps(0, 1, part)
    forward("b", 1)
    forward("a", 1)

    mean, scale = group_stats("bn1", all1)
    for e in range(n_dp):
        to_line(class_ref, e, class_means[e] - mean)
    to_line(scale_ref, 0, scale)
    loads[5].wait()

    arrived("far", far_recv)
    h_ref[...] = h_ref[...] + dot(last_pick, far_recv[...])
    for s in range(slots):
        at = slice(s * cells, (s + 1) * cells)
        move = jnp.broadcast_to(class_ref[pl.ds(sources[s], 1), :], (cells, middle))
        h_ref[at] = jax.nn.relu((h_ref[at] + move) * scale_ref[0:1, :middle])
    act = h_ref[...]
    cell = lax.broadcasted_iota(jnp.int32, act.shape, 0) % cells
    before = jnp.where(cell == 0, 0.0, pltpu.roll(act, 1, 0)).astype(bf16)
    after = jnp.where(cell == cells - 1, 0.0, pltpu.roll(act, rows - 1, 0)).astype(bf16)
    h_ref[...] = dot(before, mid_ref[0]) + dot(act.astype(bf16), mid_ref[1]) + dot(after, mid_ref[2])
    send_stats("bn2", h_ref[...], own2, all2)
    part = queue_steps(1, 3, part)
    forward("b", 2)
    forward("a", 2)
    loads[6].wait()
    mean, scale = group_stats("bn2", all2)
    to_line(mean_ref, 0, mean)
    to_line(scale_ref, 0, scale)

    second = jax.nn.relu((h_ref[...] - mean_ref[0:1, :middle]) * scale_ref[0:1, :middle]).astype(bf16)
    wide_ref[...] = dot(second, out_ref[...])
    send_stats("bn3", wide_ref[...], own3, all3)
    part = queue_steps(3, 8, part)
    part_own[...] = jnp.sum(part, axis=0, keepdims=True)
    part_all[d] = part_own[...]
    column_peers("queue", part_own, part_all)
    loads[7].wait()
    mean, scale = group_stats("bn3", all3)
    to_line(mean_ref, 0, mean)
    to_line(scale_ref, 0, scale)

    z = None
    for name in ("a", "b"):
        at = columns[name]
        normal = (wide_ref[:, at] - mean_ref[0:1, at]) * scale_ref[0:1, at]
        block = jax.nn.relu(normal + features_of(name)).astype(bf16)
        pooled = jnp.mean(block.astype(f32).reshape(slots, cells, wide_half), axis=1).astype(bf16)
        term = dot(pooled, head_ref[at])
        z = term if z is None else z + term
    key_own[...] = (z * lax.rsqrt(jnp.sum(z * z, axis=-1, keepdims=True) + EPS_UNIT)).astype(bf16)
    key_all[d] = key_own[...]
    column_peers("key", key_own, key_all)

    arrived("queue", most(part_all))
    negative_all = jnp.sum(part_all[...], axis=0)
    mine = lax.broadcasted_iota(jnp.int32, (slots, n_dp * slots), 1) == (
        lax.broadcasted_iota(jnp.int32, (slots, n_dp * slots), 0) + d * slots
    )
    negative_col = jnp.sum(jnp.where(mine, negative_all, 0.0), axis=1, keepdims=True)
    negative = jnp.sum(jnp.where(lane == sub, negative_col, 0.0), axis=0, keepdims=True)

    arrived("key", most(key_all))
    keys = key_all[...].reshape(n_dp * slots, key_all.shape[2])
    products = lax.dot_general(keys, query_own[...], (((1,), (1,)), ((), ())), preferred_element_type=f32)
    chosen = lax.broadcasted_iota(jnp.int32, products.shape, 0) == want
    logit = jnp.sum(jnp.where(chosen, products, 0.0), axis=0, keepdims=True) * INV_TEMP
    loss_ref[...] = jnp.log(jnp.exp(logit - INV_TEMP) + negative) + INV_TEMP - logit

    for phase, every_part in (("query", query_all), ("queue", part_all), ("key", key_all), ("sum1", sum_recv), ("bn1", all1), ("bn2", all2), ("bn3", all3)):
        sent(phase, most(every_part))
    sent("class", class_send)
    sent("far", far_send)
    for name in ("a", "b"):
        for step in range(3):
            sent(name + str(step), sends[name].at[step])


def on_device_shuffled(n_dp, n_bn, features, shuffle_masks, conv_in, conv_mid, conv_out, head, queries, queue, positive):
    f32, bf16 = jnp.float32, jnp.bfloat16
    slots, cells, channels = features.shape
    rows = slots * cells
    middle = conv_in.shape[1]
    width = queries.shape[1]

    def group_parts(c):
        tile = (2 * (c // LANES), LANES)
        return [pltpu.VMEM(tile, f32), pltpu.VMEM((n_bn,) + tile, f32)]

    half_features = [
        pltpu.VMEM((3, rows // 2, channels // 2), bf16),
        pltpu.VMEM((rows, channels // 2), bf16),
        pltpu.VMEM((rows // 2, channels // 2), bf16),
    ]
    sums = pltpu.VMEM((n_dp, 2 * (middle // LANES), LANES), f32)
    hbm = pl.BlockSpec(memory_space=pltpu.HBM)
    loss = pl.pallas_call(
        functools.partial(shuffled_kernel, n_dp, n_bn),
        out_shape=jax.ShapeDtypeStruct((1, slots), f32),
        in_specs=[hbm] * 9,
        out_specs=pl.BlockSpec(memory_space=pltpu.VMEM),
        scratch_shapes=[
            pltpu.SMEM(shuffle_masks.shape, jnp.int32),
            pltpu.SMEM(positive.shape, jnp.int32),
            pltpu.VMEM(queries.shape, bf16),
            pltpu.VMEM((rows, channels), bf16),
            pltpu.VMEM(conv_in.shape, bf16),
            pltpu.VMEM(conv_mid.shape, bf16),
            pltpu.VMEM(conv_out.shape, bf16),
            pltpu.VMEM(head.shape, bf16),
            pltpu.VMEM(queue.shape, bf16),
            pltpu.VMEM((rows, middle), f32),
            pltpu.VMEM((rows, channels), f32),
            pltpu.VMEM((n_dp, middle), f32),
            pltpu.VMEM((8, channels), f32),
            pltpu.VMEM((8, channels), f32),
            pltpu.VMEM((rows, middle), bf16),
            pltpu.VMEM((3 * rows // 2, middle), bf16),
            pltpu.VMEM((3 * rows // 2, middle), bf16),
            pltpu.VMEM((rows // 2, middle), bf16),
            pltpu.VMEM((rows // 2, middle), bf16),
        ]
        + half_features * 2
        + [sums, sums]
        + group_parts(middle)
        + group_parts(middle)
        + group_parts(channels)
        + [
            pltpu.VMEM((slots, width), bf16),
            pltpu.VMEM((n_dp, slots, width), bf16),
            pltpu.VMEM((1, n_dp * slots), f32),
            pltpu.VMEM((n_dp, 1, n_dp * slots), f32),
            pltpu.VMEM((slots, width), bf16),
            pltpu.VMEM((n_dp, slots, width), bf16),
            pltpu.SemaphoreType.DMA((8,)),
            pltpu.SemaphoreType.DMA((PANELS,)),
            pltpu.SemaphoreType.DMA((len(PHASES),)),
            pltpu.SemaphoreType.DMA((len(PHASES),)),
        ],
        compiler_params=pltpu.CompilerParams(
            collective_id=0, has_side_effects=True, vmem_limit_bytes=48 << 20
        ),
        name="shuffled_crops",
    )(shuffle_masks, positive, queries, features.reshape(rows, channels), conv_in, conv_mid, conv_out, head, queue)
    return loss.reshape(slots)


def on_device(n_dp, n_bn, *arrays):
    features, conv_in = arrays[0], arrays[2]
    slots, cells, channels = features.shape
    whole_lanes = conv_in.shape[1] % (2 * LANES) == 0 and channels % (4 * LANES) == 0
    if whole_lanes and n_dp == 8 and slots * cells == LANES and cells == 8 and n_bn <= 4:
        return on_device_shuffled(n_dp, n_bn, *arrays)
    return on_device_moving(*arrays)


def solution(mesh):
    return jax.shard_map(
        functools.partial(on_device, mesh.shape["dp"], mesh.shape["bn"]),
        mesh=mesh,
        in_specs=(
            P(("dp", "bn"), None, None),
            P(),
            P(),
            P(),
            P(),
            P(),
            P(("dp", "bn"), None),
            P("dp", None),
            P(("dp", "bn")),
        ),
        out_specs=P(("dp", "bn")),
        check_vma=False,
    )
```

```python
import functools

import jax
import jax.numpy as jnp
from jax import lax
from jax.experimental import pallas as pl
from jax.experimental.pallas import tpu as pltpu
from jax.sharding import PartitionSpec as P

EPS_BN = 1e-05
EPS_UNIT = 1e-06
INV_TEMP = 1.0 / 0.07


def partner_2(value, axis, distance):
    return lax.ppermute(value, axis, [(i, i ^ 1 << distance) for i in range(lax.axis_size(axis))])


def unit_rows(values):
    values = values.astype(jnp.float32)
    return values * lax.rsqrt(jnp.sum(values * values, axis=-1, keepdims=True) + EPS_UNIT)


def group_norm(values, row_total):
    first = lax.psum(jnp.sum(values, axis=0), "bn")
    center = first / row_total
    spread = lax.psum(jnp.sum(jnp.square(values - center), axis=0), "bn") / row_total
    return (values - center) * lax.rsqrt(spread + EPS_BN)


def moving_slots(shuffle_masks, level, half):
    flags = jnp.bitwise_and(jnp.right_shift(shuffle_masks, level), 1)
    return jnp.argsort(1 - flags, stable=True)[:half]


def on_device_moving(features, shuffle_masks, conv_in, conv_mid, conv_out, head, queries, queue, positive):
    dp_count = lax.axis_size("dp")
    bn_count = lax.axis_size("bn")
    bit_count = dp_count.bit_length() - 1
    crop_dev, positions, channels = features.shape
    half = crop_dev // 2
    middle = conv_in.shape[1]
    query_unit = unit_rows(queries).astype(jnp.bfloat16)
    query_all = lax.all_gather(query_unit, "dp", axis=0, tiled=True)
    shuffled = features
    for level in range(bit_count):
        moving = moving_slots(shuffle_masks, level, half)
        chosen = (moving[:, None] == jnp.arange(crop_dev)[None, :]).astype(jnp.bfloat16)
        leaving = jnp.dot(
            chosen, shuffled.reshape(crop_dev, positions * channels), preferred_element_type=jnp.float32
        ).astype(jnp.bfloat16)
        partner = partner_2(leaving.reshape(half, positions, channels), "dp", level)
        shuffled = shuffled.at[moving].set(partner)
    row_total = crop_dev * positions * bn_count
    flat_rows = shuffled.reshape(crop_dev * positions, channels)
    first_sum = jnp.dot(flat_rows, conv_in, preferred_element_type=jnp.float32)
    first_act = jax.nn.relu(group_norm(first_sum, row_total)).astype(jnp.bfloat16)
    tap_maps = first_act.reshape(crop_dev, positions, middle)
    padded = jnp.pad(tap_maps, ((0, 0), (1, 1), (0, 0)))
    stacked = jnp.concatenate([padded[:, tap : tap + positions, :] for tap in range(3)], axis=2)
    second_sum = jnp.dot(
        stacked.reshape(crop_dev * positions, 3 * middle),
        conv_mid.reshape(3 * middle, middle),
        preferred_element_type=jnp.float32,
    )
    second_act = jax.nn.relu(group_norm(second_sum, row_total)).astype(jnp.bfloat16)
    third_sum = jnp.dot(second_act, conv_out, preferred_element_type=jnp.float32)
    block = jax.nn.relu(group_norm(third_sum, row_total) + flat_rows.astype(jnp.float32)).astype(
        jnp.bfloat16
    )
    pooled = jnp.mean(
        block.reshape(crop_dev, positions, channels).astype(jnp.float32), axis=1
    ).astype(jnp.bfloat16)
    key_unit = unit_rows(jnp.dot(pooled, head, preferred_element_type=jnp.float32)).astype(
        jnp.bfloat16
    )
    for level in range(bit_count):
        moving = moving_slots(shuffle_masks, level, half)
        partner = partner_2(jnp.take(key_unit, moving, axis=0), "dp", level)
        key_unit = key_unit.at[moving].set(partner)
    queue_unit = unit_rows(queue).astype(jnp.bfloat16)
    scores = jnp.dot(query_all, queue_unit.T, preferred_element_type=jnp.float32) * INV_TEMP
    queue_part = jnp.sum(jnp.exp(scores - INV_TEMP), axis=1)
    key_all = lax.all_gather(key_unit, "dp", axis=0, tiled=True)
    slot_of = positive % crop_dev
    column = positive // crop_dev // bn_count
    picked = jnp.take(key_all, column * crop_dev + slot_of, axis=0)
    positive_logit = (
        jnp.sum(query_unit.astype(jnp.float32) * picked.astype(jnp.float32), axis=-1) * INV_TEMP
    )
    negative = lax.psum_scatter(queue_part, "dp", scatter_dimension=0, tiled=True)
    return jnp.log(jnp.exp(positive_logit - INV_TEMP) + negative) + INV_TEMP - positive_logit


MESH = pl.DeviceIdType.MESH
LANES = 128
QUEUE_STEPS = 8
PANELS = 4
PHASES = (
    "query", "queue", "key", "sum1", "bn1", "bn2", "bn3", "class", "far",
    "a0", "a1", "a2", "b0", "b1", "b2",
)
ORDERS = {"a": (2, 0, 1), "b": (0, 1, 2)}


def shuffled_kernel(
    n_dp, n_bn,
    masks_hbm, positive_hbm, queries_hbm, x_hbm, in_hbm, mid_hbm, out_hbm, head_hbm, queue_hbm,
    loss_ref,
    masks, positive, queries,
    x_ref, in_ref, mid_ref, out_ref, head_ref, queue_ref,
    h_ref, wide_ref, class_ref, mean_ref, scale_ref,
    dev_ref, class_send, class_recv, far_send, far_recv,
    a_send, a_pair, a_last, b_send, b_pair, b_last,
    sum_send, sum_recv, own1, all1, own2, all2, own3, all3,
    query_own, query_all, part_own, part_all, key_own, key_all,
    load_sem, panel_sem, send_sem, recv_sem,
):
    f32, bf16 = jnp.float32, jnp.bfloat16
    d = lax.axis_index("dp")
    b = lax.axis_index("bn")
    rows, channels = x_ref.shape
    slots = masks.shape[0]
    cells = rows // slots
    half = rows // 2
    middle = in_ref.shape[1]
    wide_half = channels // 2
    total = float(rows * n_bn)

    panel = channels // PANELS
    panels = [
        pltpu.make_async_copy(
            in_hbm.at[pl.ds(i * panel, panel)], in_ref.at[pl.ds(i * panel, panel)], panel_sem.at[i]
        )
        for i in range(PANELS)
    ]
    loads = [
        pltpu.make_async_copy(src, dst, load_sem.at[i])
        for i, (src, dst) in enumerate(
            [(masks_hbm, masks), (positive_hbm, positive), (queries_hbm, queries), (x_hbm, x_ref), (queue_hbm, queue_ref), (mid_hbm, mid_ref), (out_hbm, out_ref), (head_hbm, head_ref)]
        )
    ]
    for load in loads[:4] + panels:
        load.start()

    barrier = pltpu.get_barrier_semaphore()
    dp_peers = [(d ^ k, b) for k in range(1, n_dp)]
    bn_peers = [(d, lax.rem(b + k, n_bn)) for k in range(1, n_bn)]
    for peer in dp_peers + bn_peers:
        pl.semaphore_signal(barrier, inc=1, device_id=peer, device_id_type=MESH)

    def push(phase, src, dst, peer):
        i = PHASES.index(phase)
        pltpu.make_async_remote_copy(
            src_ref=src, dst_ref=dst, send_sem=send_sem.at[i], recv_sem=recv_sem.at[i],
            device_id=peer, device_id_type=MESH,
        ).start()

    def arrived(phase, view):
        pltpu.make_async_copy(view, view, recv_sem.at[PHASES.index(phase)]).wait()

    def sent(phase, view):
        pltpu.make_async_copy(view, view, send_sem.at[PHASES.index(phase)]).wait()

    def most(ref):
        return ref.at[pl.ds(0, ref.shape[0] - 1)]

    def column_peers(phase, src, dst):
        for peer in dp_peers:
            push(phase, src, dst.at[d], peer)

    def exact(a, c):
        return jnp.dot(a, c, preferred_element_type=f32, precision=lax.Precision.HIGHEST)

    def dot(a, c):
        return jnp.dot(a, c, preferred_element_type=f32)

    for load in loads[:3]:
        load.wait()

    q = queries[...].astype(f32)
    query_unit = (q * lax.rsqrt(jnp.sum(q * q, axis=-1, keepdims=True) + EPS_UNIT)).astype(bf16)
    query_own[...] = query_unit
    query_all[d] = query_unit

    lane = lax.broadcasted_iota(jnp.int32, (slots, slots), 1)
    sub = lax.broadcasted_iota(jnp.int32, (slots, slots), 0)
    lane1 = lax.broadcasted_iota(jnp.int32, (1, slots), 1)
    lane_8 = lax.broadcasted_iota(jnp.int32, (8, LANES), 1)
    sub_8 = lax.broadcasted_iota(jnp.int32, (8, LANES), 0)
    slot_8 = lane_8 // cells
    mask_row = jnp.zeros((slots, slots), jnp.int32)
    mask_col = jnp.zeros((slots, slots), jnp.int32)
    want = jnp.zeros((1, slots), jnp.int32)
    mask_8 = jnp.zeros((8, LANES), jnp.int32)
    sources = []
    for s in range(slots):
        mask = masks[s]
        sources.append(mask ^ d)
        mask_row = jnp.where(lane == s, sources[s], mask_row)
        mask_col = jnp.where(sub == s, sources[s], mask_col)
        mask_8 = jnp.where(slot_8 == s, mask, mask_8)
        place = positive[s]
        slot = lax.rem(place, slots)
        column = lax.div(place, slots * n_bn) ^ masks[slot]
        want = jnp.where(lane1 == s, column * slots + slot, want)
    same = (mask_row == mask_col).astype(f32)
    local_mean = same / (jnp.sum(same, axis=0, keepdims=True) * float(cells))
    member = (mask_row[:n_dp] == sub[:n_dp]).astype(f32)
    counts = []
    for e in range(n_dp):
        count = jnp.int32(0)
        for s in range(slots):
            count = count + (sources[s] == e).astype(jnp.int32)
        counts.append((count * cells).astype(f32))

    bits = [(mask_8 & (1 << level)) != 0 for level in range(3)]
    kind = mask_8 & 3
    flags = jnp.where(sub_8 == 0, mask_8 & 1, jnp.where(sub_8 == 1, (mask_8 >> 1) & 1, (mask_8 >> 2) & 1))
    flags = jnp.where(sub_8 >= 3, (kind == sub_8 - 2).astype(jnp.int32), flags)
    before_r = lax.broadcasted_iota(jnp.int32, (rows, rows), 0)
    before_c = lax.broadcasted_iota(jnp.int32, (rows, rows), 1)
    earlier = jnp.logical_and(before_r % cells == 0, before_r // cells < before_c // cells)
    rank = dot(flags.astype(f32).astype(bf16), jnp.where(earlier, 1.0, 0.0).astype(bf16))
    places = jnp.where(flags != 0, rank * float(cells) + (lane_8 % cells + 1).astype(f32), 0.0)

    def every(i):
        return jnp.broadcast_to(places[i : i + 1], (8, LANES))

    to_level = [every(i) for i in range(3)]
    tag = (lane_8 + 1).astype(f32)

    def picks(count, codes):
        wanted = (lax.broadcasted_iota(jnp.int32, (count, codes.shape[1]), 0) + 1).astype(f32)
        return jnp.where(wanted == codes, 1.0, 0.0).astype(bf16)

    gather = [picks(half, places[i : i + 1]) for i in range(6)]

    def moved(table, which):
        stacked = jnp.zeros((8, LANES), f32)
        for i, line in enumerate(table):
            stacked = jnp.where(sub_8 == i, line, stacked)
        return lax.dot_general(
            stacked.astype(bf16), which, (((1,), (1,)), ((), ())), preferred_element_type=f32
        )

    low_lane = lax.broadcasted_iota(jnp.int32, (1, LANES), 1) < half

    def unless(flag, line):
        return jnp.where(flag, 0.0, line)

    routes = {}
    for name, (i, j, k) in ORDERS.items():
        table = [
            to_level[j], unless(bits[j], to_level[k]), to_level[k],
            unless(jnp.logical_or(bits[j], bits[k]), tag), unless(bits[k], tag),
        ]
        pair = moved(table, jnp.concatenate([gather[i], gather[j]], axis=0))
        second = jnp.concatenate([unless(bits[i], to_level[j])[:1], pair[0:1]], axis=1)
        third = jnp.concatenate(
            [
                unless(jnp.logical_or(bits[i], bits[j]), to_level[k])[:1],
                jnp.where(low_lane, pair[1:2], pair[2:3]),
            ],
            axis=1,
        )
        final = jnp.concatenate(
            [unless(mask_8 != 0, tag)[:1], jnp.where(low_lane, pair[3:4], pair[4:5])], axis=1
        )
        last = moved([tag], gather[k])[:1]
        routes[name] = (gather[i], picks(half, second)[:, : rows + half], picks(half, third), picks(rows, final), picks(rows, last))
    table = [to_level[2], unless(bits[2], tag)]
    near = moved(table, jnp.concatenate(gather[3:5], axis=0))
    both = moved(table, gather[5])
    far_codes = jnp.concatenate([unless(kind != 0, to_level[2])[:1], near[0:1]], axis=1)
    stay_codes = jnp.concatenate([unless(mask_8 != 0, tag)[:1], near[1:2]], axis=1)
    far_pick = (picks(half, far_codes), picks(half, both[0:1]))
    stay_pick = (picks(rows, stay_codes), picks(rows, both[1:2]))
    last_pick = routes["b"][4]

    sends = {"a": a_send, "b": b_send}
    pairs = {"a": a_pair, "b": b_pair}
    lasts = {"a": a_last, "b": b_last}
    columns = {"a": slice(0, wide_half), "b": slice(wide_half, channels)}

    def stage(name, step):
        held = x_ref[:, columns[name]]
        if step:
            held = jnp.concatenate([held, pairs[name][: step * half]], axis=0)
        sends[name][step] = dot(routes[name][step], held).astype(bf16)

    def landing(name, step):
        return lasts[name] if step == 2 else pairs[name].at[pl.ds(step * half, half)]

    def ship(name, step):
        peer = (d ^ (1 << ORDERS[name][step]), b)
        push(name + str(step), sends[name].at[step], landing(name, step), peer)

    def forward(name, step):
        arrived(name + str(step - 1), landing(name, step - 1))
        stage(name, step)
        ship(name, step)

    def features_of(name):
        arrived(name + "2", lasts[name])
        held = jnp.concatenate([x_ref[:, columns[name]], pairs[name][...]], axis=0)
        return dot(routes[name][3], held) + dot(routes[name][4], lasts[name][...])

    def to_rows(ref, at, values):
        for r in range(values.shape[1] // LANES):
            ref[at + r : at + r + 1, :] = values[:, r * LANES : (r + 1) * LANES]

    def to_line(ref, at, values):
        for r in range(values.shape[0]):
            ref[at : at + 1, r * LANES : (r + 1) * LANES] = values[r : r + 1]

    def group_peers(phase, own, every_part):
        every_part[b] = own[...]
        for peer in bn_peers:
            push(phase, own, every_part.at[b], peer)

    def group_stats(phase, every_part):
        arrived(phase, most(every_part))
        lines = every_part.shape[1] // 2
        parts = every_part[...]
        means = parts[:, :lines]
        mean = jnp.sum(means, axis=0) * (1.0 / n_bn)
        spread = jnp.sum(parts[:, lines:], axis=0) + float(rows) * jnp.sum(
            jnp.square(means - mean[None]), axis=0
        )
        return mean, lax.rsqrt(spread * (1.0 / total) + EPS_BN)

    def send_stats(phase, h, own, every_part):
        mean = jnp.sum(h, axis=0, keepdims=True) * (1.0 / rows)
        squares = jnp.sum(jnp.square(h - mean), axis=0, keepdims=True)
        to_rows(own, 0, mean)
        to_rows(own, own.shape[0] // 2, squares)
        group_peers(phase, own, every_part)

    ones = jnp.ones((LANES, LANES), bf16)
    step_rows = queue_ref.shape[0] // QUEUE_STEPS

    def queue_step(c, total_part):
        raw = queue_ref[pl.ds(c * step_rows, step_rows), :].astype(f32)
        square = raw * raw
        high = square.astype(bf16)
        low = (square - high.astype(f32)).astype(bf16)
        norm = dot(high, ones) + dot(low, ones)
        unit = (raw * lax.rsqrt(norm + EPS_UNIT)).astype(bf16)
        flat_queries = query_all[...].reshape(n_dp * slots, query_all.shape[2])
        scores = lax.dot_general(unit, flat_queries, (((1,), (1,)), ((), ())), preferred_element_type=f32)
        terms = jnp.exp(scores * INV_TEMP - INV_TEMP)
        return total_part + jnp.sum(terms.reshape(step_rows // 8, 8, n_dp * slots), axis=0)

    def queue_steps(first, last, total_part):
        return lax.fori_loop(first, last, queue_step, total_part)

    loads[3].wait()
    stage("a", 0)
    stage("b", 0)
    first = None
    for i in range(PANELS):
        panels[i].wait()
        at = slice(i * panel, (i + 1) * panel)
        term = dot(x_ref[:, at], in_ref[at])
        first = term if first is None else first + term
        if i == 0:
            for load in loads[4:]:
                load.start()
    shaped = first.reshape(slots, cells, middle)
    sums = jnp.sum(shaped, axis=1)
    center = exact(local_mean, sums)
    offset = shaped - center[:, None, :]
    squares = jnp.sum(jnp.square(offset), axis=1)
    dev_ref[...] = offset.reshape(rows, middle).astype(bf16)
    for c in range(3):
        class_send[c * half : (c + 1) * half] = dot(gather[3 + c], dev_ref[...]).astype(bf16)
    lines = middle // LANES
    for at, values in ((0, exact(member, sums)), (lines, exact(member, squares))):
        for g in range(n_dp):
            for r in range(lines):
                sum_send[g, at + r : at + r + 1, :] = values[g : g + 1, r * LANES : (r + 1) * LANES]
    sum_recv[d] = sum_send[d]

    pl.semaphore_wait(barrier, n_dp + n_bn - 2)
    for c in range(3):
        at = pl.ds(c * half, half)
        push("class", class_send.at[at], class_recv.at[at], (d ^ (c + 1), b))
    for k in range(1, n_dp):
        push("sum1", sum_send.at[d ^ k], sum_recv.at[d], (d ^ k, b))
    ship("a", 0)
    ship("b", 0)
    column_peers("query", query_own, query_all)

    part = jnp.zeros((8, n_dp * slots), f32)
    loads[4].wait()

    arrived("sum1", most(sum_recv))
    parts = sum_recv[...]
    class_sums = parts[:, :lines]
    column_mean = jnp.sum(class_sums, axis=0) * (1.0 / rows)
    column_squares = jnp.sum(parts[:, lines:], axis=0)
    class_means = []
    for e in range(n_dp):
        class_means.append(class_sums[e] / jnp.maximum(counts[e], 1.0))
        column_squares = column_squares + counts[e] * jnp.square(class_means[e] - column_mean)
    own1[:lines] = column_mean
    own1[lines:] = column_squares
    group_peers("bn1", own1, all1)

    arrived("class", class_recv)
    near_held = jnp.concatenate([dev_ref[...], class_recv[:rows]], axis=0)
    far_send[...] = (dot(far_pick[0], near_held) + dot(far_pick[1], class_recv[rows:])).astype(bf16)
    push("far", far_send, far_recv, (d ^ 4, b))

    h_ref[...] = dot(stay_pick[0], near_held) + dot(stay_pick[1], class_recv[rows:])
    arrived("query", most(query_all))
    part = queue_steps(0, 1, part)
    forward("b", 1)
    forward("a", 1)

    mean, scale = group_stats("bn1", all1)
    for e in range(n_dp):
        to_line(class_ref, e, class_means[e] - mean)
    to_line(scale_ref, 0, scale)
    loads[5].wait()

    arrived("far", far_recv)
    h_ref[...] = h_ref[...] + dot(last_pick, far_recv[...])
    for s in range(slots):
        at = slice(s * cells, (s + 1) * cells)
        move = jnp.broadcast_to(class_ref[pl.ds(sources[s], 1), :], (cells, middle))
        h_ref[at] = jax.nn.relu((h_ref[at] + move) * scale_ref[0:1, :middle])
    act = h_ref[...]
    cell = lax.broadcasted_iota(jnp.int32, act.shape, 0) % cells
    before = jnp.where(cell == 0, 0.0, pltpu.roll(act, 1, 0)).astype(bf16)
    after = jnp.where(cell == cells - 1, 0.0, pltpu.roll(act, rows - 1, 0)).astype(bf16)
    h_ref[...] = dot(before, mid_ref[0]) + dot(act.astype(bf16), mid_ref[1]) + dot(after, mid_ref[2])
    send_stats("bn2", h_ref[...], own2, all2)
    part = queue_steps(1, 3, part)
    forward("b", 2)
    forward("a", 2)
    loads[6].wait()
    mean, scale = group_stats("bn2", all2)
    to_line(mean_ref, 0, mean)
    to_line(scale_ref, 0, scale)

    second = jax.nn.relu((h_ref[...] - mean_ref[0:1, :middle]) * scale_ref[0:1, :middle]).astype(bf16)
    wide_ref[...] = dot(second, out_ref[...])
    send_stats("bn3", wide_ref[...], own3, all3)
    part = queue_steps(3, 8, part)
    part_own[...] = jnp.sum(part, axis=0, keepdims=True)
    part_all[d] = part_own[...]
    column_peers("queue", part_own, part_all)
    loads[7].wait()
    mean, scale = group_stats("bn3", all3)
    to_line(mean_ref, 0, mean)
    to_line(scale_ref, 0, scale)

    z = None
    for name in ("a", "b"):
        at = columns[name]
        normal = (wide_ref[:, at] - mean_ref[0:1, at]) * scale_ref[0:1, at]
        block = jax.nn.relu(normal + features_of(name)).astype(bf16)
        pooled = jnp.mean(block.astype(f32).reshape(slots, cells, wide_half), axis=1).astype(bf16)
        term = dot(pooled, head_ref[at])
        z = term if z is None else z + term
    key_own[...] = (z * lax.rsqrt(jnp.sum(z * z, axis=-1, keepdims=True) + EPS_UNIT)).astype(bf16)
    key_all[d] = key_own[...]
    column_peers("key", key_own, key_all)

    arrived("queue", most(part_all))
    negative_all = jnp.sum(part_all[...], axis=0)
    mine = lax.broadcasted_iota(jnp.int32, (slots, n_dp * slots), 1) == (
        lax.broadcasted_iota(jnp.int32, (slots, n_dp * slots), 0) + d * slots
    )
    negative_col = jnp.sum(jnp.where(mine, negative_all, 0.0), axis=1, keepdims=True)
    negative = jnp.sum(jnp.where(lane == sub, negative_col, 0.0), axis=0, keepdims=True)

    arrived("key", most(key_all))
    keys = key_all[...].reshape(n_dp * slots, key_all.shape[2])
    products = lax.dot_general(keys, query_own[...], (((1,), (1,)), ((), ())), preferred_element_type=f32)
    chosen = lax.broadcasted_iota(jnp.int32, products.shape, 0) == want
    logit = jnp.sum(jnp.where(chosen, products, 0.0), axis=0, keepdims=True) * INV_TEMP
    loss_ref[...] = jnp.log(jnp.exp(logit - INV_TEMP) + negative) + INV_TEMP - logit

    for phase, every_part in (("query", query_all), ("queue", part_all), ("key", key_all), ("sum1", sum_recv), ("bn1", all1), ("bn2", all2), ("bn3", all3)):
        sent(phase, most(every_part))
    sent("class", class_send)
    sent("far", far_send)
    for name in ("a", "b"):
        for step in range(3):
            sent(name + str(step), sends[name].at[step])


def on_device_shuffled(n_dp, n_bn, features, shuffle_masks, conv_in, conv_mid, conv_out, head, queries, queue, positive):
    f32, bf16 = jnp.float32, jnp.bfloat16
    slots, cells, channels = features.shape
    rows = slots * cells
    middle = conv_in.shape[1]
    width = queries.shape[1]

    def group_parts(c):
        tile = (2 * (c // LANES), LANES)
        return [pltpu.VMEM(tile, f32), pltpu.VMEM((n_bn,) + tile, f32)]

    half_features = [
        pltpu.VMEM((3, rows // 2, channels // 2), bf16),
        pltpu.VMEM((rows, channels // 2), bf16),
        pltpu.VMEM((rows // 2, channels // 2), bf16),
    ]
    sums = pltpu.VMEM((n_dp, 2 * (middle // LANES), LANES), f32)
    hbm = pl.BlockSpec(memory_space=pltpu.HBM)
    loss = pl.pallas_call(
        functools.partial(shuffled_kernel, n_dp, n_bn),
        out_shape=jax.ShapeDtypeStruct((1, slots), f32),
        in_specs=[hbm] * 9,
        out_specs=pl.BlockSpec(memory_space=pltpu.VMEM),
        scratch_shapes=[
            pltpu.SMEM(shuffle_masks.shape, jnp.int32),
            pltpu.SMEM(positive.shape, jnp.int32),
            pltpu.VMEM(queries.shape, bf16),
            pltpu.VMEM((rows, channels), bf16),
            pltpu.VMEM(conv_in.shape, bf16),
            pltpu.VMEM(conv_mid.shape, bf16),
            pltpu.VMEM(conv_out.shape, bf16),
            pltpu.VMEM(head.shape, bf16),
            pltpu.VMEM(queue.shape, bf16),
            pltpu.VMEM((rows, middle), f32),
            pltpu.VMEM((rows, channels), f32),
            pltpu.VMEM((n_dp, middle), f32),
            pltpu.VMEM((8, channels), f32),
            pltpu.VMEM((8, channels), f32),
            pltpu.VMEM((rows, middle), bf16),
            pltpu.VMEM((3 * rows // 2, middle), bf16),
            pltpu.VMEM((3 * rows // 2, middle), bf16),
            pltpu.VMEM((rows // 2, middle), bf16),
            pltpu.VMEM((rows // 2, middle), bf16),
        ]
        + half_features * 2
        + [sums, sums]
        + group_parts(middle)
        + group_parts(middle)
        + group_parts(channels)
        + [
            pltpu.VMEM((slots, width), bf16),
            pltpu.VMEM((n_dp, slots, width), bf16),
            pltpu.VMEM((1, n_dp * slots), f32),
            pltpu.VMEM((n_dp, 1, n_dp * slots), f32),
            pltpu.VMEM((slots, width), bf16),
            pltpu.VMEM((n_dp, slots, width), bf16),
            pltpu.SemaphoreType.DMA((8,)),
            pltpu.SemaphoreType.DMA((PANELS,)),
            pltpu.SemaphoreType.DMA((len(PHASES),)),
            pltpu.SemaphoreType.DMA((len(PHASES),)),
        ],
        compiler_params=pltpu.CompilerParams(
            collective_id=0, has_side_effects=True, vmem_limit_bytes=64 << 20
        ),
        name="shuffled_crops",
    )(shuffle_masks, positive, queries, features.reshape(rows, channels), conv_in, conv_mid, conv_out, head, queue)
    return loss.reshape(slots)


def on_device(n_dp, n_bn, *arrays):
    features, conv_in = arrays[0], arrays[2]
    slots, cells, channels = features.shape
    whole_lanes = conv_in.shape[1] % (2 * LANES) == 0 and channels % (4 * LANES) == 0
    if whole_lanes and n_dp == 8 and slots * cells == LANES and cells == 8 and n_bn <= 4:
        return on_device_shuffled(n_dp, n_bn, *arrays)
    return on_device_moving(*arrays)


def solution(mesh):
    return jax.shard_map(
        functools.partial(on_device, mesh.shape["dp"], mesh.shape["bn"]),
        mesh=mesh,
        in_specs=(
            P(("dp", "bn"), None, None),
            P(),
            P(),
            P(),
            P(),
            P(),
            P(("dp", "bn"), None),
            P("dp", None),
            P(("dp", "bn")),
        ),
        out_specs=P(("dp", "bn")),
        check_vma=False,
    )
```

```python
import functools

import jax
import jax.numpy as jnp
from jax import lax
from jax.experimental import pallas as pl
from jax.experimental.pallas import tpu as pltpu
from jax.sharding import PartitionSpec as P

EPS_BN = 1e-05
EPS_UNIT = 1e-06
INV_TEMP = 1.0 / 0.07


def partner_2(value, axis, distance):
    return lax.ppermute(value, axis, [(i, i ^ 1 << distance) for i in range(lax.axis_size(axis))])


def unit_rows(values):
    values = values.astype(jnp.float32)
    return values * lax.rsqrt(jnp.sum(values * values, axis=-1, keepdims=True) + EPS_UNIT)


def group_norm(values, row_total):
    first = lax.psum(jnp.sum(values, axis=0), "bn")
    center = first / row_total
    spread = lax.psum(jnp.sum(jnp.square(values - center), axis=0), "bn") / row_total
    return (values - center) * lax.rsqrt(spread + EPS_BN)


def moving_slots(shuffle_masks, level, half):
    flags = jnp.bitwise_and(jnp.right_shift(shuffle_masks, level), 1)
    return jnp.argsort(1 - flags, stable=True)[:half]


def on_device_moving(features, shuffle_masks, conv_in, conv_mid, conv_out, head, queries, queue, positive):
    dp_count = lax.axis_size("dp")
    bn_count = lax.axis_size("bn")
    bit_count = dp_count.bit_length() - 1
    crop_dev, positions, channels = features.shape
    half = crop_dev // 2
    middle = conv_in.shape[1]
    query_unit = unit_rows(queries).astype(jnp.bfloat16)
    query_all = lax.all_gather(query_unit, "dp", axis=0, tiled=True)
    shuffled = features
    for level in range(bit_count):
        moving = moving_slots(shuffle_masks, level, half)
        chosen = (moving[:, None] == jnp.arange(crop_dev)[None, :]).astype(jnp.bfloat16)
        leaving = jnp.dot(
            chosen, shuffled.reshape(crop_dev, positions * channels), preferred_element_type=jnp.float32
        ).astype(jnp.bfloat16)
        partner = partner_2(leaving.reshape(half, positions, channels), "dp", level)
        shuffled = shuffled.at[moving].set(partner)
    row_total = crop_dev * positions * bn_count
    flat_rows = shuffled.reshape(crop_dev * positions, channels)
    first_sum = jnp.dot(flat_rows, conv_in, preferred_element_type=jnp.float32)
    first_act = jax.nn.relu(group_norm(first_sum, row_total)).astype(jnp.bfloat16)
    tap_maps = first_act.reshape(crop_dev, positions, middle)
    padded = jnp.pad(tap_maps, ((0, 0), (1, 1), (0, 0)))
    stacked = jnp.concatenate([padded[:, tap : tap + positions, :] for tap in range(3)], axis=2)
    second_sum = jnp.dot(
        stacked.reshape(crop_dev * positions, 3 * middle),
        conv_mid.reshape(3 * middle, middle),
        preferred_element_type=jnp.float32,
    )
    second_act = jax.nn.relu(group_norm(second_sum, row_total)).astype(jnp.bfloat16)
    third_sum = jnp.dot(second_act, conv_out, preferred_element_type=jnp.float32)
    block = jax.nn.relu(group_norm(third_sum, row_total) + flat_rows.astype(jnp.float32)).astype(
        jnp.bfloat16
    )
    pooled = jnp.mean(
        block.reshape(crop_dev, positions, channels).astype(jnp.float32), axis=1
    ).astype(jnp.bfloat16)
    key_unit = unit_rows(jnp.dot(pooled, head, preferred_element_type=jnp.float32)).astype(
        jnp.bfloat16
    )
    for level in range(bit_count):
        moving = moving_slots(shuffle_masks, level, half)
        partner = partner_2(jnp.take(key_unit, moving, axis=0), "dp", level)
        key_unit = key_unit.at[moving].set(partner)
    queue_unit = unit_rows(queue).astype(jnp.bfloat16)
    scores = jnp.dot(query_all, queue_unit.T, preferred_element_type=jnp.float32) * INV_TEMP
    queue_part = jnp.sum(jnp.exp(scores - INV_TEMP), axis=1)
    key_all = lax.all_gather(key_unit, "dp", axis=0, tiled=True)
    slot_of = positive % crop_dev
    column = positive // crop_dev // bn_count
    picked = jnp.take(key_all, column * crop_dev + slot_of, axis=0)
    positive_logit = (
        jnp.sum(query_unit.astype(jnp.float32) * picked.astype(jnp.float32), axis=-1) * INV_TEMP
    )
    negative = lax.psum_scatter(queue_part, "dp", scatter_dimension=0, tiled=True)
    return jnp.log(jnp.exp(positive_logit - INV_TEMP) + negative) + INV_TEMP - positive_logit


MESH = pl.DeviceIdType.MESH
LANES = 128
QUEUE_STEPS = 8
PANELS = 4
PHASES = (
    "query", "queue", "key", "sum1", "bn1", "bn2", "bn3", "class", "far",
    "a0", "a1", "a2", "b0", "b1", "b2", "c0", "c1", "c2", "d0", "d1", "d2",
)
ORDERS = {"a": (2, 0, 1), "b": (2, 0, 1), "c": (0, 1, 2), "d": (0, 1, 2)}


def shuffled_kernel(
    n_dp, n_bn,
    masks_hbm, positive_hbm, queries_hbm, x_hbm, in_hbm, mid_hbm, out_hbm, head_hbm, queue_hbm,
    loss_ref,
    masks, positive, queries,
    x_ref, in_ref, mid_ref, out_ref, head_ref, queue_ref,
    h_ref, wide_ref, class_ref, mean_ref, scale_ref,
    dev_ref, class_send, class_recv, far_send, far_recv,
    a_send, a_pair, a_last, b_send, b_pair, b_last, c_send, c_pair, c_last, d_send, d_pair, d_last,
    feature_ref,
    sum_send, sum_recv, own1, all1, own2, all2, own3, all3,
    query_own, query_all, part_own, part_all, key_own, key_all,
    load_sem, panel_sem, send_sem, recv_sem,
):
    f32, bf16 = jnp.float32, jnp.bfloat16
    d = lax.axis_index("dp")
    b = lax.axis_index("bn")
    rows, channels = x_ref.shape
    slots = masks.shape[0]
    cells = rows // slots
    half = rows // 2
    middle = in_ref.shape[1]
    chunk = channels // len(ORDERS)
    total = float(rows * n_bn)

    panel = channels // PANELS
    panels = [
        pltpu.make_async_copy(
            in_hbm.at[pl.ds(i * panel, panel)], in_ref.at[pl.ds(i * panel, panel)], panel_sem.at[i]
        )
        for i in range(PANELS)
    ]
    loads = [
        pltpu.make_async_copy(src, dst, load_sem.at[i])
        for i, (src, dst) in enumerate(
            [(masks_hbm, masks), (positive_hbm, positive), (queries_hbm, queries), (x_hbm, x_ref), (queue_hbm, queue_ref), (mid_hbm, mid_ref), (out_hbm, out_ref), (head_hbm, head_ref)]
        )
    ]
    for load in loads[:4] + panels:
        load.start()

    barrier = pltpu.get_barrier_semaphore()
    dp_peers = [(d ^ k, b) for k in range(1, n_dp)]
    bn_peers = [(d, lax.rem(b + k, n_bn)) for k in range(1, n_bn)]
    for peer in dp_peers + bn_peers:
        pl.semaphore_signal(barrier, inc=1, device_id=peer, device_id_type=MESH)

    def push(phase, src, dst, peer):
        i = PHASES.index(phase)
        pltpu.make_async_remote_copy(
            src_ref=src, dst_ref=dst, send_sem=send_sem.at[i], recv_sem=recv_sem.at[i],
            device_id=peer, device_id_type=MESH,
        ).start()

    def arrived(phase, view):
        pltpu.make_async_copy(view, view, recv_sem.at[PHASES.index(phase)]).wait()

    def sent(phase, view):
        pltpu.make_async_copy(view, view, send_sem.at[PHASES.index(phase)]).wait()

    def most(ref):
        return ref.at[pl.ds(0, ref.shape[0] - 1)]

    def column_peers(phase, src, dst):
        for peer in dp_peers:
            push(phase, src, dst.at[d], peer)

    def exact(a, c):
        return jnp.dot(a, c, preferred_element_type=f32, precision=lax.Precision.HIGHEST)

    def dot(a, c):
        return jnp.dot(a, c, preferred_element_type=f32)

    for load in loads[:3]:
        load.wait()

    q = queries[...].astype(f32)
    query_unit = (q * lax.rsqrt(jnp.sum(q * q, axis=-1, keepdims=True) + EPS_UNIT)).astype(bf16)
    query_own[...] = query_unit
    query_all[d] = query_unit

    lane = lax.broadcasted_iota(jnp.int32, (slots, slots), 1)
    sub = lax.broadcasted_iota(jnp.int32, (slots, slots), 0)
    lane1 = lax.broadcasted_iota(jnp.int32, (1, slots), 1)
    lane_8 = lax.broadcasted_iota(jnp.int32, (8, LANES), 1)
    sub_8 = lax.broadcasted_iota(jnp.int32, (8, LANES), 0)
    slot_8 = lane_8 // cells
    mask_row = jnp.zeros((slots, slots), jnp.int32)
    mask_col = jnp.zeros((slots, slots), jnp.int32)
    want = jnp.zeros((1, slots), jnp.int32)
    mask_8 = jnp.zeros((8, LANES), jnp.int32)
    sources = []
    for s in range(slots):
        mask = masks[s]
        sources.append(mask ^ d)
        mask_row = jnp.where(lane == s, sources[s], mask_row)
        mask_col = jnp.where(sub == s, sources[s], mask_col)
        mask_8 = jnp.where(slot_8 == s, mask, mask_8)
        place = positive[s]
        slot = lax.rem(place, slots)
        column = lax.div(place, slots * n_bn) ^ masks[slot]
        want = jnp.where(lane1 == s, column * slots + slot, want)
    same = (mask_row == mask_col).astype(f32)
    local_mean = same / (jnp.sum(same, axis=0, keepdims=True) * float(cells))
    member = (mask_row[:n_dp] == sub[:n_dp]).astype(f32)
    counts = []
    for e in range(n_dp):
        count = jnp.int32(0)
        for s in range(slots):
            count = count + (sources[s] == e).astype(jnp.int32)
        counts.append((count * cells).astype(f32))

    bits = [(mask_8 & (1 << level)) != 0 for level in range(3)]
    kind = mask_8 & 3
    flags = jnp.where(sub_8 == 0, mask_8 & 1, jnp.where(sub_8 == 1, (mask_8 >> 1) & 1, (mask_8 >> 2) & 1))
    flags = jnp.where(sub_8 >= 3, (kind == sub_8 - 2).astype(jnp.int32), flags)
    before_r = lax.broadcasted_iota(jnp.int32, (rows, rows), 0)
    before_c = lax.broadcasted_iota(jnp.int32, (rows, rows), 1)
    earlier = jnp.logical_and(before_r % cells == 0, before_r // cells < before_c // cells)
    rank = dot(flags.astype(f32).astype(bf16), jnp.where(earlier, 1.0, 0.0).astype(bf16))
    places = jnp.where(flags != 0, rank * float(cells) + (lane_8 % cells + 1).astype(f32), 0.0)

    def every(i):
        return jnp.broadcast_to(places[i : i + 1], (8, LANES))

    to_level = [every(i) for i in range(3)]
    tag = (lane_8 + 1).astype(f32)

    def picks(count, codes):
        wanted = (lax.broadcasted_iota(jnp.int32, (count, codes.shape[1]), 0) + 1).astype(f32)
        return jnp.where(wanted == codes, 1.0, 0.0).astype(bf16)

    gather = [picks(half, places[i : i + 1]) for i in range(6)]

    def moved(table, which):
        stacked = jnp.zeros((8, LANES), f32)
        for i, line in enumerate(table):
            stacked = jnp.where(sub_8 == i, line, stacked)
        return lax.dot_general(
            stacked.astype(bf16), which, (((1,), (1,)), ((), ())), preferred_element_type=f32
        )

    low_lane = lax.broadcasted_iota(jnp.int32, (1, LANES), 1) < half

    def unless(flag, line):
        return jnp.where(flag, 0.0, line)

    by_order = {}
    for i, j, k in sorted(set(ORDERS.values())):
        table = [
            to_level[j], unless(bits[j], to_level[k]), to_level[k],
            unless(jnp.logical_or(bits[j], bits[k]), tag), unless(bits[k], tag),
        ]
        pair = moved(table, jnp.concatenate([gather[i], gather[j]], axis=0))
        second = jnp.concatenate([unless(bits[i], to_level[j])[:1], pair[0:1]], axis=1)
        third = jnp.concatenate(
            [
                unless(jnp.logical_or(bits[i], bits[j]), to_level[k])[:1],
                jnp.where(low_lane, pair[1:2], pair[2:3]),
            ],
            axis=1,
        )
        final = jnp.concatenate(
            [unless(mask_8 != 0, tag)[:1], jnp.where(low_lane, pair[3:4], pair[4:5])], axis=1
        )
        last = moved([tag], gather[k])[:1]
        by_order[i, j, k] = (gather[i], picks(half, second)[:, : rows + half], picks(half, third), picks(rows, final), picks(rows, last))
    table = [to_level[2], unless(bits[2], tag)]
    near = moved(table, jnp.concatenate(gather[3:5], axis=0))
    both = moved(table, gather[5])
    far_codes = jnp.concatenate([unless(kind != 0, to_level[2])[:1], near[0:1]], axis=1)
    stay_codes = jnp.concatenate([unless(mask_8 != 0, tag)[:1], near[1:2]], axis=1)
    far_pick = (picks(half, far_codes), picks(half, both[0:1]))
    stay_pick = (picks(rows, stay_codes), picks(rows, both[1:2]))
    routes = {name: by_order[order] for name, order in ORDERS.items()}
    last_pick = routes["c"][4]

    sends = {"a": a_send, "b": b_send, "c": c_send, "d": d_send}
    pairs = {"a": a_pair, "b": b_pair, "c": c_pair, "d": d_pair}
    lasts = {"a": a_last, "b": b_last, "c": c_last, "d": d_last}
    columns = {name: slice(i * chunk, (i + 1) * chunk) for i, name in enumerate(ORDERS)}

    def stage(name, step):
        held = x_ref[:, columns[name]]
        if step:
            held = jnp.concatenate([held, pairs[name][: step * half]], axis=0)
        sends[name][step] = dot(routes[name][step], held).astype(bf16)

    def landing(name, step):
        return lasts[name] if step == 2 else pairs[name].at[pl.ds(step * half, half)]

    def ship(name, step):
        peer = (d ^ (1 << ORDERS[name][step]), b)
        push(name + str(step), sends[name].at[step], landing(name, step), peer)

    def forward(name, step):
        arrived(name + str(step - 1), landing(name, step - 1))
        stage(name, step)
        ship(name, step)

    def settle(name):
        arrived(name + "2", lasts[name])
        held = jnp.concatenate([x_ref[:, columns[name]], pairs[name][...]], axis=0)
        feature_ref[:, columns[name]] = dot(routes[name][3], held) + dot(routes[name][4], lasts[name][...])

    def to_rows(ref, at, values):
        for r in range(values.shape[1] // LANES):
            ref[at + r : at + r + 1, :] = values[:, r * LANES : (r + 1) * LANES]

    def to_line(ref, at, values):
        for r in range(values.shape[0]):
            ref[at : at + 1, r * LANES : (r + 1) * LANES] = values[r : r + 1]

    def group_peers(phase, own, every_part):
        every_part[b] = own[...]
        for peer in bn_peers:
            push(phase, own, every_part.at[b], peer)

    def group_stats(phase, every_part):
        arrived(phase, most(every_part))
        lines = every_part.shape[1] // 2
        parts = every_part[...]
        means = parts[:, :lines]
        mean = jnp.sum(means, axis=0) * (1.0 / n_bn)
        spread = jnp.sum(parts[:, lines:], axis=0) + float(rows) * jnp.sum(
            jnp.square(means - mean[None]), axis=0
        )
        return mean, lax.rsqrt(spread * (1.0 / total) + EPS_BN)

    def send_stats(phase, h, own, every_part):
        mean = jnp.sum(h, axis=0, keepdims=True) * (1.0 / rows)
        squares = jnp.sum(jnp.square(h - mean), axis=0, keepdims=True)
        to_rows(own, 0, mean)
        to_rows(own, own.shape[0] // 2, squares)
        group_peers(phase, own, every_part)

    ones = jnp.ones((LANES, LANES), bf16)
    step_rows = queue_ref.shape[0] // QUEUE_STEPS

    def queue_step(c, total_part):
        raw = queue_ref[pl.ds(c * step_rows, step_rows), :].astype(f32)
        square = raw * raw
        high = square.astype(bf16)
        low = (square - high.astype(f32)).astype(bf16)
        norm = dot(high, ones) + dot(low, ones)
        unit = (raw * lax.rsqrt(norm + EPS_UNIT)).astype(bf16)
        flat_queries = query_all[...].reshape(n_dp * slots, query_all.shape[2])
        scores = lax.dot_general(unit, flat_queries, (((1,), (1,)), ((), ())), preferred_element_type=f32)
        terms = jnp.exp(scores * INV_TEMP - INV_TEMP)
        return total_part + jnp.sum(terms.reshape(step_rows // 8, 8, n_dp * slots), axis=0)

    def queue_steps(first, last, total_part):
        return lax.fori_loop(first, last, queue_step, total_part)

    loads[3].wait()
    for name in ORDERS:
        stage(name, 0)
    first = None
    for i in range(PANELS):
        panels[i].wait()
        at = slice(i * panel, (i + 1) * panel)
        term = dot(x_ref[:, at], in_ref[at])
        first = term if first is None else first + term
        if i == 0:
            for load in loads[4:]:
                load.start()
    shaped = first.reshape(slots, cells, middle)
    sums = jnp.sum(shaped, axis=1)
    center = exact(local_mean, sums)
    offset = shaped - center[:, None, :]
    squares = jnp.sum(jnp.square(offset), axis=1)
    dev_ref[...] = offset.reshape(rows, middle).astype(bf16)
    for c in range(3):
        class_send[c * half : (c + 1) * half] = dot(gather[3 + c], dev_ref[...]).astype(bf16)
    lines = middle // LANES
    for at, values in ((0, exact(member, sums)), (lines, exact(member, squares))):
        for g in range(n_dp):
            for r in range(lines):
                sum_send[g, at + r : at + r + 1, :] = values[g : g + 1, r * LANES : (r + 1) * LANES]
    sum_recv[d] = sum_send[d]

    pl.semaphore_wait(barrier, n_dp + n_bn - 2)
    for c in range(3):
        at = pl.ds(c * half, half)
        push("class", class_send.at[at], class_recv.at[at], (d ^ (c + 1), b))
    for k in range(1, n_dp):
        push("sum1", sum_send.at[d ^ k], sum_recv.at[d], (d ^ k, b))
    for name in "acbd":
        ship(name, 0)
    column_peers("query", query_own, query_all)

    part = jnp.zeros((8, n_dp * slots), f32)
    loads[4].wait()

    arrived("sum1", most(sum_recv))
    parts = sum_recv[...]
    class_sums = parts[:, :lines]
    column_mean = jnp.sum(class_sums, axis=0) * (1.0 / rows)
    column_squares = jnp.sum(parts[:, lines:], axis=0)
    class_means = []
    for e in range(n_dp):
        class_means.append(class_sums[e] / jnp.maximum(counts[e], 1.0))
        column_squares = column_squares + counts[e] * jnp.square(class_means[e] - column_mean)
    own1[:lines] = column_mean
    own1[lines:] = column_squares
    group_peers("bn1", own1, all1)

    arrived("class", class_recv)
    near_held = jnp.concatenate([dev_ref[...], class_recv[:rows]], axis=0)
    far_send[...] = (dot(far_pick[0], near_held) + dot(far_pick[1], class_recv[rows:])).astype(bf16)
    push("far", far_send, far_recv, (d ^ 4, b))

    h_ref[...] = dot(stay_pick[0], near_held) + dot(stay_pick[1], class_recv[rows:])
    arrived("query", most(query_all))
    forward("c", 1)
    forward("a", 1)
    part = queue_steps(0, 1, part)
    forward("d", 1)
    forward("b", 1)

    mean, scale = group_stats("bn1", all1)
    for e in range(n_dp):
        to_line(class_ref, e, class_means[e] - mean)
    to_line(scale_ref, 0, scale)
    loads[5].wait()

    arrived("far", far_recv)
    h_ref[...] = h_ref[...] + dot(last_pick, far_recv[...])
    for s in range(slots):
        at = slice(s * cells, (s + 1) * cells)
        move = jnp.broadcast_to(class_ref[pl.ds(sources[s], 1), :], (cells, middle))
        h_ref[at] = jax.nn.relu((h_ref[at] + move) * scale_ref[0:1, :middle])
    act = h_ref[...]
    cell = lax.broadcasted_iota(jnp.int32, act.shape, 0) % cells
    before = jnp.where(cell == 0, 0.0, pltpu.roll(act, 1, 0)).astype(bf16)
    after = jnp.where(cell == cells - 1, 0.0, pltpu.roll(act, rows - 1, 0)).astype(bf16)
    h_ref[...] = dot(before, mid_ref[0]) + dot(act.astype(bf16), mid_ref[1]) + dot(after, mid_ref[2])
    send_stats("bn2", h_ref[...], own2, all2)
    forward("c", 2)
    forward("a", 2)
    part = queue_steps(1, 3, part)
    forward("d", 2)
    forward("b", 2)
    loads[6].wait()
    mean, scale = group_stats("bn2", all2)
    to_line(mean_ref, 0, mean)
    to_line(scale_ref, 0, scale)

    second = jax.nn.relu((h_ref[...] - mean_ref[0:1, :middle]) * scale_ref[0:1, :middle]).astype(bf16)
    wide_ref[...] = dot(second, out_ref[...])
    send_stats("bn3", wide_ref[...], own3, all3)
    part = queue_steps(3, 8, part)
    part_own[...] = jnp.sum(part, axis=0, keepdims=True)
    part_all[d] = part_own[...]
    column_peers("queue", part_own, part_all)
    loads[7].wait()
    for name in "acbd":
        settle(name)
    mean, scale = group_stats("bn3", all3)
    to_line(mean_ref, 0, mean)
    to_line(scale_ref, 0, scale)

    z = None
    for at in columns.values():
        normal = (wide_ref[:, at] - mean_ref[0:1, at]) * scale_ref[0:1, at]
        block = jax.nn.relu(normal + feature_ref[:, at]).astype(bf16)
        pooled = jnp.mean(block.astype(f32).reshape(slots, cells, chunk), axis=1).astype(bf16)
        term = dot(pooled, head_ref[at])
        z = term if z is None else z + term
    key_own[...] = (z * lax.rsqrt(jnp.sum(z * z, axis=-1, keepdims=True) + EPS_UNIT)).astype(bf16)
    key_all[d] = key_own[...]
    column_peers("key", key_own, key_all)

    arrived("queue", most(part_all))
    negative_all = jnp.sum(part_all[...], axis=0)
    mine = lax.broadcasted_iota(jnp.int32, (slots, n_dp * slots), 1) == (
        lax.broadcasted_iota(jnp.int32, (slots, n_dp * slots), 0) + d * slots
    )
    negative_col = jnp.sum(jnp.where(mine, negative_all, 0.0), axis=1, keepdims=True)
    negative = jnp.sum(jnp.where(lane == sub, negative_col, 0.0), axis=0, keepdims=True)

    arrived("key", most(key_all))
    keys = key_all[...].reshape(n_dp * slots, key_all.shape[2])
    products = lax.dot_general(keys, query_own[...], (((1,), (1,)), ((), ())), preferred_element_type=f32)
    chosen = lax.broadcasted_iota(jnp.int32, products.shape, 0) == want
    logit = jnp.sum(jnp.where(chosen, products, 0.0), axis=0, keepdims=True) * INV_TEMP
    loss_ref[...] = jnp.log(jnp.exp(logit - INV_TEMP) + negative) + INV_TEMP - logit

    for phase, every_part in (("query", query_all), ("queue", part_all), ("key", key_all), ("sum1", sum_recv), ("bn1", all1), ("bn2", all2), ("bn3", all3)):
        sent(phase, most(every_part))
    sent("class", class_send)
    sent("far", far_send)
    for name in ORDERS:
        for step in range(3):
            sent(name + str(step), sends[name].at[step])


def on_device_shuffled(n_dp, n_bn, features, shuffle_masks, conv_in, conv_mid, conv_out, head, queries, queue, positive):
    f32, bf16 = jnp.float32, jnp.bfloat16
    slots, cells, channels = features.shape
    rows = slots * cells
    middle = conv_in.shape[1]
    width = queries.shape[1]

    def group_parts(c):
        tile = (2 * (c // LANES), LANES)
        return [pltpu.VMEM(tile, f32), pltpu.VMEM((n_bn,) + tile, f32)]

    chunk = channels // len(ORDERS)
    feature_parts = [
        pltpu.VMEM((3, rows // 2, chunk), bf16),
        pltpu.VMEM((rows, chunk), bf16),
        pltpu.VMEM((rows // 2, chunk), bf16),
    ]
    sums = pltpu.VMEM((n_dp, 2 * (middle // LANES), LANES), f32)
    hbm = pl.BlockSpec(memory_space=pltpu.HBM)
    loss = pl.pallas_call(
        functools.partial(shuffled_kernel, n_dp, n_bn),
        out_shape=jax.ShapeDtypeStruct((1, slots), f32),
        in_specs=[hbm] * 9,
        out_specs=pl.BlockSpec(memory_space=pltpu.VMEM),
        scratch_shapes=[
            pltpu.SMEM(shuffle_masks.shape, jnp.int32),
            pltpu.SMEM(positive.shape, jnp.int32),
            pltpu.VMEM(queries.shape, bf16),
            pltpu.VMEM((rows, channels), bf16),
            pltpu.VMEM(conv_in.shape, bf16),
            pltpu.VMEM(conv_mid.shape, bf16),
            pltpu.VMEM(conv_out.shape, bf16),
            pltpu.VMEM(head.shape, bf16),
            pltpu.VMEM(queue.shape, bf16),
            pltpu.VMEM((rows, middle), f32),
            pltpu.VMEM((rows, channels), f32),
            pltpu.VMEM((n_dp, middle), f32),
            pltpu.VMEM((8, channels), f32),
            pltpu.VMEM((8, channels), f32),
            pltpu.VMEM((rows, middle), bf16),
            pltpu.VMEM((3 * rows // 2, middle), bf16),
            pltpu.VMEM((3 * rows // 2, middle), bf16),
            pltpu.VMEM((rows // 2, middle), bf16),
            pltpu.VMEM((rows // 2, middle), bf16),
        ]
        + feature_parts * len(ORDERS)
        + [pltpu.VMEM((rows, channels), f32), sums, sums]
        + group_parts(middle)
        + group_parts(middle)
        + group_parts(channels)
        + [
            pltpu.VMEM((slots, width), bf16),
            pltpu.VMEM((n_dp, slots, width), bf16),
            pltpu.VMEM((1, n_dp * slots), f32),
            pltpu.VMEM((n_dp, 1, n_dp * slots), f32),
            pltpu.VMEM((slots, width), bf16),
            pltpu.VMEM((n_dp, slots, width), bf16),
            pltpu.SemaphoreType.DMA((8,)),
            pltpu.SemaphoreType.DMA((PANELS,)),
            pltpu.SemaphoreType.DMA((len(PHASES),)),
            pltpu.SemaphoreType.DMA((len(PHASES),)),
        ],
        compiler_params=pltpu.CompilerParams(
            collective_id=0, has_side_effects=True, vmem_limit_bytes=64 << 20
        ),
        name="shuffled_crops",
    )(shuffle_masks, positive, queries, features.reshape(rows, channels), conv_in, conv_mid, conv_out, head, queue)
    return loss.reshape(slots)


def on_device(n_dp, n_bn, *arrays):
    features, conv_in = arrays[0], arrays[2]
    slots, cells, channels = features.shape
    whole_lanes = conv_in.shape[1] % (2 * LANES) == 0 and channels % (4 * LANES) == 0
    if whole_lanes and n_dp == 8 and slots * cells == LANES and cells == 8 and n_bn <= 4:
        return on_device_shuffled(n_dp, n_bn, *arrays)
    return on_device_moving(*arrays)


def solution(mesh):
    return jax.shard_map(
        functools.partial(on_device, mesh.shape["dp"], mesh.shape["bn"]),
        mesh=mesh,
        in_specs=(
            P(("dp", "bn"), None, None),
            P(),
            P(),
            P(),
            P(),
            P(),
            P(("dp", "bn"), None),
            P("dp", None),
            P(("dp", "bn")),
        ),
        out_specs=P(("dp", "bn")),
        check_vma=False,
    )
```

```python
import functools

import jax
import jax.numpy as jnp
from jax import lax
from jax.experimental import pallas as pl
from jax.experimental.pallas import tpu as pltpu
from jax.sharding import PartitionSpec as P

EPS_BN = 1e-05
EPS_UNIT = 1e-06
INV_TEMP = 1.0 / 0.07


def partner_2(value, axis, distance):
    return lax.ppermute(value, axis, [(i, i ^ 1 << distance) for i in range(lax.axis_size(axis))])


def unit_rows(values):
    values = values.astype(jnp.float32)
    return values * lax.rsqrt(jnp.sum(values * values, axis=-1, keepdims=True) + EPS_UNIT)


def group_norm(values, row_total):
    first = lax.psum(jnp.sum(values, axis=0), "bn")
    center = first / row_total
    spread = lax.psum(jnp.sum(jnp.square(values - center), axis=0), "bn") / row_total
    return (values - center) * lax.rsqrt(spread + EPS_BN)


def moving_slots(shuffle_masks, level, half):
    flags = jnp.bitwise_and(jnp.right_shift(shuffle_masks, level), 1)
    return jnp.argsort(1 - flags, stable=True)[:half]


def on_device_moving(features, shuffle_masks, conv_in, conv_mid, conv_out, head, queries, queue, positive):
    dp_count = lax.axis_size("dp")
    bn_count = lax.axis_size("bn")
    bit_count = dp_count.bit_length() - 1
    crop_dev, positions, channels = features.shape
    half = crop_dev // 2
    middle = conv_in.shape[1]
    query_unit = unit_rows(queries).astype(jnp.bfloat16)
    query_all = lax.all_gather(query_unit, "dp", axis=0, tiled=True)
    shuffled = features
    for level in range(bit_count):
        moving = moving_slots(shuffle_masks, level, half)
        chosen = (moving[:, None] == jnp.arange(crop_dev)[None, :]).astype(jnp.bfloat16)
        leaving = jnp.dot(
            chosen, shuffled.reshape(crop_dev, positions * channels), preferred_element_type=jnp.float32
        ).astype(jnp.bfloat16)
        partner = partner_2(leaving.reshape(half, positions, channels), "dp", level)
        shuffled = shuffled.at[moving].set(partner)
    row_total = crop_dev * positions * bn_count
    flat_rows = shuffled.reshape(crop_dev * positions, channels)
    first_sum = jnp.dot(flat_rows, conv_in, preferred_element_type=jnp.float32)
    first_act = jax.nn.relu(group_norm(first_sum, row_total)).astype(jnp.bfloat16)
    tap_maps = first_act.reshape(crop_dev, positions, middle)
    padded = jnp.pad(tap_maps, ((0, 0), (1, 1), (0, 0)))
    stacked = jnp.concatenate([padded[:, tap : tap + positions, :] for tap in range(3)], axis=2)
    second_sum = jnp.dot(
        stacked.reshape(crop_dev * positions, 3 * middle),
        conv_mid.reshape(3 * middle, middle),
        preferred_element_type=jnp.float32,
    )
    second_act = jax.nn.relu(group_norm(second_sum, row_total)).astype(jnp.bfloat16)
    third_sum = jnp.dot(second_act, conv_out, preferred_element_type=jnp.float32)
    block = jax.nn.relu(group_norm(third_sum, row_total) + flat_rows.astype(jnp.float32)).astype(
        jnp.bfloat16
    )
    pooled = jnp.mean(
        block.reshape(crop_dev, positions, channels).astype(jnp.float32), axis=1
    ).astype(jnp.bfloat16)
    key_unit = unit_rows(jnp.dot(pooled, head, preferred_element_type=jnp.float32)).astype(
        jnp.bfloat16
    )
    for level in range(bit_count):
        moving = moving_slots(shuffle_masks, level, half)
        partner = partner_2(jnp.take(key_unit, moving, axis=0), "dp", level)
        key_unit = key_unit.at[moving].set(partner)
    queue_unit = unit_rows(queue).astype(jnp.bfloat16)
    scores = jnp.dot(query_all, queue_unit.T, preferred_element_type=jnp.float32) * INV_TEMP
    queue_part = jnp.sum(jnp.exp(scores - INV_TEMP), axis=1)
    key_all = lax.all_gather(key_unit, "dp", axis=0, tiled=True)
    slot_of = positive % crop_dev
    column = positive // crop_dev // bn_count
    picked = jnp.take(key_all, column * crop_dev + slot_of, axis=0)
    positive_logit = (
        jnp.sum(query_unit.astype(jnp.float32) * picked.astype(jnp.float32), axis=-1) * INV_TEMP
    )
    negative = lax.psum_scatter(queue_part, "dp", scatter_dimension=0, tiled=True)
    return jnp.log(jnp.exp(positive_logit - INV_TEMP) + negative) + INV_TEMP - positive_logit


MESH = pl.DeviceIdType.MESH
LANES = 128
QUEUE_STEPS = 8
PANELS = 4
PHASES = (
    "query", "queue", "key", "sum1", "bn1", "bn2", "bn3", "class", "far",
    "a0", "a1", "a2", "b0", "b1", "b2", "c0", "c1", "c2", "d0", "d1", "d2",
)
ORDERS = {'a': (2, 0, 1), 'b': (2, 0, 1), 'c': (0, 1, 2), 'd': (0, 1, 2)}


def shuffled_kernel(
    n_dp, n_bn,
    masks_hbm, positive_hbm, queries_hbm, x_hbm, in_hbm, mid_hbm, out_hbm, head_hbm, queue_hbm,
    loss_ref,
    masks, positive, queries,
    x_ref, in_ref, mid_ref, out_ref, head_ref, queue_ref,
    h_ref, wide_ref, class_ref, mean_ref, scale_ref,
    dev_ref, class_send, class_recv, far_send, far_recv,
    a_send, a_pair, a_last, b_send, b_pair, b_last, c_send, c_pair, c_last, d_send, d_pair, d_last,
    feature_ref,
    sum_send, sum_recv, own1, all1, own2, all2, own3, all3,
    query_own, query_all, part_own, part_all, key_own, key_all,
    load_sem, panel_sem, send_sem, recv_sem,
):
    f32, bf16 = jnp.float32, jnp.bfloat16
    d = lax.axis_index("dp")
    b = lax.axis_index("bn")
    rows, channels = x_ref.shape
    slots = masks.shape[0]
    cells = rows // slots
    half = rows // 2
    middle = in_ref.shape[1]
    chunk = channels // len(ORDERS)
    total = float(rows * n_bn)

    panel = channels // PANELS
    panels = [
        pltpu.make_async_copy(
            in_hbm.at[pl.ds(i * panel, panel)], in_ref.at[pl.ds(i * panel, panel)], panel_sem.at[i]
        )
        for i in range(PANELS)
    ]
    loads = [
        pltpu.make_async_copy(src, dst, load_sem.at[i])
        for i, (src, dst) in enumerate(
            [(masks_hbm, masks), (positive_hbm, positive), (queries_hbm, queries), (x_hbm, x_ref), (queue_hbm, queue_ref), (mid_hbm, mid_ref), (out_hbm, out_ref), (head_hbm, head_ref)]
        )
    ]
    for load in loads[:4] + panels:
        load.start()

    barrier = pltpu.get_barrier_semaphore()
    dp_peers = [(d ^ k, b) for k in range(1, n_dp)]
    bn_peers = [(d, lax.rem(b + k, n_bn)) for k in range(1, n_bn)]
    for peer in dp_peers + bn_peers:
        pl.semaphore_signal(barrier, inc=1, device_id=peer, device_id_type=MESH)

    def push(phase, src, dst, peer):
        i = PHASES.index(phase)
        pltpu.make_async_remote_copy(
            src_ref=src, dst_ref=dst, send_sem=send_sem.at[i], recv_sem=recv_sem.at[i],
            device_id=peer, device_id_type=MESH,
        ).start()

    def arrived(phase, view):
        pltpu.make_async_copy(view, view, recv_sem.at[PHASES.index(phase)]).wait()

    def sent(phase, view):
        pltpu.make_async_copy(view, view, send_sem.at[PHASES.index(phase)]).wait()

    def most(ref):
        return ref.at[pl.ds(0, ref.shape[0] - 1)]

    def column_peers(phase, src, dst):
        for peer in dp_peers:
            push(phase, src, dst.at[d], peer)

    def exact(a, c):
        return jnp.dot(a, c, preferred_element_type=f32, precision=lax.Precision.HIGHEST)

    def dot(a, c):
        return jnp.dot(a, c, preferred_element_type=f32)

    for load in loads[:3]:
        load.wait()

    q = queries[...].astype(f32)
    query_unit = (q * lax.rsqrt(jnp.sum(q * q, axis=-1, keepdims=True) + EPS_UNIT)).astype(bf16)
    query_own[...] = query_unit
    query_all[d] = query_unit

    lane = lax.broadcasted_iota(jnp.int32, (slots, slots), 1)
    sub = lax.broadcasted_iota(jnp.int32, (slots, slots), 0)
    lane1 = lax.broadcasted_iota(jnp.int32, (1, slots), 1)
    lane_8 = lax.broadcasted_iota(jnp.int32, (8, LANES), 1)
    sub_8 = lax.broadcasted_iota(jnp.int32, (8, LANES), 0)
    slot_8 = lane_8 // cells
    mask_row = jnp.zeros((slots, slots), jnp.int32)
    mask_col = jnp.zeros((slots, slots), jnp.int32)
    want = jnp.zeros((1, slots), jnp.int32)
    mask_8 = jnp.zeros((8, LANES), jnp.int32)
    sources = []
    for s in range(slots):
        mask = masks[s]
        sources.append(mask ^ d)
        mask_row = jnp.where(lane == s, sources[s], mask_row)
        mask_col = jnp.where(sub == s, sources[s], mask_col)
        mask_8 = jnp.where(slot_8 == s, mask, mask_8)
        place = positive[s]
        slot = lax.rem(place, slots)
        column = lax.div(place, slots * n_bn) ^ masks[slot]
        want = jnp.where(lane1 == s, column * slots + slot, want)
    same = (mask_row == mask_col).astype(f32)
    local_mean = same / (jnp.sum(same, axis=0, keepdims=True) * float(cells))
    member = (mask_row[:n_dp] == sub[:n_dp]).astype(f32)
    counts = []
    for e in range(n_dp):
        count = jnp.int32(0)
        for s in range(slots):
            count = count + (sources[s] == e).astype(jnp.int32)
        counts.append((count * cells).astype(f32))

    bits = [(mask_8 & (1 << level)) != 0 for level in range(3)]
    kind = mask_8 & 3
    flags = jnp.where(sub_8 == 0, mask_8 & 1, jnp.where(sub_8 == 1, (mask_8 >> 1) & 1, (mask_8 >> 2) & 1))
    flags = jnp.where(sub_8 >= 3, (kind == sub_8 - 2).astype(jnp.int32), flags)
    before_r = lax.broadcasted_iota(jnp.int32, (rows, rows), 0)
    before_c = lax.broadcasted_iota(jnp.int32, (rows, rows), 1)
    earlier = jnp.logical_and(before_r % cells == 0, before_r // cells < before_c // cells)
    rank = dot(flags.astype(f32).astype(bf16), jnp.where(earlier, 1.0, 0.0).astype(bf16))
    places = jnp.where(flags != 0, rank * float(cells) + (lane_8 % cells + 1).astype(f32), 0.0)

    def every(i):
        return jnp.broadcast_to(places[i : i + 1], (8, LANES))

    to_level = [every(i) for i in range(3)]
    tag = (lane_8 + 1).astype(f32)

    def picks(count, codes):
        wanted = (lax.broadcasted_iota(jnp.int32, (count, codes.shape[1]), 0) + 1).astype(f32)
        return jnp.where(wanted == codes, 1.0, 0.0).astype(bf16)

    gather = [picks(half, places[i : i + 1]) for i in range(6)]

    def moved(table, which):
        stacked = jnp.zeros((8, LANES), f32)
        for i, line in enumerate(table):
            stacked = jnp.where(sub_8 == i, line, stacked)
        return lax.dot_general(
            stacked.astype(bf16), which, (((1,), (1,)), ((), ())), preferred_element_type=f32
        )

    low_lane = lax.broadcasted_iota(jnp.int32, (1, LANES), 1) < half

    def unless(flag, line):
        return jnp.where(flag, 0.0, line)

    by_order = {}
    for i, j, k in sorted(set(ORDERS.values())):
        table = [
            to_level[j], unless(bits[j], to_level[k]), to_level[k],
            unless(jnp.logical_or(bits[j], bits[k]), tag), unless(bits[k], tag),
        ]
        pair = moved(table, jnp.concatenate([gather[i], gather[j]], axis=0))
        second = jnp.concatenate([unless(bits[i], to_level[j])[:1], pair[0:1]], axis=1)
        third = jnp.concatenate(
            [
                unless(jnp.logical_or(bits[i], bits[j]), to_level[k])[:1],
                jnp.where(low_lane, pair[1:2], pair[2:3]),
            ],
            axis=1,
        )
        final = jnp.concatenate(
            [unless(mask_8 != 0, tag)[:1], jnp.where(low_lane, pair[3:4], pair[4:5])], axis=1
        )
        last = moved([tag], gather[k])[:1]
        by_order[i, j, k] = (gather[i], picks(half, second)[:, : rows + half], picks(half, third), picks(rows, final), picks(rows, last))
    table = [to_level[2], unless(bits[2], tag)]
    near = moved(table, jnp.concatenate(gather[3:5], axis=0))
    both = moved(table, gather[5])
    far_codes = jnp.concatenate([unless(kind != 0, to_level[2])[:1], near[0:1]], axis=1)
    stay_codes = jnp.concatenate([unless(mask_8 != 0, tag)[:1], near[1:2]], axis=1)
    far_pick = (picks(half, far_codes), picks(half, both[0:1]))
    stay_pick = (picks(rows, stay_codes), picks(rows, both[1:2]))
    routes = {name: by_order[order] for name, order in ORDERS.items()}
    last_pick = picks(rows, moved([tag], gather[2])[:1])

    sends = {"a": a_send, "b": b_send, "c": c_send, "d": d_send}
    pairs = {"a": a_pair, "b": b_pair, "c": c_pair, "d": d_pair}
    lasts = {"a": a_last, "b": b_last, "c": c_last, "d": d_last}
    columns = {name: slice(i * chunk, (i + 1) * chunk) for i, name in enumerate(ORDERS)}

    def stage(name, step):
        held = x_ref[:, columns[name]]
        if step:
            held = jnp.concatenate([held, pairs[name][: step * half]], axis=0)
        sends[name][step] = dot(routes[name][step], held).astype(bf16)

    def landing(name, step):
        return lasts[name] if step == 2 else pairs[name].at[pl.ds(step * half, half)]

    def ship(name, step):
        peer = (d ^ (1 << ORDERS[name][step]), b)
        push(name + str(step), sends[name].at[step], landing(name, step), peer)

    def forward(name, step):
        arrived(name + str(step - 1), landing(name, step - 1))
        stage(name, step)
        ship(name, step)

    def settle(name):
        held = jnp.concatenate([x_ref[:, columns[name]], pairs[name][...]], axis=0)
        feature_ref[:, columns[name]] = dot(routes[name][3], held)

    def to_rows(ref, at, values):
        for r in range(values.shape[1] // LANES):
            ref[at + r : at + r + 1, :] = values[:, r * LANES : (r + 1) * LANES]

    def to_line(ref, at, values):
        for r in range(values.shape[0]):
            ref[at : at + 1, r * LANES : (r + 1) * LANES] = values[r : r + 1]

    def group_peers(phase, own, every_part):
        every_part[b] = own[...]
        for peer in bn_peers:
            push(phase, own, every_part.at[b], peer)

    def group_stats(phase, every_part):
        arrived(phase, most(every_part))
        lines = every_part.shape[1] // 2
        parts = every_part[...]
        means = parts[:, :lines]
        mean = jnp.sum(means, axis=0) * (1.0 / n_bn)
        spread = jnp.sum(parts[:, lines:], axis=0) + float(rows) * jnp.sum(
            jnp.square(means - mean[None]), axis=0
        )
        return mean, lax.rsqrt(spread * (1.0 / total) + EPS_BN)

    def send_stats(phase, h, own, every_part):
        mean = jnp.sum(h, axis=0, keepdims=True) * (1.0 / rows)
        squares = jnp.sum(jnp.square(h - mean), axis=0, keepdims=True)
        to_rows(own, 0, mean)
        to_rows(own, own.shape[0] // 2, squares)
        group_peers(phase, own, every_part)

    ones = jnp.ones((LANES, LANES), bf16)
    step_rows = queue_ref.shape[0] // QUEUE_STEPS

    def queue_step(c, total_part):
        raw = queue_ref[pl.ds(c * step_rows, step_rows), :].astype(f32)
        square = raw * raw
        high = square.astype(bf16)
        low = (square - high.astype(f32)).astype(bf16)
        norm = dot(high, ones) + dot(low, ones)
        unit = (raw * lax.rsqrt(norm + EPS_UNIT)).astype(bf16)
        flat_queries = query_all[...].reshape(n_dp * slots, query_all.shape[2])
        scores = lax.dot_general(unit, flat_queries, (((1,), (1,)), ((), ())), preferred_element_type=f32)
        terms = jnp.exp(scores * INV_TEMP - INV_TEMP)
        return total_part + jnp.sum(terms.reshape(step_rows // 8, 8, n_dp * slots), axis=0)

    def queue_steps(first, last, total_part):
        return lax.fori_loop(first, last, queue_step, total_part)

    loads[3].wait()
    for name in ORDERS:
        stage(name, 0)
    first = None
    for i in range(PANELS):
        panels[i].wait()
        at = slice(i * panel, (i + 1) * panel)
        term = dot(x_ref[:, at], in_ref[at])
        first = term if first is None else first + term
        if i == 0:
            for load in loads[4:]:
                load.start()
    shaped = first.reshape(slots, cells, middle)
    sums = jnp.sum(shaped, axis=1)
    center = exact(local_mean, sums)
    offset = shaped - center[:, None, :]
    squares = jnp.sum(jnp.square(offset), axis=1)
    dev_ref[...] = offset.reshape(rows, middle).astype(bf16)
    for c in range(3):
        class_send[c * half : (c + 1) * half] = dot(gather[3 + c], dev_ref[...]).astype(bf16)
    lines = middle // LANES
    for at, values in ((0, exact(member, sums)), (lines, exact(member, squares))):
        for g in range(n_dp):
            for r in range(lines):
                sum_send[g, at + r : at + r + 1, :] = values[g : g + 1, r * LANES : (r + 1) * LANES]
    sum_recv[d] = sum_send[d]

    pl.semaphore_wait(barrier, n_dp + n_bn - 2)
    column_peers("query", query_own, query_all)
    for c in range(3):
        at = pl.ds(c * half, half)
        push("class", class_send.at[at], class_recv.at[at], (d ^ (c + 1), b))
    for k in range(1, n_dp):
        push("sum1", sum_send.at[d ^ k], sum_recv.at[d], (d ^ k, b))
    ship("a", 0)
    ship("c", 0)
    ship("b", 0)
    ship("d", 0)

    part = jnp.zeros((8, n_dp * slots), f32)
    loads[4].wait()

    arrived("sum1", most(sum_recv))
    parts = sum_recv[...]
    class_sums = parts[:, :lines]
    column_mean = jnp.sum(class_sums, axis=0) * (1.0 / rows)
    column_squares = jnp.sum(parts[:, lines:], axis=0)
    class_means = []
    for e in range(n_dp):
        class_means.append(class_sums[e] / jnp.maximum(counts[e], 1.0))
        column_squares = column_squares + counts[e] * jnp.square(class_means[e] - column_mean)
    own1[:lines] = column_mean
    own1[lines:] = column_squares
    group_peers("bn1", own1, all1)

    arrived("class", class_recv)
    near_held = jnp.concatenate([dev_ref[...], class_recv[:rows]], axis=0)
    far_send[...] = (dot(far_pick[0], near_held) + dot(far_pick[1], class_recv[rows:])).astype(bf16)
    push("far", far_send, far_recv, (d ^ 4, b))

    h_ref[...] = dot(stay_pick[0], near_held) + dot(stay_pick[1], class_recv[rows:])
    arrived("query", most(query_all))
    forward("c", 1)
    forward("a", 1)
    part = queue_steps(0, 1, part)
    forward("d", 1)
    forward("b", 1)
    mean, scale = group_stats("bn1", all1)
    for e in range(n_dp):
        to_line(class_ref, e, class_means[e] - mean)
    to_line(scale_ref, 0, scale)
    loads[5].wait()

    arrived("far", far_recv)
    h_ref[...] = h_ref[...] + dot(last_pick, far_recv[...])
    for s in range(slots):
        at = slice(s * cells, (s + 1) * cells)
        move = jnp.broadcast_to(class_ref[pl.ds(sources[s], 1), :], (cells, middle))
        h_ref[at] = jax.nn.relu((h_ref[at] + move) * scale_ref[0:1, :middle])
    act = h_ref[...]
    cell = lax.broadcasted_iota(jnp.int32, act.shape, 0) % cells
    before = jnp.where(cell == 0, 0.0, pltpu.roll(act, 1, 0)).astype(bf16)
    after = jnp.where(cell == cells - 1, 0.0, pltpu.roll(act, rows - 1, 0)).astype(bf16)
    h_ref[...] = dot(before, mid_ref[0]) + dot(act.astype(bf16), mid_ref[1]) + dot(after, mid_ref[2])
    send_stats("bn2", h_ref[...], own2, all2)
    forward("c", 2)
    forward("a", 2)
    part = queue_steps(1, 3, part)
    forward("d", 2)
    forward("b", 2)
    loads[6].wait()
    mean, scale = group_stats("bn2", all2)
    to_line(mean_ref, 0, mean)
    to_line(scale_ref, 0, scale)

    second = jax.nn.relu((h_ref[...] - mean_ref[0:1, :middle]) * scale_ref[0:1, :middle]).astype(bf16)
    wide_ref[...] = dot(second, out_ref[...])
    send_stats("bn3", wide_ref[...], own3, all3)
    part = queue_steps(3, 8, part)
    part_own[...] = jnp.sum(part, axis=0, keepdims=True)
    part_all[d] = part_own[...]
    column_peers("queue", part_own, part_all)
    for name in ORDERS:
        settle(name)
    loads[7].wait()
    mean, scale = group_stats("bn3", all3)
    to_line(mean_ref, 0, mean)
    to_line(scale_ref, 0, scale)

    z = None
    for name in "acbd":
        at = columns[name]
        normal = (wide_ref[:, at] - mean_ref[0:1, at]) * scale_ref[0:1, at]
        arrived(name + "2", lasts[name])
        feature = feature_ref[:, at] + dot(routes[name][4], lasts[name][...])
        block = jax.nn.relu(normal + feature).astype(bf16)
        pooled = jnp.mean(block.astype(f32).reshape(slots, cells, chunk), axis=1).astype(bf16)
        term = dot(pooled, head_ref[at])
        z = term if z is None else z + term
    key_own[...] = (z * lax.rsqrt(jnp.sum(z * z, axis=-1, keepdims=True) + EPS_UNIT)).astype(bf16)
    key_all[d] = key_own[...]
    column_peers("key", key_own, key_all)

    arrived("queue", most(part_all))
    negative_all = jnp.sum(part_all[...], axis=0)
    mine = lax.broadcasted_iota(jnp.int32, (slots, n_dp * slots), 1) == (
        lax.broadcasted_iota(jnp.int32, (slots, n_dp * slots), 0) + d * slots
    )
    negative_col = jnp.sum(jnp.where(mine, negative_all, 0.0), axis=1, keepdims=True)
    negative = jnp.sum(jnp.where(lane == sub, negative_col, 0.0), axis=0, keepdims=True)

    arrived("key", most(key_all))
    keys = key_all[...].reshape(n_dp * slots, key_all.shape[2])
    products = lax.dot_general(keys, query_own[...], (((1,), (1,)), ((), ())), preferred_element_type=f32)
    chosen = lax.broadcasted_iota(jnp.int32, products.shape, 0) == want
    logit = jnp.sum(jnp.where(chosen, products, 0.0), axis=0, keepdims=True) * INV_TEMP
    loss_ref[...] = jnp.log(jnp.exp(logit - INV_TEMP) + negative) + INV_TEMP - logit

    for phase, every_part in (("query", query_all), ("queue", part_all), ("key", key_all), ("sum1", sum_recv), ("bn1", all1), ("bn2", all2), ("bn3", all3)):
        sent(phase, most(every_part))
    sent("class", class_send)
    sent("far", far_send)
    for name in ORDERS:
        for step in range(3):
            sent(name + str(step), sends[name].at[step])


def on_device_shuffled(n_dp, n_bn, features, shuffle_masks, conv_in, conv_mid, conv_out, head, queries, queue, positive):
    f32, bf16 = jnp.float32, jnp.bfloat16
    slots, cells, channels = features.shape
    rows = slots * cells
    middle = conv_in.shape[1]
    width = queries.shape[1]

    def group_parts(c):
        tile = (2 * (c // LANES), LANES)
        return [pltpu.VMEM(tile, f32), pltpu.VMEM((n_bn,) + tile, f32)]

    chunk = channels // len(ORDERS)
    feature_parts = [
        pltpu.VMEM((3, rows // 2, chunk), bf16),
        pltpu.VMEM((rows, chunk), bf16),
        pltpu.VMEM((rows // 2, chunk), bf16),
    ]
    sums = pltpu.VMEM((n_dp, 2 * (middle // LANES), LANES), f32)
    hbm = pl.BlockSpec(memory_space=pltpu.HBM)
    loss = pl.pallas_call(
        functools.partial(shuffled_kernel, n_dp, n_bn),
        out_shape=jax.ShapeDtypeStruct((1, slots), f32),
        in_specs=[hbm] * 9,
        out_specs=pl.BlockSpec(memory_space=pltpu.VMEM),
        scratch_shapes=[
            pltpu.SMEM(shuffle_masks.shape, jnp.int32),
            pltpu.SMEM(positive.shape, jnp.int32),
            pltpu.VMEM(queries.shape, bf16),
            pltpu.VMEM((rows, channels), bf16),
            pltpu.VMEM(conv_in.shape, bf16),
            pltpu.VMEM(conv_mid.shape, bf16),
            pltpu.VMEM(conv_out.shape, bf16),
            pltpu.VMEM(head.shape, bf16),
            pltpu.VMEM(queue.shape, bf16),
            pltpu.VMEM((rows, middle), f32),
            pltpu.VMEM((rows, channels), f32),
            pltpu.VMEM((n_dp, middle), f32),
            pltpu.VMEM((8, channels), f32),
            pltpu.VMEM((8, channels), f32),
            pltpu.VMEM((rows, middle), bf16),
            pltpu.VMEM((3 * rows // 2, middle), bf16),
            pltpu.VMEM((3 * rows // 2, middle), bf16),
            pltpu.VMEM((rows // 2, middle), bf16),
            pltpu.VMEM((rows // 2, middle), bf16),
        ]
        + feature_parts * len(ORDERS)
        + [pltpu.VMEM((rows, channels), f32), sums, sums]
        + group_parts(middle)
        + group_parts(middle)
        + group_parts(channels)
        + [
            pltpu.VMEM((slots, width), bf16),
            pltpu.VMEM((n_dp, slots, width), bf16),
            pltpu.VMEM((1, n_dp * slots), f32),
            pltpu.VMEM((n_dp, 1, n_dp * slots), f32),
            pltpu.VMEM((slots, width), bf16),
            pltpu.VMEM((n_dp, slots, width), bf16),
            pltpu.SemaphoreType.DMA((8,)),
            pltpu.SemaphoreType.DMA((PANELS,)),
            pltpu.SemaphoreType.DMA((len(PHASES),)),
            pltpu.SemaphoreType.DMA((len(PHASES),)),
        ],
        compiler_params=pltpu.CompilerParams(
            collective_id=0, has_side_effects=True, vmem_limit_bytes=64 << 20
        ),
        name="shuffled_crops",
    )(shuffle_masks, positive, queries, features.reshape(rows, channels), conv_in, conv_mid, conv_out, head, queue)
    return loss.reshape(slots)


def on_device(n_dp, n_bn, *arrays):
    features, conv_in = arrays[0], arrays[2]
    slots, cells, channels = features.shape
    whole_lanes = conv_in.shape[1] % (2 * LANES) == 0 and channels % (4 * LANES) == 0
    if whole_lanes and n_dp == 8 and slots * cells == LANES and cells == 8 and n_bn <= 4:
        return on_device_shuffled(n_dp, n_bn, *arrays)
    return on_device_moving(*arrays)


def solution(mesh):
    return jax.shard_map(
        functools.partial(on_device, mesh.shape["dp"], mesh.shape["bn"]),
        mesh=mesh,
        in_specs=(
            P(("dp", "bn"), None, None),
            P(),
            P(),
            P(),
            P(),
            P(),
            P(("dp", "bn"), None),
            P("dp", None),
            P(("dp", "bn")),
        ),
        out_specs=P(("dp", "bn")),
        check_vma=False,
    )
```

```python
import functools

import jax
import jax.numpy as jnp
from jax import lax
from jax.experimental import pallas as pl
from jax.experimental.pallas import tpu as pltpu
from jax.sharding import PartitionSpec as P

EPS_BN = 1e-05
EPS_UNIT = 1e-06
INV_TEMP = 1.0 / 0.07


def partner_2(value, axis, distance):
    return lax.ppermute(value, axis, [(i, i ^ 1 << distance) for i in range(lax.axis_size(axis))])


def unit_rows(values):
    values = values.astype(jnp.float32)
    return values * lax.rsqrt(jnp.sum(values * values, axis=-1, keepdims=True) + EPS_UNIT)


def group_norm(values, row_total):
    first = lax.psum(jnp.sum(values, axis=0), "bn")
    center = first / row_total
    spread = lax.psum(jnp.sum(jnp.square(values - center), axis=0), "bn") / row_total
    return (values - center) * lax.rsqrt(spread + EPS_BN)


def moving_slots(shuffle_masks, level, half):
    flags = jnp.bitwise_and(jnp.right_shift(shuffle_masks, level), 1)
    return jnp.argsort(1 - flags, stable=True)[:half]


def on_device_moving(features, shuffle_masks, conv_in, conv_mid, conv_out, head, queries, queue, positive):
    dp_count = lax.axis_size("dp")
    bn_count = lax.axis_size("bn")
    bit_count = dp_count.bit_length() - 1
    crop_dev, positions, channels = features.shape
    half = crop_dev // 2
    middle = conv_in.shape[1]
    query_unit = unit_rows(queries).astype(jnp.bfloat16)
    query_all = lax.all_gather(query_unit, "dp", axis=0, tiled=True)
    shuffled = features
    for level in range(bit_count):
        moving = moving_slots(shuffle_masks, level, half)
        chosen = (moving[:, None] == jnp.arange(crop_dev)[None, :]).astype(jnp.bfloat16)
        leaving = jnp.dot(
            chosen, shuffled.reshape(crop_dev, positions * channels), preferred_element_type=jnp.float32
        ).astype(jnp.bfloat16)
        partner = partner_2(leaving.reshape(half, positions, channels), "dp", level)
        shuffled = shuffled.at[moving].set(partner)
    row_total = crop_dev * positions * bn_count
    flat_rows = shuffled.reshape(crop_dev * positions, channels)
    first_sum = jnp.dot(flat_rows, conv_in, preferred_element_type=jnp.float32)
    first_act = jax.nn.relu(group_norm(first_sum, row_total)).astype(jnp.bfloat16)
    tap_maps = first_act.reshape(crop_dev, positions, middle)
    padded = jnp.pad(tap_maps, ((0, 0), (1, 1), (0, 0)))
    stacked = jnp.concatenate([padded[:, tap : tap + positions, :] for tap in range(3)], axis=2)
    second_sum = jnp.dot(
        stacked.reshape(crop_dev * positions, 3 * middle),
        conv_mid.reshape(3 * middle, middle),
        preferred_element_type=jnp.float32,
    )
    second_act = jax.nn.relu(group_norm(second_sum, row_total)).astype(jnp.bfloat16)
    third_sum = jnp.dot(second_act, conv_out, preferred_element_type=jnp.float32)
    block = jax.nn.relu(group_norm(third_sum, row_total) + flat_rows.astype(jnp.float32)).astype(
        jnp.bfloat16
    )
    pooled = jnp.mean(
        block.reshape(crop_dev, positions, channels).astype(jnp.float32), axis=1
    ).astype(jnp.bfloat16)
    key_unit = unit_rows(jnp.dot(pooled, head, preferred_element_type=jnp.float32)).astype(
        jnp.bfloat16
    )
    for level in range(bit_count):
        moving = moving_slots(shuffle_masks, level, half)
        partner = partner_2(jnp.take(key_unit, moving, axis=0), "dp", level)
        key_unit = key_unit.at[moving].set(partner)
    queue_unit = unit_rows(queue).astype(jnp.bfloat16)
    scores = jnp.dot(query_all, queue_unit.T, preferred_element_type=jnp.float32) * INV_TEMP
    queue_part = jnp.sum(jnp.exp(scores - INV_TEMP), axis=1)
    key_all = lax.all_gather(key_unit, "dp", axis=0, tiled=True)
    slot_of = positive % crop_dev
    column = positive // crop_dev // bn_count
    picked = jnp.take(key_all, column * crop_dev + slot_of, axis=0)
    positive_logit = (
        jnp.sum(query_unit.astype(jnp.float32) * picked.astype(jnp.float32), axis=-1) * INV_TEMP
    )
    negative = lax.psum_scatter(queue_part, "dp", scatter_dimension=0, tiled=True)
    return jnp.log(jnp.exp(positive_logit - INV_TEMP) + negative) + INV_TEMP - positive_logit


MESH = pl.DeviceIdType.MESH
LANES = 128
QUEUE_STEPS = 8
PANELS = 2
PHASES = (
    "query", "queue", "key", "sum1", "bn1", "bn2", "bn3", "class0", "class1", "far0", "far1",
)
ORDERS = {'a': (2, 0, 1), 'b': (2, 0, 1), 'c': (0, 1, 2), 'd': (0, 1, 2)}
STEPS = tuple(name + str(step) for name in ORDERS for step in range(3))


def shuffled_kernel(
    n_dp, n_bn,
    masks_hbm, positive_hbm, queries_hbm, x_hbm, in_hbm, mid_hbm, out_hbm, head_hbm, queue_hbm,
    loss_ref,
    masks, positive, queries,
    x_ref, in_ref, mid_ref, out_ref, head_ref, queue_ref,
    h_ref, wide_ref, class_ref, mean_ref, scale_ref,
    dev_ref, class_send, class_recv, far_send, far_recv,
    feature_ref,
    sum_send, sum_recv, own1, all1, own2, all2, own3, all3,
    query_own, query_all, part_own, part_all, key_own, key_all,
    load_sem, panel_sem, send_sem, recv_sem,
    *piece_refs,
):
    f32, bf16 = jnp.float32, jnp.bfloat16
    d = lax.axis_index("dp")
    b = lax.axis_index("bn")
    rows, channels = x_ref.shape
    slots = masks.shape[0]
    cells = rows // slots
    half = rows // 2
    middle = in_ref.shape[1]
    chunk = channels // len(ORDERS)
    total = float(rows * n_bn)
    sides = [slice(0, middle // 2), slice(middle // 2, middle)]

    panel = channels // PANELS
    panels = [
        pltpu.make_async_copy(
            in_hbm.at[pl.ds(i * panel, panel)], in_ref.at[pl.ds(i * panel, panel)], panel_sem.at[i]
        )
        for i in range(PANELS)
    ]
    loads = [
        pltpu.make_async_copy(src, dst, load_sem.at[i])
        for i, (src, dst) in enumerate(
            [(masks_hbm, masks), (positive_hbm, positive), (queries_hbm, queries), (x_hbm, x_ref), (queue_hbm, queue_ref), (mid_hbm, mid_ref), (out_hbm, out_ref), (head_hbm, head_ref)]
        )
    ]
    for load in loads[:4] + panels:
        load.start()

    barrier = pltpu.get_barrier_semaphore()
    dp_peers = [(d ^ k, b) for k in range(1, n_dp)]
    bn_peers = [(d, lax.rem(b + k, n_bn)) for k in range(1, n_bn)]
    for peer in dp_peers + bn_peers:
        pl.semaphore_signal(barrier, inc=1, device_id=peer, device_id_type=MESH)

    def push(phase, src, dst, peer):
        i = (PHASES + STEPS).index(phase)
        pltpu.make_async_remote_copy(
            src_ref=src, dst_ref=dst, send_sem=send_sem.at[i], recv_sem=recv_sem.at[i],
            device_id=peer, device_id_type=MESH,
        ).start()

    def arrived(phase, view):
        pltpu.make_async_copy(view, view, recv_sem.at[(PHASES + STEPS).index(phase)]).wait()

    def sent(phase, view):
        pltpu.make_async_copy(view, view, send_sem.at[(PHASES + STEPS).index(phase)]).wait()

    def most(ref):
        return ref.at[pl.ds(0, ref.shape[0] - 1)]

    def column_peers(phase, src, dst):
        for peer in dp_peers:
            push(phase, src, dst.at[d], peer)

    def exact(a, c):
        return jnp.dot(a, c, preferred_element_type=f32, precision=lax.Precision.HIGHEST)

    def dot(a, c):
        return jnp.dot(a, c, preferred_element_type=f32)

    for load in loads[:3]:
        load.wait()

    q = queries[...].astype(f32)
    query_unit = (q * lax.rsqrt(jnp.sum(q * q, axis=-1, keepdims=True) + EPS_UNIT)).astype(bf16)
    query_own[...] = query_unit
    query_all[d] = query_unit

    lane = lax.broadcasted_iota(jnp.int32, (slots, slots), 1)
    sub = lax.broadcasted_iota(jnp.int32, (slots, slots), 0)
    lane1 = lax.broadcasted_iota(jnp.int32, (1, slots), 1)
    lane_8 = lax.broadcasted_iota(jnp.int32, (8, LANES), 1)
    sub_8 = lax.broadcasted_iota(jnp.int32, (8, LANES), 0)
    slot_8 = lane_8 // cells
    mask_row = jnp.zeros((slots, slots), jnp.int32)
    mask_col = jnp.zeros((slots, slots), jnp.int32)
    want = jnp.zeros((1, slots), jnp.int32)
    mask_8 = jnp.zeros((8, LANES), jnp.int32)
    sources = []
    for s in range(slots):
        mask = masks[s]
        sources.append(mask ^ d)
        mask_row = jnp.where(lane == s, sources[s], mask_row)
        mask_col = jnp.where(sub == s, sources[s], mask_col)
        mask_8 = jnp.where(slot_8 == s, mask, mask_8)
        place = positive[s]
        slot = lax.rem(place, slots)
        column = lax.div(place, slots * n_bn) ^ masks[slot]
        want = jnp.where(lane1 == s, column * slots + slot, want)
    same = (mask_row == mask_col).astype(f32)
    local_mean = same / (jnp.sum(same, axis=0, keepdims=True) * float(cells))
    member = (mask_row[:n_dp] == sub[:n_dp]).astype(f32)
    counts = []
    for e in range(n_dp):
        count = jnp.int32(0)
        for s in range(slots):
            count = count + (sources[s] == e).astype(jnp.int32)
        counts.append((count * cells).astype(f32))

    bits = [(mask_8 & (1 << level)) != 0 for level in range(3)]
    kind = mask_8 & 3
    flags = jnp.where(sub_8 == 0, mask_8 & 1, jnp.where(sub_8 == 1, (mask_8 >> 1) & 1, (mask_8 >> 2) & 1))
    flags = jnp.where(sub_8 >= 3, (kind == sub_8 - 2).astype(jnp.int32), flags)
    before_r = lax.broadcasted_iota(jnp.int32, (rows, rows), 0)
    before_c = lax.broadcasted_iota(jnp.int32, (rows, rows), 1)
    earlier = jnp.logical_and(before_r % cells == 0, before_r // cells < before_c // cells)
    rank = dot(flags.astype(f32).astype(bf16), jnp.where(earlier, 1.0, 0.0).astype(bf16))
    places = jnp.where(flags != 0, rank * float(cells) + (lane_8 % cells + 1).astype(f32), 0.0)

    def every(i):
        return jnp.broadcast_to(places[i : i + 1], (8, LANES))

    to_level = [every(i) for i in range(3)]
    tag = (lane_8 + 1).astype(f32)

    def picks(count, codes):
        wanted = (lax.broadcasted_iota(jnp.int32, (count, codes.shape[1]), 0) + 1).astype(f32)
        return jnp.where(wanted == codes, 1.0, 0.0).astype(bf16)

    gather = [picks(half, places[i : i + 1]) for i in range(6)]

    def moved(table, which):
        stacked = jnp.zeros((8, LANES), f32)
        for i, line in enumerate(table):
            stacked = jnp.where(sub_8 == i, line, stacked)
        return lax.dot_general(
            stacked.astype(bf16), which, (((1,), (1,)), ((), ())), preferred_element_type=f32
        )

    low_lane = lax.broadcasted_iota(jnp.int32, (1, LANES), 1) < half

    def unless(flag, line):
        return jnp.where(flag, 0.0, line)

    by_order = {}
    for i, j, k in sorted(set(ORDERS.values())):
        table = [
            to_level[j], unless(bits[j], to_level[k]), to_level[k],
            unless(jnp.logical_or(bits[j], bits[k]), tag), unless(bits[k], tag),
        ]
        pair = moved(table, jnp.concatenate([gather[i], gather[j]], axis=0))
        second = jnp.concatenate([unless(bits[i], to_level[j])[:1], pair[0:1]], axis=1)
        third = jnp.concatenate(
            [
                unless(jnp.logical_or(bits[i], bits[j]), to_level[k])[:1],
                jnp.where(low_lane, pair[1:2], pair[2:3]),
            ],
            axis=1,
        )
        final = jnp.concatenate(
            [unless(mask_8 != 0, tag)[:1], jnp.where(low_lane, pair[3:4], pair[4:5])], axis=1
        )
        last = moved([tag], gather[k])[:1]
        by_order[i, j, k] = (gather[i], picks(half, second)[:, : rows + half], picks(half, third), picks(rows, final), picks(rows, last))
    table = [to_level[2], unless(bits[2], tag)]
    near = moved(table, jnp.concatenate(gather[3:5], axis=0))
    both = moved(table, gather[5])
    far_codes = jnp.concatenate([unless(kind != 0, to_level[2])[:1], near[0:1]], axis=1)
    stay_codes = jnp.concatenate([unless(mask_8 != 0, tag)[:1], near[1:2]], axis=1)
    far_pick = (picks(half, far_codes), picks(half, both[0:1]))
    stay_pick = (picks(rows, stay_codes), picks(rows, both[1:2]))
    routes = {name: by_order[order] for name, order in ORDERS.items()}
    last_pick = picks(rows, moved([tag], gather[2])[:1])

    sends = dict(zip(ORDERS, piece_refs[0::3]))
    pairs = dict(zip(ORDERS, piece_refs[1::3]))
    lasts = dict(zip(ORDERS, piece_refs[2::3]))
    columns = {name: slice(i * chunk, (i + 1) * chunk) for i, name in enumerate(ORDERS)}

    def stage(name, step):
        held = x_ref[:, columns[name]]
        if step:
            held = jnp.concatenate([held, pairs[name][: step * half]], axis=0)
        sends[name][step] = dot(routes[name][step], held).astype(bf16)

    def landing(name, step):
        return lasts[name] if step == 2 else pairs[name].at[pl.ds(step * half, half)]

    def ship(name, step):
        peer = (d ^ (1 << ORDERS[name][step]), b)
        push(name + str(step), sends[name].at[step], landing(name, step), peer)

    def forward(name, step):
        arrived(name + str(step - 1), landing(name, step - 1))
        stage(name, step)
        ship(name, step)

    def settle(name):
        held = jnp.concatenate([x_ref[:, columns[name]], pairs[name][...]], axis=0)
        feature_ref[:, columns[name]] = dot(routes[name][3], held)

    def to_rows(ref, at, values):
        for r in range(values.shape[1] // LANES):
            ref[at + r : at + r + 1, :] = values[:, r * LANES : (r + 1) * LANES]

    def to_line(ref, at, values):
        for r in range(values.shape[0]):
            ref[at : at + 1, r * LANES : (r + 1) * LANES] = values[r : r + 1]

    def group_peers(phase, own, every_part):
        every_part[b] = own[...]
        for peer in bn_peers:
            push(phase, own, every_part.at[b], peer)

    def group_stats(phase, every_part):
        arrived(phase, most(every_part))
        lines = every_part.shape[1] // 2
        parts = every_part[...]
        means = parts[:, :lines]
        mean = jnp.sum(means, axis=0) * (1.0 / n_bn)
        spread = jnp.sum(parts[:, lines:], axis=0) + float(rows) * jnp.sum(
            jnp.square(means - mean[None]), axis=0
        )
        return mean, lax.rsqrt(spread * (1.0 / total) + EPS_BN)

    def send_stats(phase, h, own, every_part):
        mean = jnp.sum(h, axis=0, keepdims=True) * (1.0 / rows)
        squares = jnp.sum(jnp.square(h - mean), axis=0, keepdims=True)
        to_rows(own, 0, mean)
        to_rows(own, own.shape[0] // 2, squares)
        group_peers(phase, own, every_part)

    ones = jnp.ones((LANES, LANES), bf16)
    step_rows = queue_ref.shape[0] // QUEUE_STEPS

    def queue_step(c, total_part):
        raw = queue_ref[pl.ds(c * step_rows, step_rows), :].astype(f32)
        square = raw * raw
        high = square.astype(bf16)
        low = (square - high.astype(f32)).astype(bf16)
        norm = dot(high, ones) + dot(low, ones)
        unit = (raw * lax.rsqrt(norm + EPS_UNIT)).astype(bf16)
        flat_queries = query_all[...].reshape(n_dp * slots, query_all.shape[2])
        scores = lax.dot_general(unit, flat_queries, (((1,), (1,)), ((), ())), preferred_element_type=f32)
        terms = jnp.exp(scores * INV_TEMP - INV_TEMP)
        return total_part + jnp.sum(terms.reshape(step_rows // 8, 8, n_dp * slots), axis=0)

    def queue_steps(first, last, total_part):
        return lax.fori_loop(first, last, queue_step, total_part)

    loads[3].wait()
    first = None
    for i in range(PANELS):
        panels[i].wait()
        at = slice(i * panel, (i + 1) * panel)
        term = dot(x_ref[:, at], in_ref[at])
        first = term if first is None else first + term
        if i == 0:
            for load in loads[4:]:
                load.start()
    shaped = first.reshape(slots, cells, middle)
    sums = jnp.sum(shaped, axis=1)
    center = exact(local_mean, sums)
    offset = shaped - center[:, None, :]
    squares = jnp.sum(jnp.square(offset), axis=1)
    dev_ref[...] = offset.reshape(rows, middle).astype(bf16)
    for side, at in enumerate(sides):
        for c in range(3):
            class_send[side, c * half : (c + 1) * half] = dot(gather[3 + c], dev_ref[:, at]).astype(bf16)
    lines = middle // LANES
    for at, values in ((0, exact(member, sums)), (lines, exact(member, squares))):
        for g in range(n_dp):
            for r in range(lines):
                sum_send[g, at + r : at + r + 1, :] = values[g : g + 1, r * LANES : (r + 1) * LANES]
    sum_recv[d] = sum_send[d]

    pl.semaphore_wait(barrier, n_dp + n_bn - 2)
    column_peers("query", query_own, query_all)
    for side in range(2):
        for c in range(3):
            at = pl.ds(c * half, half)
            push("class" + str(side), class_send.at[side, at], class_recv.at[side, at], (d ^ (c + 1), b))
    for k in range(1, n_dp):
        push("sum1", sum_send.at[d ^ k], sum_recv.at[d], (d ^ k, b))
    stage("a", 0)
    ship("a", 0)
    stage("c", 0)
    ship("c", 0)
    stage("b", 0)
    ship("b", 0)
    stage("d", 0)
    ship("d", 0)

    part = jnp.zeros((8, n_dp * slots), f32)
    loads[4].wait()

    arrived("sum1", most(sum_recv))
    parts = sum_recv[...]
    class_sums = parts[:, :lines]
    column_mean = jnp.sum(class_sums, axis=0) * (1.0 / rows)
    column_squares = jnp.sum(parts[:, lines:], axis=0)
    class_means = []
    for e in range(n_dp):
        class_means.append(class_sums[e] / jnp.maximum(counts[e], 1.0))
        column_squares = column_squares + counts[e] * jnp.square(class_means[e] - column_mean)
    own1[:lines] = column_mean
    own1[lines:] = column_squares
    group_peers("bn1", own1, all1)

    for side, at in enumerate(sides):
        arrived("class" + str(side), class_recv.at[side])
        near_held = jnp.concatenate([dev_ref[:, at], class_recv[side, :rows]], axis=0)
        far_send[side] = (dot(far_pick[0], near_held) + dot(far_pick[1], class_recv[side, rows:])).astype(bf16)
        push("far" + str(side), far_send.at[side], far_recv.at[side], (d ^ 4, b))
    for side, at in enumerate(sides):
        near_held = jnp.concatenate([dev_ref[:, at], class_recv[side, :rows]], axis=0)
        h_ref[:, at] = dot(stay_pick[0], near_held) + dot(stay_pick[1], class_recv[side, rows:])
    arrived("query", most(query_all))
    forward("c", 1)
    forward("a", 1)
    part = queue_steps(0, 1, part)
    forward("d", 1)
    forward("b", 1)
    mean, scale = group_stats("bn1", all1)
    for e in range(n_dp):
        to_line(class_ref, e, class_means[e] - mean)
    to_line(scale_ref, 0, scale)
    loads[5].wait()

    for side, at in enumerate(sides):
        arrived("far" + str(side), far_recv.at[side])
        h_ref[:, at] = h_ref[:, at] + dot(last_pick, far_recv[side])
    for s in range(slots):
        at = slice(s * cells, (s + 1) * cells)
        move = jnp.broadcast_to(class_ref[pl.ds(sources[s], 1), :], (cells, middle))
        h_ref[at] = jax.nn.relu((h_ref[at] + move) * scale_ref[0:1, :middle])
    act = h_ref[...]
    cell = lax.broadcasted_iota(jnp.int32, act.shape, 0) % cells
    before = jnp.where(cell == 0, 0.0, pltpu.roll(act, 1, 0)).astype(bf16)
    after = jnp.where(cell == cells - 1, 0.0, pltpu.roll(act, rows - 1, 0)).astype(bf16)
    h_ref[...] = dot(before, mid_ref[0]) + dot(act.astype(bf16), mid_ref[1]) + dot(after, mid_ref[2])
    send_stats("bn2", h_ref[...], own2, all2)
    forward("c", 2)
    forward("a", 2)
    part = queue_steps(1, 3, part)
    forward("d", 2)
    forward("b", 2)
    loads[6].wait()
    mean, scale = group_stats("bn2", all2)
    to_line(mean_ref, 0, mean)
    to_line(scale_ref, 0, scale)

    second = jax.nn.relu((h_ref[...] - mean_ref[0:1, :middle]) * scale_ref[0:1, :middle]).astype(bf16)
    wide_ref[...] = dot(second, out_ref[...])
    send_stats("bn3", wide_ref[...], own3, all3)
    part = queue_steps(3, 8, part)
    part_own[...] = jnp.sum(part, axis=0, keepdims=True)
    part_all[d] = part_own[...]
    column_peers("queue", part_own, part_all)
    for name in ORDERS:
        settle(name)
    loads[7].wait()
    mean, scale = group_stats("bn3", all3)
    to_line(mean_ref, 0, mean)
    to_line(scale_ref, 0, scale)

    z = None
    for name in "acbd":
        at = columns[name]
        normal = (wide_ref[:, at] - mean_ref[0:1, at]) * scale_ref[0:1, at]
        arrived(name + "2", lasts[name])
        feature = feature_ref[:, at] + dot(routes[name][4], lasts[name][...])
        block = jax.nn.relu(normal + feature).astype(bf16)
        pooled = jnp.mean(block.astype(f32).reshape(slots, cells, chunk), axis=1).astype(bf16)
        term = dot(pooled, head_ref[at])
        z = term if z is None else z + term
    key_own[...] = (z * lax.rsqrt(jnp.sum(z * z, axis=-1, keepdims=True) + EPS_UNIT)).astype(bf16)
    key_all[d] = key_own[...]
    column_peers("key", key_own, key_all)

    arrived("queue", most(part_all))
    negative_all = jnp.sum(part_all[...], axis=0)
    mine = lax.broadcasted_iota(jnp.int32, (slots, n_dp * slots), 1) == (
        lax.broadcasted_iota(jnp.int32, (slots, n_dp * slots), 0) + d * slots
    )
    negative_col = jnp.sum(jnp.where(mine, negative_all, 0.0), axis=1, keepdims=True)
    negative = jnp.sum(jnp.where(lane == sub, negative_col, 0.0), axis=0, keepdims=True)

    arrived("key", most(key_all))
    keys = key_all[...].reshape(n_dp * slots, key_all.shape[2])
    products = lax.dot_general(keys, query_own[...], (((1,), (1,)), ((), ())), preferred_element_type=f32)
    chosen = lax.broadcasted_iota(jnp.int32, products.shape, 0) == want
    logit = jnp.sum(jnp.where(chosen, products, 0.0), axis=0, keepdims=True) * INV_TEMP
    loss_ref[...] = jnp.log(jnp.exp(logit - INV_TEMP) + negative) + INV_TEMP - logit

    for phase, every_part in (("query", query_all), ("queue", part_all), ("key", key_all), ("sum1", sum_recv), ("bn1", all1), ("bn2", all2), ("bn3", all3)):
        sent(phase, most(every_part))
    for side in range(2):
        sent("class" + str(side), class_send.at[side])
        sent("far" + str(side), far_send.at[side])
    for name in ORDERS:
        for step in range(3):
            sent(name + str(step), sends[name].at[step])


def on_device_shuffled(n_dp, n_bn, features, shuffle_masks, conv_in, conv_mid, conv_out, head, queries, queue, positive):
    f32, bf16 = jnp.float32, jnp.bfloat16
    slots, cells, channels = features.shape
    rows = slots * cells
    middle = conv_in.shape[1]
    width = queries.shape[1]

    def group_parts(c):
        tile = (2 * (c // LANES), LANES)
        return [pltpu.VMEM(tile, f32), pltpu.VMEM((n_bn,) + tile, f32)]

    chunk = channels // len(ORDERS)
    feature_parts = [
        pltpu.VMEM((3, rows // 2, chunk), bf16),
        pltpu.VMEM((rows, chunk), bf16),
        pltpu.VMEM((rows // 2, chunk), bf16),
    ]
    sums = pltpu.VMEM((n_dp, 2 * (middle // LANES), LANES), f32)
    hbm = pl.BlockSpec(memory_space=pltpu.HBM)
    loss = pl.pallas_call(
        functools.partial(shuffled_kernel, n_dp, n_bn),
        out_shape=jax.ShapeDtypeStruct((1, slots), f32),
        in_specs=[hbm] * 9,
        out_specs=pl.BlockSpec(memory_space=pltpu.VMEM),
        scratch_shapes=[
            pltpu.SMEM(shuffle_masks.shape, jnp.int32),
            pltpu.SMEM(positive.shape, jnp.int32),
            pltpu.VMEM(queries.shape, bf16),
            pltpu.VMEM((rows, channels), bf16),
            pltpu.VMEM(conv_in.shape, bf16),
            pltpu.VMEM(conv_mid.shape, bf16),
            pltpu.VMEM(conv_out.shape, bf16),
            pltpu.VMEM(head.shape, bf16),
            pltpu.VMEM(queue.shape, bf16),
            pltpu.VMEM((rows, middle), f32),
            pltpu.VMEM((rows, channels), f32),
            pltpu.VMEM((n_dp, middle), f32),
            pltpu.VMEM((8, channels), f32),
            pltpu.VMEM((8, channels), f32),
            pltpu.VMEM((rows, middle), bf16),
            pltpu.VMEM((2, 3 * rows // 2, middle // 2), bf16),
            pltpu.VMEM((2, 3 * rows // 2, middle // 2), bf16),
            pltpu.VMEM((2, rows // 2, middle // 2), bf16),
            pltpu.VMEM((2, rows // 2, middle // 2), bf16),
        ]
        + [pltpu.VMEM((rows, channels), f32), sums, sums]
        + group_parts(middle)
        + group_parts(middle)
        + group_parts(channels)
        + [
            pltpu.VMEM((slots, width), bf16),
            pltpu.VMEM((n_dp, slots, width), bf16),
            pltpu.VMEM((1, n_dp * slots), f32),
            pltpu.VMEM((n_dp, 1, n_dp * slots), f32),
            pltpu.VMEM((slots, width), bf16),
            pltpu.VMEM((n_dp, slots, width), bf16),
            pltpu.SemaphoreType.DMA((8,)),
            pltpu.SemaphoreType.DMA((PANELS,)),
            pltpu.SemaphoreType.DMA((len(PHASES + STEPS),)),
            pltpu.SemaphoreType.DMA((len(PHASES + STEPS),)),
        ]
        + feature_parts * len(ORDERS),
        compiler_params=pltpu.CompilerParams(
            collective_id=0, has_side_effects=True, vmem_limit_bytes=64 << 20
        ),
        name="shuffled_crops",
    )(shuffle_masks, positive, queries, features.reshape(rows, channels), conv_in, conv_mid, conv_out, head, queue)
    return loss.reshape(slots)


def on_device(n_dp, n_bn, *arrays):
    features, conv_in = arrays[0], arrays[2]
    slots, cells, channels = features.shape
    whole_lanes = conv_in.shape[1] % (2 * LANES) == 0 and channels % (4 * LANES) == 0
    if whole_lanes and n_dp == 8 and slots * cells == LANES and cells == 8 and n_bn <= 4:
        return on_device_shuffled(n_dp, n_bn, *arrays)
    return on_device_moving(*arrays)


def solution(mesh):
    return jax.shard_map(
        functools.partial(on_device, mesh.shape["dp"], mesh.shape["bn"]),
        mesh=mesh,
        in_specs=(
            P(("dp", "bn"), None, None),
            P(),
            P(),
            P(),
            P(),
            P(),
            P(("dp", "bn"), None),
            P("dp", None),
            P(("dp", "bn")),
        ),
        out_specs=P(("dp", "bn")),
        check_vma=False,
    )
```

```python
import functools

import jax
import jax.numpy as jnp
from jax import lax
from jax.experimental import pallas as pl
from jax.experimental.pallas import tpu as pltpu
from jax.sharding import PartitionSpec as P

EPS_BN = 1e-05
EPS_UNIT = 1e-06
INV_TEMP = 1.0 / 0.07


def partner_2(value, axis, distance):
    return lax.ppermute(value, axis, [(i, i ^ 1 << distance) for i in range(lax.axis_size(axis))])


def unit_rows(values):
    values = values.astype(jnp.float32)
    return values * lax.rsqrt(jnp.sum(values * values, axis=-1, keepdims=True) + EPS_UNIT)


def group_norm(values, row_total):
    first = lax.psum(jnp.sum(values, axis=0), "bn")
    center = first / row_total
    spread = lax.psum(jnp.sum(jnp.square(values - center), axis=0), "bn") / row_total
    return (values - center) * lax.rsqrt(spread + EPS_BN)


def moving_slots(shuffle_masks, level, half):
    flags = jnp.bitwise_and(jnp.right_shift(shuffle_masks, level), 1)
    return jnp.argsort(1 - flags, stable=True)[:half]


def on_device_moving(features, shuffle_masks, conv_in, conv_mid, conv_out, head, queries, queue, positive):
    dp_count = lax.axis_size("dp")
    bn_count = lax.axis_size("bn")
    bit_count = dp_count.bit_length() - 1
    crop_dev, positions, channels = features.shape
    half = crop_dev // 2
    middle = conv_in.shape[1]
    query_unit = unit_rows(queries).astype(jnp.bfloat16)
    query_all = lax.all_gather(query_unit, "dp", axis=0, tiled=True)
    shuffled = features
    for level in range(bit_count):
        moving = moving_slots(shuffle_masks, level, half)
        chosen = (moving[:, None] == jnp.arange(crop_dev)[None, :]).astype(jnp.bfloat16)
        leaving = jnp.dot(
            chosen, shuffled.reshape(crop_dev, positions * channels), preferred_element_type=jnp.float32
        ).astype(jnp.bfloat16)
        partner = partner_2(leaving.reshape(half, positions, channels), "dp", level)
        shuffled = shuffled.at[moving].set(partner)
    row_total = crop_dev * positions * bn_count
    flat_rows = shuffled.reshape(crop_dev * positions, channels)
    first_sum = jnp.dot(flat_rows, conv_in, preferred_element_type=jnp.float32)
    first_act = jax.nn.relu(group_norm(first_sum, row_total)).astype(jnp.bfloat16)
    tap_maps = first_act.reshape(crop_dev, positions, middle)
    padded = jnp.pad(tap_maps, ((0, 0), (1, 1), (0, 0)))
    stacked = jnp.concatenate([padded[:, tap : tap + positions, :] for tap in range(3)], axis=2)
    second_sum = jnp.dot(
        stacked.reshape(crop_dev * positions, 3 * middle),
        conv_mid.reshape(3 * middle, middle),
        preferred_element_type=jnp.float32,
    )
    second_act = jax.nn.relu(group_norm(second_sum, row_total)).astype(jnp.bfloat16)
    third_sum = jnp.dot(second_act, conv_out, preferred_element_type=jnp.float32)
    block = jax.nn.relu(group_norm(third_sum, row_total) + flat_rows.astype(jnp.float32)).astype(
        jnp.bfloat16
    )
    pooled = jnp.mean(
        block.reshape(crop_dev, positions, channels).astype(jnp.float32), axis=1
    ).astype(jnp.bfloat16)
    key_unit = unit_rows(jnp.dot(pooled, head, preferred_element_type=jnp.float32)).astype(
        jnp.bfloat16
    )
    for level in range(bit_count):
        moving = moving_slots(shuffle_masks, level, half)
        partner = partner_2(jnp.take(key_unit, moving, axis=0), "dp", level)
        key_unit = key_unit.at[moving].set(partner)
    queue_unit = unit_rows(queue).astype(jnp.bfloat16)
    scores = jnp.dot(query_all, queue_unit.T, preferred_element_type=jnp.float32) * INV_TEMP
    queue_part = jnp.sum(jnp.exp(scores - INV_TEMP), axis=1)
    key_all = lax.all_gather(key_unit, "dp", axis=0, tiled=True)
    slot_of = positive % crop_dev
    column = positive // crop_dev // bn_count
    picked = jnp.take(key_all, column * crop_dev + slot_of, axis=0)
    positive_logit = (
        jnp.sum(query_unit.astype(jnp.float32) * picked.astype(jnp.float32), axis=-1) * INV_TEMP
    )
    negative = lax.psum_scatter(queue_part, "dp", scatter_dimension=0, tiled=True)
    return jnp.log(jnp.exp(positive_logit - INV_TEMP) + negative) + INV_TEMP - positive_logit


MESH = pl.DeviceIdType.MESH
LANES = 128
QUEUE_STEPS = 8
PANELS = 2
PHASES = (
    "query", "queue", "key", "sum1", "bn1", "bn2", "bn3", "class0", "class1", "far0", "far1",
)
ORDERS = {'a': (2, 0, 1), 'b': (2, 0, 1), 'c': (0, 1, 2), 'd': (0, 1, 2)}
STEPS = tuple(name + str(step) for name in ORDERS for step in range(3))


def shuffled_kernel(
    n_dp, n_bn,
    masks_hbm, positive_hbm, queries_hbm, x_hbm, in_hbm, mid_hbm, out_hbm, head_hbm, queue_hbm,
    loss_ref,
    masks, positive, queries,
    x_ref, in_ref, mid_ref, out_ref, head_ref, queue_ref,
    h_ref, wide_ref, class_ref, mean_ref, scale_ref,
    dev_ref, class_send, class_recv, far_send, far_recv,
    feature_ref,
    sum_send, sum_recv, own1, all1, own2, all2, own3, all3,
    query_own, query_all, part_own, part_all, key_own, key_all,
    load_sem, panel_sem, send_sem, recv_sem,
    *piece_refs,
):
    f32, bf16 = jnp.float32, jnp.bfloat16
    d = lax.axis_index("dp")
    b = lax.axis_index("bn")
    rows, channels = x_ref.shape
    slots = masks.shape[0]
    cells = rows // slots
    half = rows // 2
    middle = in_ref.shape[1]
    chunk = channels // len(ORDERS)
    total = float(rows * n_bn)
    sides = [slice(0, middle // 2), slice(middle // 2, middle)]

    panel = channels // PANELS
    panels = [
        pltpu.make_async_copy(
            in_hbm.at[pl.ds(i * panel, panel)], in_ref.at[pl.ds(i * panel, panel)], panel_sem.at[i]
        )
        for i in range(PANELS)
    ]
    loads = [
        pltpu.make_async_copy(src, dst, load_sem.at[i])
        for i, (src, dst) in enumerate(
            [(masks_hbm, masks), (positive_hbm, positive), (queries_hbm, queries), (x_hbm, x_ref), (queue_hbm, queue_ref), (mid_hbm, mid_ref), (out_hbm, out_ref), (head_hbm, head_ref)]
        )
    ]
    for load in loads[:4] + panels:
        load.start()

    barrier = pltpu.get_barrier_semaphore()
    dp_peers = [(d ^ k, b) for k in range(1, n_dp)]
    bn_peers = [(d, lax.rem(b + k, n_bn)) for k in range(1, n_bn)]
    for peer in dp_peers + bn_peers:
        pl.semaphore_signal(barrier, inc=1, device_id=peer, device_id_type=MESH)

    def push(phase, src, dst, peer):
        i = (PHASES + STEPS).index(phase)
        pltpu.make_async_remote_copy(
            src_ref=src, dst_ref=dst, send_sem=send_sem.at[i], recv_sem=recv_sem.at[i],
            device_id=peer, device_id_type=MESH,
        ).start()

    def arrived(phase, view):
        pltpu.make_async_copy(view, view, recv_sem.at[(PHASES + STEPS).index(phase)]).wait()

    def sent(phase, view):
        pltpu.make_async_copy(view, view, send_sem.at[(PHASES + STEPS).index(phase)]).wait()

    def most(ref):
        return ref.at[pl.ds(0, ref.shape[0] - 1)]

    def column_peers(phase, src, dst):
        for peer in dp_peers:
            push(phase, src, dst.at[d], peer)

    def exact(a, c):
        return jnp.dot(a, c, preferred_element_type=f32, precision=lax.Precision.HIGHEST)

    def dot(a, c):
        return jnp.dot(a, c, preferred_element_type=f32)

    for load in loads[:3]:
        load.wait()

    q = queries[...].astype(f32)
    query_unit = (q * lax.rsqrt(jnp.sum(q * q, axis=-1, keepdims=True) + EPS_UNIT)).astype(bf16)
    query_own[...] = query_unit
    query_all[d] = query_unit

    lane = lax.broadcasted_iota(jnp.int32, (slots, slots), 1)
    sub = lax.broadcasted_iota(jnp.int32, (slots, slots), 0)
    lane1 = lax.broadcasted_iota(jnp.int32, (1, slots), 1)
    lane_8 = lax.broadcasted_iota(jnp.int32, (8, LANES), 1)
    sub_8 = lax.broadcasted_iota(jnp.int32, (8, LANES), 0)
    slot_8 = lane_8 // cells
    mask_row = jnp.zeros((slots, slots), jnp.int32)
    mask_col = jnp.zeros((slots, slots), jnp.int32)
    want = jnp.zeros((1, slots), jnp.int32)
    mask_8 = jnp.zeros((8, LANES), jnp.int32)
    sources = []
    for s in range(slots):
        mask = masks[s]
        sources.append(mask ^ d)
        mask_row = jnp.where(lane == s, sources[s], mask_row)
        mask_col = jnp.where(sub == s, sources[s], mask_col)
        mask_8 = jnp.where(slot_8 == s, mask, mask_8)
        place = positive[s]
        slot = lax.rem(place, slots)
        column = lax.div(place, slots * n_bn) ^ masks[slot]
        want = jnp.where(lane1 == s, column * slots + slot, want)
    same = (mask_row == mask_col).astype(f32)
    local_mean = same / (jnp.sum(same, axis=0, keepdims=True) * float(cells))
    member = (mask_row[:n_dp] == sub[:n_dp]).astype(f32)
    counts = []
    for e in range(n_dp):
        count = jnp.int32(0)
        for s in range(slots):
            count = count + (sources[s] == e).astype(jnp.int32)
        counts.append((count * cells).astype(f32))

    bits = [(mask_8 & (1 << level)) != 0 for level in range(3)]
    kind = mask_8 & 3
    flags = jnp.where(sub_8 == 0, mask_8 & 1, jnp.where(sub_8 == 1, (mask_8 >> 1) & 1, (mask_8 >> 2) & 1))
    flags = jnp.where(sub_8 >= 3, (kind == sub_8 - 2).astype(jnp.int32), flags)
    before_r = lax.broadcasted_iota(jnp.int32, (rows, rows), 0)
    before_c = lax.broadcasted_iota(jnp.int32, (rows, rows), 1)
    earlier = jnp.logical_and(before_r % cells == 0, before_r // cells < before_c // cells)
    rank = dot(flags.astype(f32).astype(bf16), jnp.where(earlier, 1.0, 0.0).astype(bf16))
    places = jnp.where(flags != 0, rank * float(cells) + (lane_8 % cells + 1).astype(f32), 0.0)

    def every(i):
        return jnp.broadcast_to(places[i : i + 1], (8, LANES))

    to_level = [every(i) for i in range(3)]
    tag = (lane_8 + 1).astype(f32)

    def picks(count, codes):
        wanted = (lax.broadcasted_iota(jnp.int32, (count, codes.shape[1]), 0) + 1).astype(f32)
        return jnp.where(wanted == codes, 1.0, 0.0).astype(bf16)

    gather = [picks(half, places[i : i + 1]) for i in range(6)]

    def moved(table, which):
        stacked = jnp.zeros((8, LANES), f32)
        for i, line in enumerate(table):
            stacked = jnp.where(sub_8 == i, line, stacked)
        return lax.dot_general(
            stacked.astype(bf16), which, (((1,), (1,)), ((), ())), preferred_element_type=f32
        )

    low_lane = lax.broadcasted_iota(jnp.int32, (1, LANES), 1) < half

    def unless(flag, line):
        return jnp.where(flag, 0.0, line)

    by_order = {}
    for i, j, k in sorted(set(ORDERS.values())):
        table = [
            to_level[j], unless(bits[j], to_level[k]), to_level[k],
            unless(jnp.logical_or(bits[j], bits[k]), tag), unless(bits[k], tag),
        ]
        pair = moved(table, jnp.concatenate([gather[i], gather[j]], axis=0))
        second = jnp.concatenate([unless(bits[i], to_level[j])[:1], pair[0:1]], axis=1)
        third = jnp.concatenate(
            [
                unless(jnp.logical_or(bits[i], bits[j]), to_level[k])[:1],
                jnp.where(low_lane, pair[1:2], pair[2:3]),
            ],
            axis=1,
        )
        final = jnp.concatenate(
            [unless(mask_8 != 0, tag)[:1], jnp.where(low_lane, pair[3:4], pair[4:5])], axis=1
        )
        last = moved([tag], gather[k])[:1]
        by_order[i, j, k] = (gather[i], picks(half, second)[:, : rows + half], picks(half, third), picks(rows, final), picks(rows, last))
    table = [to_level[2], unless(bits[2], tag)]
    near = moved(table, jnp.concatenate(gather[3:5], axis=0))
    both = moved(table, gather[5])
    far_codes = jnp.concatenate([unless(kind != 0, to_level[2])[:1], near[0:1]], axis=1)
    stay_codes = jnp.concatenate([unless(mask_8 != 0, tag)[:1], near[1:2]], axis=1)
    far_pick = (picks(half, far_codes), picks(half, both[0:1]))
    stay_pick = (picks(rows, stay_codes), picks(rows, both[1:2]))
    routes = {name: by_order[order] for name, order in ORDERS.items()}
    last_pick = picks(rows, moved([tag], gather[2])[:1])

    sends = dict(zip(ORDERS, piece_refs[0::3]))
    pairs = dict(zip(ORDERS, piece_refs[1::3]))
    lasts = dict(zip(ORDERS, piece_refs[2::3]))
    columns = {name: slice(i * chunk, (i + 1) * chunk) for i, name in enumerate(ORDERS)}

    def stage(name, step):
        held = x_ref[:, columns[name]]
        if step:
            held = jnp.concatenate([held, pairs[name][: step * half]], axis=0)
        sends[name][step] = dot(routes[name][step], held).astype(bf16)

    def landing(name, step):
        return lasts[name] if step == 2 else pairs[name].at[pl.ds(step * half, half)]

    def ship(name, step):
        peer = (d ^ (1 << ORDERS[name][step]), b)
        push(name + str(step), sends[name].at[step], landing(name, step), peer)

    def forward(name, step):
        arrived(name + str(step - 1), landing(name, step - 1))
        stage(name, step)
        ship(name, step)

    def settle(name):
        held = jnp.concatenate([x_ref[:, columns[name]], pairs[name][...]], axis=0)
        feature_ref[:, columns[name]] = dot(routes[name][3], held)

    def to_rows(ref, at, values):
        for r in range(values.shape[1] // LANES):
            ref[at + r : at + r + 1, :] = values[:, r * LANES : (r + 1) * LANES]

    def to_line(ref, at, values):
        for r in range(values.shape[0]):
            ref[at : at + 1, r * LANES : (r + 1) * LANES] = values[r : r + 1]

    def group_peers(phase, own, every_part):
        every_part[b] = own[...]
        for peer in bn_peers:
            push(phase, own, every_part.at[b], peer)

    def group_stats(phase, every_part):
        arrived(phase, most(every_part))
        lines = every_part.shape[1] // 2
        parts = every_part[...]
        means = parts[:, :lines]
        mean = jnp.sum(means, axis=0) * (1.0 / n_bn)
        spread = jnp.sum(parts[:, lines:], axis=0) + float(rows) * jnp.sum(
            jnp.square(means - mean[None]), axis=0
        )
        return mean, lax.rsqrt(spread * (1.0 / total) + EPS_BN)

    def send_stats(phase, h, own, every_part):
        mean = jnp.sum(h, axis=0, keepdims=True) * (1.0 / rows)
        squares = jnp.sum(jnp.square(h - mean), axis=0, keepdims=True)
        to_rows(own, 0, mean)
        to_rows(own, own.shape[0] // 2, squares)
        group_peers(phase, own, every_part)

    ones = jnp.ones((LANES, LANES), bf16)
    step_rows = queue_ref.shape[0] // QUEUE_STEPS

    def queue_step(c, total_part):
        raw = queue_ref[pl.ds(c * step_rows, step_rows), :].astype(f32)
        square = raw * raw
        high = square.astype(bf16)
        low = (square - high.astype(f32)).astype(bf16)
        norm = dot(high, ones) + dot(low, ones)
        unit = (raw * lax.rsqrt(norm + EPS_UNIT)).astype(bf16)
        flat_queries = query_all[...].reshape(n_dp * slots, query_all.shape[2])
        scores = lax.dot_general(unit, flat_queries, (((1,), (1,)), ((), ())), preferred_element_type=f32)
        terms = jnp.exp(scores * INV_TEMP - INV_TEMP)
        return total_part + jnp.sum(terms.reshape(step_rows // 8, 8, n_dp * slots), axis=0)

    def queue_steps(first, last, total_part):
        return lax.fori_loop(first, last, queue_step, total_part)

    loads[3].wait()
    first = None
    for i in range(PANELS):
        panels[i].wait()
        at = slice(i * panel, (i + 1) * panel)
        term = dot(x_ref[:, at], in_ref[at])
        first = term if first is None else first + term
        if i == 0:
            for load in loads[4:]:
                load.start()
    shaped = first.reshape(slots, cells, middle)
    sums = jnp.sum(shaped, axis=1)
    center = exact(local_mean, sums)
    offset = shaped - center[:, None, :]
    squares = jnp.sum(jnp.square(offset), axis=1)
    dev_ref[...] = offset.reshape(rows, middle).astype(bf16)
    for side, at in enumerate(sides):
        for c in range(3):
            class_send[side, c * half : (c + 1) * half] = dot(gather[3 + c], dev_ref[:, at]).astype(bf16)
    lines = middle // LANES
    for at, values in ((0, exact(member, sums)), (lines, exact(member, squares))):
        for g in range(n_dp):
            for r in range(lines):
                sum_send[g, at + r : at + r + 1, :] = values[g : g + 1, r * LANES : (r + 1) * LANES]
    sum_recv[d] = sum_send[d]

    pl.semaphore_wait(barrier, n_dp + n_bn - 2)
    column_peers("query", query_own, query_all)
    for side in range(2):
        for c in range(3):
            at = pl.ds(c * half, half)
            push("class" + str(side), class_send.at[side, at], class_recv.at[side, at], (d ^ (c + 1), b))
    for k in range(1, n_dp):
        push("sum1", sum_send.at[d ^ k], sum_recv.at[d], (d ^ k, b))
    stage("c", 0)
    ship("c", 0)
    stage("a", 0)
    ship("a", 0)
    stage("d", 0)
    ship("d", 0)
    stage("b", 0)
    ship("b", 0)

    part = jnp.zeros((8, n_dp * slots), f32)
    loads[4].wait()

    arrived("sum1", most(sum_recv))
    parts = sum_recv[...]
    class_sums = parts[:, :lines]
    column_mean = jnp.sum(class_sums, axis=0) * (1.0 / rows)
    column_squares = jnp.sum(parts[:, lines:], axis=0)
    class_means = []
    for e in range(n_dp):
        class_means.append(class_sums[e] / jnp.maximum(counts[e], 1.0))
        column_squares = column_squares + counts[e] * jnp.square(class_means[e] - column_mean)
    own1[:lines] = column_mean
    own1[lines:] = column_squares
    group_peers("bn1", own1, all1)

    for side, at in enumerate(sides):
        arrived("class" + str(side), class_recv.at[side])
        near_held = jnp.concatenate([dev_ref[:, at], class_recv[side, :rows]], axis=0)
        far_send[side] = (dot(far_pick[0], near_held) + dot(far_pick[1], class_recv[side, rows:])).astype(bf16)
        push("far" + str(side), far_send.at[side], far_recv.at[side], (d ^ 4, b))
    for side, at in enumerate(sides):
        near_held = jnp.concatenate([dev_ref[:, at], class_recv[side, :rows]], axis=0)
        h_ref[:, at] = dot(stay_pick[0], near_held) + dot(stay_pick[1], class_recv[side, rows:])
    arrived("query", most(query_all))
    forward("c", 1)
    part = queue_steps(0, 1, part)
    forward("a", 1)
    forward("d", 1)
    forward("b", 1)
    mean, scale = group_stats("bn1", all1)
    for e in range(n_dp):
        to_line(class_ref, e, class_means[e] - mean)
    to_line(scale_ref, 0, scale)
    loads[5].wait()

    for side, at in enumerate(sides):
        arrived("far" + str(side), far_recv.at[side])
        h_ref[:, at] = h_ref[:, at] + dot(last_pick, far_recv[side])
    for s in range(slots):
        at = slice(s * cells, (s + 1) * cells)
        move = jnp.broadcast_to(class_ref[pl.ds(sources[s], 1), :], (cells, middle))
        h_ref[at] = jax.nn.relu((h_ref[at] + move) * scale_ref[0:1, :middle])
    act = h_ref[...]
    cell = lax.broadcasted_iota(jnp.int32, act.shape, 0) % cells
    before = jnp.where(cell == 0, 0.0, pltpu.roll(act, 1, 0)).astype(bf16)
    after = jnp.where(cell == cells - 1, 0.0, pltpu.roll(act, rows - 1, 0)).astype(bf16)
    h_ref[...] = dot(before, mid_ref[0]) + dot(act.astype(bf16), mid_ref[1]) + dot(after, mid_ref[2])
    send_stats("bn2", h_ref[...], own2, all2)
    forward("c", 2)
    forward("a", 2)
    part = queue_steps(1, 3, part)
    forward("d", 2)
    forward("b", 2)
    loads[6].wait()
    mean, scale = group_stats("bn2", all2)
    to_line(mean_ref, 0, mean)
    to_line(scale_ref, 0, scale)

    second = jax.nn.relu((h_ref[...] - mean_ref[0:1, :middle]) * scale_ref[0:1, :middle]).astype(bf16)
    wide_ref[...] = dot(second, out_ref[...])
    send_stats("bn3", wide_ref[...], own3, all3)
    part = queue_steps(3, 8, part)
    part_own[...] = jnp.sum(part, axis=0, keepdims=True)
    part_all[d] = part_own[...]
    column_peers("queue", part_own, part_all)
    for name in ORDERS:
        settle(name)
    loads[7].wait()
    mean, scale = group_stats("bn3", all3)
    to_line(mean_ref, 0, mean)
    to_line(scale_ref, 0, scale)

    z = None
    for name in "acbd":
        at = columns[name]
        normal = (wide_ref[:, at] - mean_ref[0:1, at]) * scale_ref[0:1, at]
        arrived(name + "2", lasts[name])
        feature = feature_ref[:, at] + dot(routes[name][4], lasts[name][...])
        block = jax.nn.relu(normal + feature).astype(bf16)
        pooled = jnp.mean(block.astype(f32).reshape(slots, cells, chunk), axis=1).astype(bf16)
        term = dot(pooled, head_ref[at])
        z = term if z is None else z + term
    key_own[...] = (z * lax.rsqrt(jnp.sum(z * z, axis=-1, keepdims=True) + EPS_UNIT)).astype(bf16)
    key_all[d] = key_own[...]
    column_peers("key", key_own, key_all)

    arrived("queue", most(part_all))
    negative_all = jnp.sum(part_all[...], axis=0)
    mine = lax.broadcasted_iota(jnp.int32, (slots, n_dp * slots), 1) == (
        lax.broadcasted_iota(jnp.int32, (slots, n_dp * slots), 0) + d * slots
    )
    negative_col = jnp.sum(jnp.where(mine, negative_all, 0.0), axis=1, keepdims=True)
    negative = jnp.sum(jnp.where(lane == sub, negative_col, 0.0), axis=0, keepdims=True)

    arrived("key", most(key_all))
    keys = key_all[...].reshape(n_dp * slots, key_all.shape[2])
    products = lax.dot_general(keys, query_own[...], (((1,), (1,)), ((), ())), preferred_element_type=f32)
    chosen = lax.broadcasted_iota(jnp.int32, products.shape, 0) == want
    logit = jnp.sum(jnp.where(chosen, products, 0.0), axis=0, keepdims=True) * INV_TEMP
    loss_ref[...] = jnp.log(jnp.exp(logit - INV_TEMP) + negative) + INV_TEMP - logit

    for phase, every_part in (("query", query_all), ("queue", part_all), ("key", key_all), ("sum1", sum_recv), ("bn1", all1), ("bn2", all2), ("bn3", all3)):
        sent(phase, most(every_part))
    for side in range(2):
        sent("class" + str(side), class_send.at[side])
        sent("far" + str(side), far_send.at[side])
    for name in ORDERS:
        for step in range(3):
            sent(name + str(step), sends[name].at[step])


def on_device_shuffled(n_dp, n_bn, features, shuffle_masks, conv_in, conv_mid, conv_out, head, queries, queue, positive):
    f32, bf16 = jnp.float32, jnp.bfloat16
    slots, cells, channels = features.shape
    rows = slots * cells
    middle = conv_in.shape[1]
    width = queries.shape[1]

    def group_parts(c):
        tile = (2 * (c // LANES), LANES)
        return [pltpu.VMEM(tile, f32), pltpu.VMEM((n_bn,) + tile, f32)]

    chunk = channels // len(ORDERS)
    feature_parts = [
        pltpu.VMEM((3, rows // 2, chunk), bf16),
        pltpu.VMEM((rows, chunk), bf16),
        pltpu.VMEM((rows // 2, chunk), bf16),
    ]
    sums = pltpu.VMEM((n_dp, 2 * (middle // LANES), LANES), f32)
    hbm = pl.BlockSpec(memory_space=pltpu.HBM)
    loss = pl.pallas_call(
        functools.partial(shuffled_kernel, n_dp, n_bn),
        out_shape=jax.ShapeDtypeStruct((1, slots), f32),
        in_specs=[hbm] * 9,
        out_specs=pl.BlockSpec(memory_space=pltpu.VMEM),
        scratch_shapes=[
            pltpu.SMEM(shuffle_masks.shape, jnp.int32),
            pltpu.SMEM(positive.shape, jnp.int32),
            pltpu.VMEM(queries.shape, bf16),
            pltpu.VMEM((rows, channels), bf16),
            pltpu.VMEM(conv_in.shape, bf16),
            pltpu.VMEM(conv_mid.shape, bf16),
            pltpu.VMEM(conv_out.shape, bf16),
            pltpu.VMEM(head.shape, bf16),
            pltpu.VMEM(queue.shape, bf16),
            pltpu.VMEM((rows, middle), f32),
            pltpu.VMEM((rows, channels), f32),
            pltpu.VMEM((n_dp, middle), f32),
            pltpu.VMEM((8, channels), f32),
            pltpu.VMEM((8, channels), f32),
            pltpu.VMEM((rows, middle), bf16),
            pltpu.VMEM((2, 3 * rows // 2, middle // 2), bf16),
            pltpu.VMEM((2, 3 * rows // 2, middle // 2), bf16),
            pltpu.VMEM((2, rows // 2, middle // 2), bf16),
            pltpu.VMEM((2, rows // 2, middle // 2), bf16),
        ]
        + [pltpu.VMEM((rows, channels), f32), sums, sums]
        + group_parts(middle)
        + group_parts(middle)
        + group_parts(channels)
        + [
            pltpu.VMEM((slots, width), bf16),
            pltpu.VMEM((n_dp, slots, width), bf16),
            pltpu.VMEM((1, n_dp * slots), f32),
            pltpu.VMEM((n_dp, 1, n_dp * slots), f32),
            pltpu.VMEM((slots, width), bf16),
            pltpu.VMEM((n_dp, slots, width), bf16),
            pltpu.SemaphoreType.DMA((8,)),
            pltpu.SemaphoreType.DMA((PANELS,)),
            pltpu.SemaphoreType.DMA((len(PHASES + STEPS),)),
            pltpu.SemaphoreType.DMA((len(PHASES + STEPS),)),
        ]
        + feature_parts * len(ORDERS),
        compiler_params=pltpu.CompilerParams(
            collective_id=0, has_side_effects=True, vmem_limit_bytes=64 << 20
        ),
        name="shuffled_crops",
    )(shuffle_masks, positive, queries, features.reshape(rows, channels), conv_in, conv_mid, conv_out, head, queue)
    return loss.reshape(slots)


def on_device(n_dp, n_bn, *arrays):
    features, conv_in = arrays[0], arrays[2]
    slots, cells, channels = features.shape
    whole_lanes = conv_in.shape[1] % (2 * LANES) == 0 and channels % (4 * LANES) == 0
    if whole_lanes and n_dp == 8 and slots * cells == LANES and cells == 8 and n_bn <= 4:
        return on_device_shuffled(n_dp, n_bn, *arrays)
    return on_device_moving(*arrays)


def solution(mesh):
    return jax.shard_map(
        functools.partial(on_device, mesh.shape["dp"], mesh.shape["bn"]),
        mesh=mesh,
        in_specs=(
            P(("dp", "bn"), None, None),
            P(),
            P(),
            P(),
            P(),
            P(),
            P(("dp", "bn"), None),
            P("dp", None),
            P(("dp", "bn")),
        ),
        out_specs=P(("dp", "bn")),
        check_vma=False,
    )
```

```python
import functools

import jax
import jax.numpy as jnp
from jax import lax
from jax.experimental import pallas as pl
from jax.experimental.pallas import tpu as pltpu
from jax.sharding import PartitionSpec as P

EPS_BN = 1e-05
EPS_UNIT = 1e-06
INV_TEMP = 1.0 / 0.07


def partner_2(value, axis, distance):
    return lax.ppermute(value, axis, [(i, i ^ 1 << distance) for i in range(lax.axis_size(axis))])


def unit_rows(values):
    values = values.astype(jnp.float32)
    return values * lax.rsqrt(jnp.sum(values * values, axis=-1, keepdims=True) + EPS_UNIT)


def group_norm(values, row_total):
    first = lax.psum(jnp.sum(values, axis=0), "bn")
    center = first / row_total
    spread = lax.psum(jnp.sum(jnp.square(values - center), axis=0), "bn") / row_total
    return (values - center) * lax.rsqrt(spread + EPS_BN)


def moving_slots(shuffle_masks, level, half):
    flags = jnp.bitwise_and(jnp.right_shift(shuffle_masks, level), 1)
    return jnp.argsort(1 - flags, stable=True)[:half]


def on_device_moving(features, shuffle_masks, conv_in, conv_mid, conv_out, head, queries, queue, positive):
    dp_count = lax.axis_size("dp")
    bn_count = lax.axis_size("bn")
    bit_count = dp_count.bit_length() - 1
    crop_dev, positions, channels = features.shape
    half = crop_dev // 2
    middle = conv_in.shape[1]
    query_unit = unit_rows(queries).astype(jnp.bfloat16)
    query_all = lax.all_gather(query_unit, "dp", axis=0, tiled=True)
    shuffled = features
    for level in range(bit_count):
        moving = moving_slots(shuffle_masks, level, half)
        chosen = (moving[:, None] == jnp.arange(crop_dev)[None, :]).astype(jnp.bfloat16)
        leaving = jnp.dot(
            chosen, shuffled.reshape(crop_dev, positions * channels), preferred_element_type=jnp.float32
        ).astype(jnp.bfloat16)
        partner = partner_2(leaving.reshape(half, positions, channels), "dp", level)
        shuffled = shuffled.at[moving].set(partner)
    row_total = crop_dev * positions * bn_count
    flat_rows = shuffled.reshape(crop_dev * positions, channels)
    first_sum = jnp.dot(flat_rows, conv_in, preferred_element_type=jnp.float32)
    first_act = jax.nn.relu(group_norm(first_sum, row_total)).astype(jnp.bfloat16)
    tap_maps = first_act.reshape(crop_dev, positions, middle)
    padded = jnp.pad(tap_maps, ((0, 0), (1, 1), (0, 0)))
    stacked = jnp.concatenate([padded[:, tap : tap + positions, :] for tap in range(3)], axis=2)
    second_sum = jnp.dot(
        stacked.reshape(crop_dev * positions, 3 * middle),
        conv_mid.reshape(3 * middle, middle),
        preferred_element_type=jnp.float32,
    )
    second_act = jax.nn.relu(group_norm(second_sum, row_total)).astype(jnp.bfloat16)
    third_sum = jnp.dot(second_act, conv_out, preferred_element_type=jnp.float32)
    block = jax.nn.relu(group_norm(third_sum, row_total) + flat_rows.astype(jnp.float32)).astype(
        jnp.bfloat16
    )
    pooled = jnp.mean(
        block.reshape(crop_dev, positions, channels).astype(jnp.float32), axis=1
    ).astype(jnp.bfloat16)
    key_unit = unit_rows(jnp.dot(pooled, head, preferred_element_type=jnp.float32)).astype(
        jnp.bfloat16
    )
    for level in range(bit_count):
        moving = moving_slots(shuffle_masks, level, half)
        partner = partner_2(jnp.take(key_unit, moving, axis=0), "dp", level)
        key_unit = key_unit.at[moving].set(partner)
    queue_unit = unit_rows(queue).astype(jnp.bfloat16)
    scores = jnp.dot(query_all, queue_unit.T, preferred_element_type=jnp.float32) * INV_TEMP
    queue_part = jnp.sum(jnp.exp(scores - INV_TEMP), axis=1)
    key_all = lax.all_gather(key_unit, "dp", axis=0, tiled=True)
    slot_of = positive % crop_dev
    column = positive // crop_dev // bn_count
    picked = jnp.take(key_all, column * crop_dev + slot_of, axis=0)
    positive_logit = (
        jnp.sum(query_unit.astype(jnp.float32) * picked.astype(jnp.float32), axis=-1) * INV_TEMP
    )
    negative = lax.psum_scatter(queue_part, "dp", scatter_dimension=0, tiled=True)
    return jnp.log(jnp.exp(positive_logit - INV_TEMP) + negative) + INV_TEMP - positive_logit


MESH = pl.DeviceIdType.MESH
LANES = 128
QUEUE_STEPS = 8
PANELS = 2
PHASES = (
    "query", "queue", "key", "sum1", "bn1", "bn2", "bn3", "class0", "class1", "far0", "far1",
)
ORDERS = {'a': (2, 0, 1), 'b': (2, 0, 1), 'c': (0, 1, 2), 'd': (0, 1, 2)}
STEPS = tuple(name + str(step) for name in ORDERS for step in range(3))


def shuffled_kernel(
    n_dp, n_bn,
    masks_hbm, positive_hbm, queries_hbm, x_hbm, in_hbm, mid_hbm, out_hbm, head_hbm, queue_hbm,
    loss_ref,
    masks, positive, queries,
    x_ref, in_ref, mid_ref, out_ref, head_ref, queue_ref,
    h_ref, wide_ref, class_ref, mean_ref, scale_ref,
    dev_ref, class_send, class_recv, far_send, far_recv,
    feature_ref,
    sum_send, sum_recv, own1, all1, own2, all2, own3, all3,
    query_own, query_all, part_own, part_all, key_own, key_all,
    load_sem, panel_sem, send_sem, recv_sem,
    *piece_refs,
):
    f32, bf16 = jnp.float32, jnp.bfloat16
    d = lax.axis_index("dp")
    b = lax.axis_index("bn")
    rows, channels = x_ref.shape
    slots = masks.shape[0]
    cells = rows // slots
    half = rows // 2
    middle = in_ref.shape[1]
    chunk = channels // len(ORDERS)
    total = float(rows * n_bn)
    sides = [slice(0, middle // 2), slice(middle // 2, middle)]

    panel = channels // PANELS
    panels = [
        pltpu.make_async_copy(
            in_hbm.at[pl.ds(i * panel, panel)], in_ref.at[pl.ds(i * panel, panel)], panel_sem.at[i]
        )
        for i in range(PANELS)
    ]
    loads = [
        pltpu.make_async_copy(src, dst, load_sem.at[i])
        for i, (src, dst) in enumerate(
            [(masks_hbm, masks), (positive_hbm, positive), (queries_hbm, queries), (x_hbm, x_ref), (queue_hbm, queue_ref), (mid_hbm, mid_ref), (out_hbm, out_ref), (head_hbm, head_ref)]
        )
    ]
    for load in loads[:4] + panels:
        load.start()

    barrier = pltpu.get_barrier_semaphore()
    dp_peers = [(d ^ k, b) for k in reversed(range(1, n_dp))]
    bn_peers = [(d, lax.rem(b + k, n_bn)) for k in range(1, n_bn)]
    for peer in dp_peers + bn_peers:
        pl.semaphore_signal(barrier, inc=1, device_id=peer, device_id_type=MESH)

    def push(phase, src, dst, peer):
        i = (PHASES + STEPS).index(phase)
        pltpu.make_async_remote_copy(
            src_ref=src, dst_ref=dst, send_sem=send_sem.at[i], recv_sem=recv_sem.at[i],
            device_id=peer, device_id_type=MESH,
        ).start()

    def arrived(phase, view):
        pltpu.make_async_copy(view, view, recv_sem.at[(PHASES + STEPS).index(phase)]).wait()

    def sent(phase, view):
        pltpu.make_async_copy(view, view, send_sem.at[(PHASES + STEPS).index(phase)]).wait()

    def most(ref):
        return ref.at[pl.ds(0, ref.shape[0] - 1)]

    def column_peers(phase, src, dst):
        for peer in dp_peers:
            push(phase, src, dst.at[d], peer)

    def exact(a, c):
        return jnp.dot(a, c, preferred_element_type=f32, precision=lax.Precision.HIGHEST)

    def dot(a, c):
        return jnp.dot(a, c, preferred_element_type=f32)

    for load in loads[:3]:
        load.wait()

    q = queries[...].astype(f32)
    query_unit = (q * lax.rsqrt(jnp.sum(q * q, axis=-1, keepdims=True) + EPS_UNIT)).astype(bf16)
    query_own[...] = query_unit
    query_all[d] = query_unit

    lane = lax.broadcasted_iota(jnp.int32, (slots, slots), 1)
    sub = lax.broadcasted_iota(jnp.int32, (slots, slots), 0)
    lane1 = lax.broadcasted_iota(jnp.int32, (1, slots), 1)
    lane_8 = lax.broadcasted_iota(jnp.int32, (8, LANES), 1)
    sub_8 = lax.broadcasted_iota(jnp.int32, (8, LANES), 0)
    slot_8 = lane_8 // cells
    mask_row = jnp.zeros((slots, slots), jnp.int32)
    mask_col = jnp.zeros((slots, slots), jnp.int32)
    want = jnp.zeros((1, slots), jnp.int32)
    mask_8 = jnp.zeros((8, LANES), jnp.int32)
    sources = []
    for s in range(slots):
        mask = masks[s]
        sources.append(mask ^ d)
        mask_row = jnp.where(lane == s, sources[s], mask_row)
        mask_col = jnp.where(sub == s, sources[s], mask_col)
        mask_8 = jnp.where(slot_8 == s, mask, mask_8)
        place = positive[s]
        slot = lax.rem(place, slots)
        column = lax.div(place, slots * n_bn) ^ masks[slot]
        want = jnp.where(lane1 == s, column * slots + slot, want)
    same = (mask_row == mask_col).astype(f32)
    local_mean = same / (jnp.sum(same, axis=0, keepdims=True) * float(cells))
    member = (mask_row[:n_dp] == sub[:n_dp]).astype(f32)
    counts = []
    for e in range(n_dp):
        count = jnp.int32(0)
        for s in range(slots):
            count = count + (sources[s] == e).astype(jnp.int32)
        counts.append((count * cells).astype(f32))

    bits = [(mask_8 & (1 << level)) != 0 for level in range(3)]
    kind = mask_8 & 3
    flags = jnp.where(sub_8 == 0, mask_8 & 1, jnp.where(sub_8 == 1, (mask_8 >> 1) & 1, (mask_8 >> 2) & 1))
    flags = jnp.where(sub_8 >= 3, (kind == sub_8 - 2).astype(jnp.int32), flags)
    before_r = lax.broadcasted_iota(jnp.int32, (rows, rows), 0)
    before_c = lax.broadcasted_iota(jnp.int32, (rows, rows), 1)
    earlier = jnp.logical_and(before_r % cells == 0, before_r // cells < before_c // cells)
    rank = dot(flags.astype(f32).astype(bf16), jnp.where(earlier, 1.0, 0.0).astype(bf16))
    places = jnp.where(flags != 0, rank * float(cells) + (lane_8 % cells + 1).astype(f32), 0.0)

    def every(i):
        return jnp.broadcast_to(places[i : i + 1], (8, LANES))

    to_level = [every(i) for i in range(3)]
    tag = (lane_8 + 1).astype(f32)

    def picks(count, codes):
        wanted = (lax.broadcasted_iota(jnp.int32, (count, codes.shape[1]), 0) + 1).astype(f32)
        return jnp.where(wanted == codes, 1.0, 0.0).astype(bf16)

    gather = [picks(half, places[i : i + 1]) for i in range(6)]

    def moved(table, which):
        stacked = jnp.zeros((8, LANES), f32)
        for i, line in enumerate(table):
            stacked = jnp.where(sub_8 == i, line, stacked)
        return lax.dot_general(
            stacked.astype(bf16), which, (((1,), (1,)), ((), ())), preferred_element_type=f32
        )

    low_lane = lax.broadcasted_iota(jnp.int32, (1, LANES), 1) < half

    def unless(flag, line):
        return jnp.where(flag, 0.0, line)

    by_order = {}
    for i, j, k in sorted(set(ORDERS.values())):
        table = [
            to_level[j], unless(bits[j], to_level[k]), to_level[k],
            unless(jnp.logical_or(bits[j], bits[k]), tag), unless(bits[k], tag),
        ]
        pair = moved(table, jnp.concatenate([gather[i], gather[j]], axis=0))
        second = jnp.concatenate([unless(bits[i], to_level[j])[:1], pair[0:1]], axis=1)
        third = jnp.concatenate(
            [
                unless(jnp.logical_or(bits[i], bits[j]), to_level[k])[:1],
                jnp.where(low_lane, pair[1:2], pair[2:3]),
            ],
            axis=1,
        )
        final = jnp.concatenate(
            [unless(mask_8 != 0, tag)[:1], jnp.where(low_lane, pair[3:4], pair[4:5])], axis=1
        )
        last = moved([tag], gather[k])[:1]
        by_order[i, j, k] = (gather[i], picks(half, second)[:, : rows + half], picks(half, third), picks(rows, final), picks(rows, last))
    table = [to_level[2], unless(bits[2], tag)]
    near = moved(table, jnp.concatenate(gather[3:5], axis=0))
    both = moved(table, gather[5])
    far_codes = jnp.concatenate([unless(kind != 0, to_level[2])[:1], near[0:1]], axis=1)
    stay_codes = jnp.concatenate([unless(mask_8 != 0, tag)[:1], near[1:2]], axis=1)
    far_pick = (picks(half, far_codes), picks(half, both[0:1]))
    stay_pick = (picks(rows, stay_codes), picks(rows, both[1:2]))
    routes = {name: by_order[order] for name, order in ORDERS.items()}
    last_pick = picks(rows, moved([tag], gather[2])[:1])

    sends = dict(zip(ORDERS, piece_refs[0::3]))
    pairs = dict(zip(ORDERS, piece_refs[1::3]))
    lasts = dict(zip(ORDERS, piece_refs[2::3]))
    columns = {name: slice(i * chunk, (i + 1) * chunk) for i, name in enumerate(ORDERS)}

    def stage(name, step):
        held = x_ref[:, columns[name]]
        if step:
            held = jnp.concatenate([held, pairs[name][: step * half]], axis=0)
        sends[name][step] = dot(routes[name][step], held).astype(bf16)

    def landing(name, step):
        return lasts[name] if step == 2 else pairs[name].at[pl.ds(step * half, half)]

    def ship(name, step):
        peer = (d ^ (1 << ORDERS[name][step]), b)
        push(name + str(step), sends[name].at[step], landing(name, step), peer)

    def forward(name, step):
        arrived(name + str(step - 1), landing(name, step - 1))
        stage(name, step)
        ship(name, step)

    def settle(name):
        held = jnp.concatenate([x_ref[:, columns[name]], pairs[name][...]], axis=0)
        feature_ref[:, columns[name]] = dot(routes[name][3], held)

    def to_rows(ref, at, values):
        for r in range(values.shape[1] // LANES):
            ref[at + r : at + r + 1, :] = values[:, r * LANES : (r + 1) * LANES]

    def to_line(ref, at, values):
        for r in range(values.shape[0]):
            ref[at : at + 1, r * LANES : (r + 1) * LANES] = values[r : r + 1]

    def group_peers(phase, own, every_part):
        every_part[b] = own[...]
        for peer in bn_peers:
            push(phase, own, every_part.at[b], peer)

    def group_stats(phase, every_part):
        arrived(phase, most(every_part))
        lines = every_part.shape[1] // 2
        parts = every_part[...]
        means = parts[:, :lines]
        mean = jnp.sum(means, axis=0) * (1.0 / n_bn)
        spread = jnp.sum(parts[:, lines:], axis=0) + float(rows) * jnp.sum(
            jnp.square(means - mean[None]), axis=0
        )
        return mean, lax.rsqrt(spread * (1.0 / total) + EPS_BN)

    def send_stats(phase, h, own, every_part):
        mean = jnp.sum(h, axis=0, keepdims=True) * (1.0 / rows)
        squares = jnp.sum(jnp.square(h - mean), axis=0, keepdims=True)
        to_rows(own, 0, mean)
        to_rows(own, own.shape[0] // 2, squares)
        group_peers(phase, own, every_part)

    ones = jnp.ones((LANES, LANES), bf16)
    step_rows = queue_ref.shape[0] // QUEUE_STEPS

    def queue_step(c, total_part):
        raw = queue_ref[pl.ds(c * step_rows, step_rows), :].astype(f32)
        square = raw * raw
        high = square.astype(bf16)
        low = (square - high.astype(f32)).astype(bf16)
        norm = dot(high, ones) + dot(low, ones)
        unit = (raw * lax.rsqrt(norm + EPS_UNIT)).astype(bf16)
        flat_queries = query_all[...].reshape(n_dp * slots, query_all.shape[2])
        scores = lax.dot_general(unit, flat_queries, (((1,), (1,)), ((), ())), preferred_element_type=f32)
        terms = jnp.exp(scores * INV_TEMP - INV_TEMP)
        return total_part + jnp.sum(terms.reshape(step_rows // 8, 8, n_dp * slots), axis=0)

    def queue_steps(first, last, total_part):
        return lax.fori_loop(first, last, queue_step, total_part)

    loads[3].wait()
    first = None
    for i in range(PANELS):
        panels[i].wait()
        at = slice(i * panel, (i + 1) * panel)
        term = dot(x_ref[:, at], in_ref[at])
        first = term if first is None else first + term
        if i == 0:
            for load in loads[4:]:
                load.start()
    shaped = first.reshape(slots, cells, middle)
    sums = jnp.sum(shaped, axis=1)
    center = exact(local_mean, sums)
    offset = shaped - center[:, None, :]
    squares = jnp.sum(jnp.square(offset), axis=1)
    dev_ref[...] = offset.reshape(rows, middle).astype(bf16)
    for side, at in enumerate(sides):
        for c in range(3):
            class_send[side, c * half : (c + 1) * half] = dot(gather[3 + c], dev_ref[:, at]).astype(bf16)
    lines = middle // LANES
    for at, values in ((0, exact(member, sums)), (lines, exact(member, squares))):
        for g in range(n_dp):
            for r in range(lines):
                sum_send[g, at + r : at + r + 1, :] = values[g : g + 1, r * LANES : (r + 1) * LANES]
    sum_recv[d] = sum_send[d]

    pl.semaphore_wait(barrier, n_dp + n_bn - 2)
    column_peers("query", query_own, query_all)
    for side in range(2):
        for c in range(3):
            at = pl.ds(c * half, half)
            push("class" + str(side), class_send.at[side, at], class_recv.at[side, at], (d ^ (c + 1), b))
    for k in range(1, n_dp):
        push("sum1", sum_send.at[d ^ k], sum_recv.at[d], (d ^ k, b))
    stage("a", 0)
    ship("a", 0)
    stage("c", 0)
    ship("c", 0)
    stage("b", 0)
    ship("b", 0)
    stage("d", 0)
    ship("d", 0)

    part = jnp.zeros((8, n_dp * slots), f32)
    loads[4].wait()

    arrived("sum1", most(sum_recv))
    parts = sum_recv[...]
    class_sums = parts[:, :lines]
    column_mean = jnp.sum(class_sums, axis=0) * (1.0 / rows)
    column_squares = jnp.sum(parts[:, lines:], axis=0)
    class_means = []
    for e in range(n_dp):
        class_means.append(class_sums[e] / jnp.maximum(counts[e], 1.0))
        column_squares = column_squares + counts[e] * jnp.square(class_means[e] - column_mean)
    own1[:lines] = column_mean
    own1[lines:] = column_squares
    group_peers("bn1", own1, all1)

    for side, at in enumerate(sides):
        arrived("class" + str(side), class_recv.at[side])
        near_held = jnp.concatenate([dev_ref[:, at], class_recv[side, :rows]], axis=0)
        far_send[side] = (dot(far_pick[0], near_held) + dot(far_pick[1], class_recv[side, rows:])).astype(bf16)
        push("far" + str(side), far_send.at[side], far_recv.at[side], (d ^ 4, b))
    for side, at in enumerate(sides):
        near_held = jnp.concatenate([dev_ref[:, at], class_recv[side, :rows]], axis=0)
        h_ref[:, at] = dot(stay_pick[0], near_held) + dot(stay_pick[1], class_recv[side, rows:])
    arrived("query", most(query_all))
    forward("c", 1)
    forward("a", 1)
    part = queue_steps(0, 1, part)
    forward("d", 1)
    forward("b", 1)
    mean, scale = group_stats("bn1", all1)
    for e in range(n_dp):
        to_line(class_ref, e, class_means[e] - mean)
    to_line(scale_ref, 0, scale)
    loads[5].wait()

    for side, at in enumerate(sides):
        arrived("far" + str(side), far_recv.at[side])
        h_ref[:, at] = h_ref[:, at] + dot(last_pick, far_recv[side])
    for s in range(slots):
        at = slice(s * cells, (s + 1) * cells)
        move = jnp.broadcast_to(class_ref[pl.ds(sources[s], 1), :], (cells, middle))
        h_ref[at] = jax.nn.relu((h_ref[at] + move) * scale_ref[0:1, :middle])
    act = h_ref[...]
    cell = lax.broadcasted_iota(jnp.int32, act.shape, 0) % cells
    before = jnp.where(cell == 0, 0.0, pltpu.roll(act, 1, 0)).astype(bf16)
    after = jnp.where(cell == cells - 1, 0.0, pltpu.roll(act, rows - 1, 0)).astype(bf16)
    h_ref[...] = dot(before, mid_ref[0]) + dot(act.astype(bf16), mid_ref[1]) + dot(after, mid_ref[2])
    send_stats("bn2", h_ref[...], own2, all2)
    forward("c", 2)
    forward("a", 2)
    part = queue_steps(1, 3, part)
    forward("d", 2)
    forward("b", 2)
    loads[6].wait()
    mean, scale = group_stats("bn2", all2)
    to_line(mean_ref, 0, mean)
    to_line(scale_ref, 0, scale)

    second = jax.nn.relu((h_ref[...] - mean_ref[0:1, :middle]) * scale_ref[0:1, :middle]).astype(bf16)
    wide_ref[...] = dot(second, out_ref[...])
    send_stats("bn3", wide_ref[...], own3, all3)
    part = queue_steps(3, 8, part)
    part_own[...] = jnp.sum(part, axis=0, keepdims=True)
    part_all[d] = part_own[...]
    column_peers("queue", part_own, part_all)
    for name in ORDERS:
        settle(name)
    loads[7].wait()
    mean, scale = group_stats("bn3", all3)
    to_line(mean_ref, 0, mean)
    to_line(scale_ref, 0, scale)

    z = None
    for name in "acbd":
        at = columns[name]
        normal = (wide_ref[:, at] - mean_ref[0:1, at]) * scale_ref[0:1, at]
        arrived(name + "2", lasts[name])
        feature = feature_ref[:, at] + dot(routes[name][4], lasts[name][...])
        block = jax.nn.relu(normal + feature).astype(bf16)
        pooled = jnp.mean(block.astype(f32).reshape(slots, cells, chunk), axis=1).astype(bf16)
        term = dot(pooled, head_ref[at])
        z = term if z is None else z + term
    key_own[...] = (z * lax.rsqrt(jnp.sum(z * z, axis=-1, keepdims=True) + EPS_UNIT)).astype(bf16)
    key_all[d] = key_own[...]
    column_peers("key", key_own, key_all)

    arrived("queue", most(part_all))
    negative_all = jnp.sum(part_all[...], axis=0)
    mine = lax.broadcasted_iota(jnp.int32, (slots, n_dp * slots), 1) == (
        lax.broadcasted_iota(jnp.int32, (slots, n_dp * slots), 0) + d * slots
    )
    negative_col = jnp.sum(jnp.where(mine, negative_all, 0.0), axis=1, keepdims=True)
    negative = jnp.sum(jnp.where(lane == sub, negative_col, 0.0), axis=0, keepdims=True)

    arrived("key", most(key_all))
    keys = key_all[...].reshape(n_dp * slots, key_all.shape[2])
    products = lax.dot_general(keys, query_own[...], (((1,), (1,)), ((), ())), preferred_element_type=f32)
    chosen = lax.broadcasted_iota(jnp.int32, products.shape, 0) == want
    logit = jnp.sum(jnp.where(chosen, products, 0.0), axis=0, keepdims=True) * INV_TEMP
    loss_ref[...] = jnp.log(jnp.exp(logit - INV_TEMP) + negative) + INV_TEMP - logit

    for phase, every_part in (("query", query_all), ("queue", part_all), ("key", key_all), ("sum1", sum_recv), ("bn1", all1), ("bn2", all2), ("bn3", all3)):
        sent(phase, most(every_part))
    for side in range(2):
        sent("class" + str(side), class_send.at[side])
        sent("far" + str(side), far_send.at[side])
    for name in ORDERS:
        for step in range(3):
            sent(name + str(step), sends[name].at[step])


def on_device_shuffled(n_dp, n_bn, features, shuffle_masks, conv_in, conv_mid, conv_out, head, queries, queue, positive):
    f32, bf16 = jnp.float32, jnp.bfloat16
    slots, cells, channels = features.shape
    rows = slots * cells
    middle = conv_in.shape[1]
    width = queries.shape[1]

    def group_parts(c):
        tile = (2 * (c // LANES), LANES)
        return [pltpu.VMEM(tile, f32), pltpu.VMEM((n_bn,) + tile, f32)]

    chunk = channels // len(ORDERS)
    feature_parts = [
        pltpu.VMEM((3, rows // 2, chunk), bf16),
        pltpu.VMEM((rows, chunk), bf16),
        pltpu.VMEM((rows // 2, chunk), bf16),
    ]
    sums = pltpu.VMEM((n_dp, 2 * (middle // LANES), LANES), f32)
    hbm = pl.BlockSpec(memory_space=pltpu.HBM)
    loss = pl.pallas_call(
        functools.partial(shuffled_kernel, n_dp, n_bn),
        out_shape=jax.ShapeDtypeStruct((1, slots), f32),
        in_specs=[hbm] * 9,
        out_specs=pl.BlockSpec(memory_space=pltpu.VMEM),
        scratch_shapes=[
            pltpu.SMEM(shuffle_masks.shape, jnp.int32),
            pltpu.SMEM(positive.shape, jnp.int32),
            pltpu.VMEM(queries.shape, bf16),
            pltpu.VMEM((rows, channels), bf16),
            pltpu.VMEM(conv_in.shape, bf16),
            pltpu.VMEM(conv_mid.shape, bf16),
            pltpu.VMEM(conv_out.shape, bf16),
            pltpu.VMEM(head.shape, bf16),
            pltpu.VMEM(queue.shape, bf16),
            pltpu.VMEM((rows, middle), f32),
            pltpu.VMEM((rows, channels), f32),
            pltpu.VMEM((n_dp, middle), f32),
            pltpu.VMEM((8, channels), f32),
            pltpu.VMEM((8, channels), f32),
            pltpu.VMEM((rows, middle), bf16),
            pltpu.VMEM((2, 3 * rows // 2, middle // 2), bf16),
            pltpu.VMEM((2, 3 * rows // 2, middle // 2), bf16),
            pltpu.VMEM((2, rows // 2, middle // 2), bf16),
            pltpu.VMEM((2, rows // 2, middle // 2), bf16),
        ]
        + [pltpu.VMEM((rows, channels), f32), sums, sums]
        + group_parts(middle)
        + group_parts(middle)
        + group_parts(channels)
        + [
            pltpu.VMEM((slots, width), bf16),
            pltpu.VMEM((n_dp, slots, width), bf16),
            pltpu.VMEM((1, n_dp * slots), f32),
            pltpu.VMEM((n_dp, 1, n_dp * slots), f32),
            pltpu.VMEM((slots, width), bf16),
            pltpu.VMEM((n_dp, slots, width), bf16),
            pltpu.SemaphoreType.DMA((8,)),
            pltpu.SemaphoreType.DMA((PANELS,)),
            pltpu.SemaphoreType.DMA((len(PHASES + STEPS),)),
            pltpu.SemaphoreType.DMA((len(PHASES + STEPS),)),
        ]
        + feature_parts * len(ORDERS),
        compiler_params=pltpu.CompilerParams(
            collective_id=0, has_side_effects=True, vmem_limit_bytes=64 << 20
        ),
        name="shuffled_crops",
    )(shuffle_masks, positive, queries, features.reshape(rows, channels), conv_in, conv_mid, conv_out, head, queue)
    return loss.reshape(slots)


def on_device(n_dp, n_bn, *arrays):
    features, conv_in = arrays[0], arrays[2]
    slots, cells, channels = features.shape
    whole_lanes = conv_in.shape[1] % (2 * LANES) == 0 and channels % (4 * LANES) == 0
    if whole_lanes and n_dp == 8 and slots * cells == LANES and cells == 8 and n_bn <= 4:
        return on_device_shuffled(n_dp, n_bn, *arrays)
    return on_device_moving(*arrays)


def solution(mesh):
    return jax.shard_map(
        functools.partial(on_device, mesh.shape["dp"], mesh.shape["bn"]),
        mesh=mesh,
        in_specs=(
            P(("dp", "bn"), None, None),
            P(),
            P(),
            P(),
            P(),
            P(),
            P(("dp", "bn"), None),
            P("dp", None),
            P(("dp", "bn")),
        ),
        out_specs=P(("dp", "bn")),
        check_vma=False,
    )
```
